128 devices in a mesh: cam: 8 (over x, core), tile: 16 (over y, z).
Axes of the slice: x: 4, y: 4, z: 4, core: 2. Of those that a mesh axis runs over, the one named last changes fastest.
Arguments:
- depth_weights: bfloat16 [512, 16, 64, 128], P(('cam', 'tile')), may hold values from 0.049804688 to 1
- context: bfloat16 [512, 16, 128, 128], P(('cam', 'tile')), may hold values from -1.5 to 1.5
- block_owner: int32 [512, 16, 1], P(('cam', 'tile')), may hold values from 0 to 127; in each aligned block of 64 rows (0 to 63, 64 to 127, ..., all dimensions but the last counted through in order) at most 2 rows name the same one
- block_local: int32 [512, 16], P(('cam', 'tile')), may hold values from 0 to 15
- block_cell: int32 [512, 16, 64], P(('cam', 'tile')), may hold values from 0 to 255
- conv_weight: bfloat16 [4, 3, 3, 128, 128], replicated, may hold values from -0.25 to 0.25
- cotangent: bfloat16 [128, 4096, 128], P('cam', 'tile'), may hold values from -6 to 6
Outputs:
- bev_out: bfloat16 [128, 4096, 128], P('cam', 'tile')
- grad_depth: bfloat16 [512, 16, 64, 128], P(('cam', 'tile'))
- grad_context: bfloat16 [512, 16, 128, 128], P(('cam', 'tile'))
The draws below stay inside these ranges and needn't reach their ends.
Inputs may be any that keep to these rules, and one draw needn't show every extreme that they name: `block_owner`: among the blocks of the cameras of one device (aligned groups of 4 cameras) no owner is named by more than 2 blocks, a bound that some block reaches.
All inputs are finite; a program needn't handle non-finite values.
Results may differ from the reference program's by a relative error of at most 0.02.
Values may be sent and summed in bfloat16 or wider, within the bound.
No kernel may reach another device: no remote copies, remote signals or barrier semaphores. Data moves between devices by JAX's collectives and lax.ppermute only.
A program may use at most 128 MiB of HBM per device.

```python
import math
import jax
import jax.numpy as jnp
import numpy as np

C = 128
DB = 64
PIX = 128
BLK = 16
TS = 16
TC_DEV = 16
TR_DEV = 1
CAM_DEV = 4
LAYERS = 4
OWNERS = 128
CAMS = 512
GX = 128
GY = 4096
TILES_DEV = 16
CAP = 2
N_TILE = 16


def plant(drawn, key, smallest, high):
    shape = drawn.shape
    spot = [jax.random.randint(jax.random.fold_in(key, axis), (), 0, shape[axis]) for axis in range(len(shape))]
    drawn = drawn.at[tuple(spot)].set(smallest)
    longest = shape.index(max(shape))
    spot[longest] = (spot[longest] + 1) % shape[longest]
    return drawn.at[tuple(spot)].set(high)


def steps_of(rng, shape, pieces, smallest, high):
    def one(dim, blocks):
        heights = jax.random.uniform(jax.random.fold_in(jax.random.fold_in(rng, 6), dim), (blocks,), jnp.float32, smallest / len(pieces), high / len(pieces))
        return jnp.repeat(jnp.exp(heights), shape[dim] // blocks).reshape((-1,) + (1,) * (len(shape) - dim - 1))

    gain = one(*pieces[0])
    for cut in pieces[1:]:
        gain = gain * one(*cut)
    return gain


def routed_block(key, own, number, rows, amount, top, bound, slope):
    order = jax.random.permutation(key, amount)
    packed, ordinary = shares(amount, rows * top, bound, slope, True), shares(amount, rows * top, bound, slope, False)
    places = jnp.arange(amount)

    def named(lengths, offset_by):
        used = int((lengths > 0).sum())
        fixed = max(1, used // 4)
        shifted = fixed + (places - fixed + offset_by * (used - fixed)) % max(1, amount - fixed)
        return jnp.zeros((amount,), jnp.int32).at[order[jnp.where(places < fixed, places, shifted)]].set(jnp.asarray(lengths, jnp.int32))

    lengths = jnp.where(number % 4 == 0, named(packed, number // 4), named(ordinary, number - number // 4 - 1))
    mixed = jax.random.permutation(jax.random.fold_in(own, 3), amount)
    donor, receiver = mixed[0:amount // 2 * 2:2], mixed[1:amount // 2 * 2:2]
    room = jnp.minimum(lengths[donor] - 1, bound - lengths[receiver]) // 2
    room = jnp.where((donor == order[0]) | (receiver == order[0]) | (lengths[receiver] == 0), 0, jnp.maximum(room, 0))
    shifted = jax.random.randint(jax.random.fold_in(own, 4), (amount // 2,), 0, 1 << 20) % (room + 1)
    lengths = lengths.at[donor].add(-shifted).at[receiver].add(shifted)
    labels = jnp.searchsorted(jnp.cumsum(lengths), jnp.arange(rows * top), side="right").astype(jnp.int32)
    grid = labels.reshape(top, rows).T
    grid = grid[jax.random.permutation(jax.random.fold_in(own, 1), rows)]
    offset_by = jax.random.randint(jax.random.fold_in(own, 2), (rows, 1), 0, top)
    return jnp.take_along_axis(grid, (jnp.arange(top)[None, :] + offset_by) % top, axis=1)


def shares(count, total, bound, slope, full):
    weights = [(1 << 20) // math.isqrt(rank ** slope) + 1 for rank in range(1, count + 1)]
    largest = bound if full else min(bound, max(-(-total // count), total * weights[0] // sum(weights)))
    least = 1 if total - largest >= count - 1 else 0
    counts, rest = [largest] + [least] * (count - 1), total - largest - least * (count - 1)
    while rest > 0:
        movable = [i for i in range(1, count) if counts[i] < largest] or [i for i in range(1, count) if counts[i] < bound]
        whole, remaining = sum([weights[i] for i in movable]), rest
        for i in movable:
            more = min(bound - counts[i], max(1, remaining * weights[i] // whole), rest)
            counts[i] = counts[i] + more
            rest = rest - more
    return np.array(counts)


def gaussian(stream_key, shape, deviation, reach, cuts=(), kind=jnp.bfloat16):
    loudness = steps_of(stream_key, shape, cuts, -0.22, 0.18) if cuts else 1.0
    array = jax.random.normal(stream_key, shape, jnp.float32) * deviation * loudness
    return jnp.minimum(jnp.maximum(array, -reach), reach).astype(kind)


def setup_inputs(seed: int = 0) -> dict:
    key_list = jax.random.split(jax.random.key(seed), 8)
    depth_weights = jnp.clip(jnp.exp(math.log(1.0) - 2.9996462 * jax.random.uniform(key_list[0], (CAMS, BLK, DB, PIX), jnp.float32) ** steps_of(key_list[0], (CAMS, BLK, DB, PIX), ((0, 128),), -0.2, 0.2)), 0.049804688, 1.0).astype(jnp.bfloat16)
    context = gaussian(key_list[1], (CAMS, BLK, PIX, C), 0.25, 1.5, ((0, 128),))
    block_owner_keys = jax.random.split(jax.random.fold_in(key_list[2], 1), CAMS * BLK // (CAM_DEV * BLK))
    block_owner_turns = jax.random.permutation(jax.random.fold_in(key_list[2], 3), CAMS * BLK // (CAM_DEV * BLK))
    block_owner = jax.vmap(lambda own, number: routed_block(jax.random.fold_in(key_list[2], 2), own, number, CAM_DEV * BLK, OWNERS, 1, CAP, 2))(block_owner_keys, block_owner_turns).reshape((CAMS, BLK, 1))
    block_local = plant(jax.random.randint(key_list[3], (CAMS, BLK), 0, TILES_DEV), jax.random.fold_in(key_list[3], 1), 0, TILES_DEV - 1).astype(jnp.int32)
    block_cell = plant(jax.random.randint(key_list[4], (CAMS, BLK, DB), 0, TS * TS), jax.random.fold_in(key_list[4], 1), 0, (TS * TS) - 1).astype(jnp.int32)
    conv_weight = gaussian(key_list[5], (LAYERS, 3, 3, C, C), (4 * C) ** -0.5, 0.25)
    cotangent = gaussian(key_list[6], (GX, GY, C), 1.0, 6.0, ((0, 8), (1, 16)))
    return {"depth_weights": depth_weights, "context": context, "block_owner": block_owner, "block_local": block_local, "block_cell": block_cell, "conv_weight": conv_weight, "cotangent": cotangent}


def silu_slope(preact):
    sigma = jax.nn.sigmoid(preact)
    return sigma * (1.0 + preact * (1.0 - sigma))


def conv_taps(padded, kernel, flipped):
    rows_out = padded.shape[0] - 2
    cols_out = padded.shape[1] - 2
    total = jnp.zeros((rows_out, cols_out, kernel.shape[3]), jnp.float32)
    for row_tap in range(3):
        for col_tap in range(3):
            window = padded[row_tap:row_tap + rows_out, col_tap:col_tap + cols_out].astype(jnp.float32)
            if flipped:
                total = total + jnp.einsum("xyo,io->xyi", window, kernel[2 - row_tap, 2 - col_tap].astype(jnp.float32))
            else:
                total = total + jnp.einsum("xyi,io->xyo", window, kernel[row_tap, col_tap].astype(jnp.float32))
    return total


def pad_grid(field):
    return jnp.pad(field, ((1, 1), (1, 1), (0, 0)))


def reference(depth_weights, context, block_owner, block_local, block_cell, conv_weight, cotangent):
    grid_rows = cotangent.shape[0]
    grid_cols = cotangent.shape[1]
    channels = context.shape[3]
    depth_wide = depth_weights.astype(jnp.float32)
    context_wide = context.astype(jnp.float32)
    lifted = jnp.einsum("nbdp,nbpc->nbdc", depth_wide, context_wide).astype(jnp.bfloat16)
    owner_ids = block_owner[..., 0]
    region_rows = TR_DEV * TS
    region_cols = TC_DEV * TS
    row_base = (owner_ids // N_TILE) * region_rows + (block_local // TC_DEV) * TS
    col_base = (owner_ids % N_TILE) * region_cols + (block_local % TC_DEV) * TS
    cell_row = row_base[..., None] + block_cell // TS
    cell_col = col_base[..., None] + block_cell % TS
    cell_index = (cell_row * grid_cols + cell_col).astype(jnp.int32)
    splat_sum = jax.ops.segment_sum(lifted.reshape(-1, channels).astype(jnp.float32), cell_index.reshape(-1), num_segments=grid_rows * grid_cols)
    activation = splat_sum.reshape(grid_rows, grid_cols, channels).astype(jnp.bfloat16)
    stored = []
    for layer in range(LAYERS):
        preact = conv_taps(pad_grid(activation), conv_weight[layer], False)
        stored.append(preact)
        activation = jax.nn.silu(preact).astype(jnp.bfloat16)
    bev_out = activation
    gradient = cotangent
    for layer in range(LAYERS - 1, -1, -1):
        grad_pre = (gradient.astype(jnp.float32) * silu_slope(stored[layer])).astype(jnp.bfloat16)
        gradient = conv_taps(pad_grid(grad_pre), conv_weight[layer], True).astype(jnp.bfloat16)
    back_rows = gradient.reshape(grid_rows * grid_cols, channels)[cell_index]
    back_wide = back_rows.astype(jnp.float32)
    grad_depth = jnp.einsum("nbdc,nbpc->nbdp", back_wide, context_wide).astype(jnp.bfloat16)
    grad_context = jnp.einsum("nbdp,nbdc->nbpc", depth_wide, back_wide).astype(jnp.bfloat16)
    return (bev_out, grad_depth, grad_context)
```

```python
import jax
import jax.numpy as jnp
from jax import lax
from jax.experimental import pallas as pl
from jax.experimental.pallas import tpu as pltpu
from jax.sharding import PartitionSpec as P

TS = 16
LAYERS = 4
EXT = 2 * LAYERS
EMPTY = 256.0
BF = jnp.bfloat16
F32 = jnp.float32


def ring(axis):
    count = lax.axis_size(axis)
    ends = count - 1
    down = [(i, i + 1) for i in range(ends)]
    up = [(i + 1, i) for i in range(ends)]
    return down, up


def with_sides(cells, axis, dim, width):
    down, up = ring(axis)
    size = cells.shape[dim]
    head = lax.slice_in_dim(cells, 0, width, axis=dim)
    tail = lax.slice_in_dim(cells, size - width, size, axis=dim)
    return jnp.concatenate(
        [lax.ppermute(tail, axis, down), cells, lax.ppermute(head, axis, up)], axis=dim
    )


def take_slot(owner, count):
    rank = count[owner]
    count[owner] = rank + 1
    return rank


def clear_counts(count, size):
    @pl.loop(0, size)
    def _(i):
        count[i] = 0


def pack_kernel(owner, local, cells, depth, context, out, count, meta):
    owners, rows, width = out.shape
    bins = depth.shape[1]
    clear_counts(count, owners)
    out[...] = jnp.zeros(out.shape, BF)
    kind = lax.broadcasted_iota(jnp.int32, meta.shape, 1)
    meta[...] = jnp.where(kind == 0, EMPTY, 0.0)
    lane = lax.broadcasted_iota(jnp.int32, (1, width), 1)

    def block(b, carry):
        to = owner[b]
        rank = take_slot(to, count)
        lifted = jnp.dot(depth[b], context[b], preferred_element_type=F32)
        out[to, pl.ds(pl.multiple_of(rank * bins, bins), bins), :] = lifted.astype(BF)
        mine = (lane // bins) == rank
        meta[to, pl.ds(0, 1), :] = jnp.where(mine, cells[b], meta[to, pl.ds(0, 1), :])
        tile = local[b].astype(F32)
        meta[to, pl.ds(1, 1), :] = jnp.where(mine, tile, meta[to, pl.ds(1, 1), :])
        return carry

    lax.fori_loop(0, depth.shape[0], block, 0, unroll=4)
    out[:, pl.ds(2 * bins, 8), :] = meta[...].astype(BF)


def pack(owner, local, cells, depth, context, owners):
    blocks, bins, pixels = depth.shape
    channels = context.shape[2]
    smem = pl.BlockSpec(memory_space=pltpu.SMEM)
    vmem = pl.BlockSpec(memory_space=pltpu.VMEM)
    return pl.pallas_call(
        pack_kernel,
        out_shape=jax.ShapeDtypeStruct((owners, 2 * bins + 8, channels), BF),
        in_specs=[smem, smem, vmem, vmem, vmem],
        out_specs=vmem,
        scratch_shapes=[pltpu.SMEM((owners,), jnp.int32), pltpu.VMEM((owners, 8, channels), F32)],
        compiler_params=pltpu.CompilerParams(vmem_limit_bytes=40 << 20),
        name="pack",
    )(owner, local, cells, depth, context)


def cell_onehot(cell_row, cells):
    number = lax.broadcasted_iota(jnp.int32, (cells, cell_row.shape[1]), 0)
    return jnp.where(number == cell_row, 1.0, 0.0).astype(BF)


def splat_kernel(tiles, message, out, acc):
    step = pl.program_id(0)
    sources, rows, channels = message.shape
    bins = (rows - 8) // 2
    cells = TS * TS

    @pl.when(step == 0)
    def _():
        acc[...] = jnp.zeros(acc.shape, F32)

    def source(s, carry):
        meta = message[s, pl.ds(2 * bins, 8), :].astype(jnp.int32)
        hot = cell_onehot(meta[0:1], cells)
        first = message[s, 0:bins, :]
        second = message[s, bins : 2 * bins, :]
        nothing = jnp.zeros((bins, channels), BF)
        both = jnp.concatenate(
            [
                jnp.concatenate([first, nothing], axis=0),
                jnp.concatenate([nothing, second], axis=0),
            ],
            axis=1,
        )
        sums = jnp.dot(hot, both, preferred_element_type=F32)
        for rank in range(2):
            tile = tiles[(step * sources + s) * 2 + rank]
            at = pl.ds(pl.multiple_of(tile * TS, TS), TS)
            part = sums[:, rank * channels : (rank + 1) * channels]
            acc[:, at, :] += part.reshape(TS, TS, channels)
        return carry

    lax.fori_loop(0, sources, source, 0, unroll=2)

    @pl.when(step == pl.num_programs(0) - 1)
    def _():
        out[...] = acc[...].astype(BF)


def splat(tiles, message, rows, cols):
    owners, height, channels = message.shape
    chunk = owners // 8
    return pl.pallas_call(
        splat_kernel,
        out_shape=jax.ShapeDtypeStruct((rows, cols, channels), BF),
        grid=(owners // chunk,),
        in_specs=[
            pl.BlockSpec(memory_space=pltpu.SMEM),
            pl.BlockSpec((chunk, height, channels), lambda i: (i, 0, 0)),
        ],
        out_specs=pl.BlockSpec((rows, cols, channels), lambda i: (0, 0, 0)),
        scratch_shapes=[pltpu.VMEM((rows, cols, channels), F32)],
        compiler_params=pltpu.CompilerParams(vmem_limit_bytes=40 << 20),
        name="splat",
    )(tiles, message)


def conv_kernel(
    edges, middle, above, below, left, right, corner_above, corner_below, cot, weights,
    bev, grad, ping, pong, slopes, half,
):
    rows, cols, channels = middle.shape
    wide = cols + 2 * EXT
    three = 3 * channels
    pairs = rows // 2 + EXT
    column = lax.broadcasted_iota(jnp.int32, (wide, channels), 0)
    gone = ((column < EXT) & (edges[2] == 1)) | ((column >= wide - EXT) & (edges[3] == 1))
    half[0] = jnp.zeros((wide, channels), F32)
    half[1] = jnp.where(gone, 0.0, 0.5)

    def put(ref, pair, side, value):
        base = side * three
        ref[pair, :, base : base + channels] = pltpu.roll(value, 1, 0).astype(BF)
        ref[pair, :, base + channels : base + 2 * channels] = value.astype(BF)
        ref[pair, :, base + 2 * channels : base + three] = pltpu.roll(value, wide - 1, 0).astype(BF)

    def load(pair, side, west, center, east):
        joined = jnp.concatenate(
            [west.astype(F32), center.astype(F32), east.astype(F32)], axis=0
        )
        put(ping, pair, side, joined)

    def load_outer(k, carry):
        for side in range(2):
            row = 2 * k + side
            for refs, base in (((corner_above, above), 0), ((corner_below, below), EXT + rows)):
                corner, field = refs
                load(
                    base // 2 + k, side, corner[row, 0:EXT, :], field[row], corner[row, EXT:, :]
                )
        return carry

    def load_inner(k, carry):
        for side in range(2):
            row = 2 * k + side
            load(EXT // 2 + k, side, left[row], middle[row], right[row])
        return carry

    lax.fori_loop(0, EXT // 2, load_outer, 0)
    lax.fori_loop(0, rows // 2, load_inner, 0)

    def conv(ref, k, layer):
        return jnp.dot(
            ref[k], weights[layer, 0 : 2 * three, :], preferred_element_type=F32
        ) + jnp.dot(ref[k + 1], weights[layer, 2 * three :, :], preferred_element_type=F32)

    source, target = ping, pong
    offset = 0
    offsets = []
    for layer in range(LAYERS):
        count = pairs - 1 - layer
        offsets.append(offset)

        def forward(k, carry, layer=layer, source=source, target=target, offset=offset):
            total = conv(source, k, layer)
            for side in range(2):
                row = layer + 1 + 2 * k + side
                inside = jnp.where(
                    ((row < EXT) & (edges[0] == 1)) | ((row >= EXT + rows) & (edges[1] == 1)), 0, 1
                )
                preact = total[:, side * channels : (side + 1) * channels]
                scale = half[inside]
                sigma = scale + scale * jnp.tanh(0.5 * preact)
                active = preact * sigma
                slope = sigma + (active - active * sigma)
                if layer < LAYERS - 1:
                    put(target, k, side, active)
                    slopes[offset + k, side] = slope
                else:
                    @pl.when((row >= EXT) & (row < EXT + rows))
                    def _(row=row, active=active):
                        bev[row - EXT] = active[EXT : EXT + cols].astype(BF)

                    put(target, k, side, cot[row - LAYERS].astype(F32) * slope)
            return carry

        lax.fori_loop(0, count, forward, 0)
        offset += count
        source, target = target, source

    for step in range(LAYERS):
        layer = LAYERS - 1 - step
        count = rows // 2 + layer

        def backward(k, carry, layer=layer, source=source, target=target, step=step):
            total = conv(source, k, LAYERS + layer)
            for side in range(2):
                value = total[:, side * channels : (side + 1) * channels]
                if layer > 0:
                    below_at = offsets[layer - 1] + k + step + 1
                    put(target, k, side, value * slopes[below_at, side])
                else:
                    grad[2 * k + side] = value[EXT : EXT + cols].astype(BF)
            return carry

        lax.fori_loop(0, count, backward, 0)
        source, target = target, source


def convs(edges, middle, above, below, left, right, corner_above, corner_below, cot, weights):
    rows, cols, channels = middle.shape
    wide = cols + 2 * EXT
    pairs = rows // 2 + EXT
    kept = sum(pairs - 1 - layer for layer in range(LAYERS - 1))
    vmem = pl.BlockSpec(memory_space=pltpu.VMEM)
    buffer = pltpu.VMEM((pairs, wide, 6 * channels), BF)
    return pl.pallas_call(
        conv_kernel,
        out_shape=(
            jax.ShapeDtypeStruct((rows, cols, channels), BF),
            jax.ShapeDtypeStruct((rows, cols, channels), BF),
        ),
        in_specs=[pl.BlockSpec(memory_space=pltpu.SMEM)] + [vmem] * 9,
        out_specs=(vmem, vmem),
        scratch_shapes=[
            buffer,
            buffer,
            pltpu.VMEM((kept, 2, wide, channels), F32),
            pltpu.VMEM((2, wide, channels), F32),
        ],
        compiler_params=pltpu.CompilerParams(vmem_limit_bytes=60 << 20),
        name="convs",
    )(edges, middle, above, below, left, right, corner_above, corner_below, cot, weights)


def gather_kernel(tiles, message, grad, out, turned):
    step = pl.program_id(0)
    sources, _, channels = message.shape
    rows, cols, _ = grad.shape
    cells = TS * TS

    @pl.when(step == 0)
    def _():
        for tile in range(cols // TS):
            piece = grad[:, tile * TS : (tile + 1) * TS, :].reshape(cells, channels)
            turned[tile] = piece.astype(F32).T.astype(BF)

    lane = lax.broadcasted_iota(jnp.int32, (channels, channels), 1)

    def source(s, carry):
        meta = message[s].astype(jnp.int32)
        hot = cell_onehot(meta[0:1], cells)
        at = (step * sources + s) * 2
        first = jnp.dot(turned[tiles[at]], hot, preferred_element_type=F32)
        second = jnp.dot(turned[tiles[at + 1]], hot, preferred_element_type=F32)
        out[s] = jnp.where(lane < channels // 2, first, second).astype(BF)
        return carry

    lax.fori_loop(0, sources, source, 0, unroll=2)


def gather(tiles, message, grad):
    owners, height, channels = message.shape
    rows, cols, _ = grad.shape
    chunk = owners // 8
    return pl.pallas_call(
        gather_kernel,
        out_shape=jax.ShapeDtypeStruct((owners, channels, height - 8), BF),
        grid=(owners // chunk,),
        in_specs=[
            pl.BlockSpec(memory_space=pltpu.SMEM),
            pl.BlockSpec((chunk, 8, channels), lambda i: (i, height // 8 - 1, 0)),
            pl.BlockSpec((rows, cols, channels), lambda i: (0, 0, 0)),
        ],
        out_specs=pl.BlockSpec((chunk, channels, height - 8), lambda i: (i, 0, 0)),
        scratch_shapes=[pltpu.VMEM((cols // TS, channels, TS * TS), BF)],
        compiler_params=pltpu.CompilerParams(vmem_limit_bytes=40 << 20),
        name="gather",
    )(tiles, message, grad)


def final_kernel(owner, returned, depth, context, grad_depth, grad_context, count):
    step = pl.program_id(0)
    blocks, bins, _ = depth.shape

    @pl.when(step == 0)
    def _():
        clear_counts(count, returned.shape[0])

    def block(b, carry):
        to = owner[step * blocks + b]
        rank = take_slot(to, count)
        turned = returned[to].astype(F32).T
        rows = jnp.where(rank == 0, turned[0:bins], turned[bins : 2 * bins]).astype(BF)
        grad_depth[b] = lax.dot_general(
            rows, context[b], (((1,), (1,)), ((), ())), preferred_element_type=F32
        ).astype(BF)
        grad_context[b] = lax.dot_general(
            depth[b], rows, (((0,), (0,)), ((), ())), preferred_element_type=F32
        ).astype(BF)
        return carry

    lax.fori_loop(0, blocks, block, 0, unroll=4)


def final(owner, returned, depth, context):
    blocks, bins, pixels = depth.shape
    channels = context.shape[2]
    chunk = blocks // 4
    whole = pl.BlockSpec(returned.shape, lambda i: (0, 0, 0))
    depth_block = pl.BlockSpec((chunk, bins, pixels), lambda i: (i, 0, 0))
    context_block = pl.BlockSpec((chunk, pixels, channels), lambda i: (i, 0, 0))
    return pl.pallas_call(
        final_kernel,
        out_shape=(
            jax.ShapeDtypeStruct(depth.shape, BF),
            jax.ShapeDtypeStruct(context.shape, BF),
        ),
        grid=(blocks // chunk,),
        in_specs=[pl.BlockSpec(memory_space=pltpu.SMEM), whole, depth_block, context_block],
        out_specs=(depth_block, context_block),
        scratch_shapes=[pltpu.SMEM((returned.shape[0],), jnp.int32)],
        compiler_params=pltpu.CompilerParams(vmem_limit_bytes=40 << 20),
        name="final",
    )(owner, returned, depth, context)


def paired_weights(kernel):
    layers, _, _, inner, outer = kernel.shape
    upper = jnp.pad(kernel, ((0, 0), (0, 1), (0, 0), (0, 0), (0, 0)))
    lower = jnp.pad(kernel, ((0, 0), (1, 0), (0, 0), (0, 0), (0, 0)))
    return jnp.concatenate([upper, lower], axis=4).reshape(layers, 12 * inner, 2 * outer)


def per_device(
    depth_weights, context, block_owner, block_local, block_cell, conv_weight, cotangent
):
    cams_here, blocks_cam, bins, pixels = depth_weights.shape
    channels = context.shape[3]
    rows, cols, _ = cotangent.shape
    axes = ("cam", "tile")
    owners = lax.axis_size(axes)
    blocks = cams_here * blocks_cam
    depth = depth_weights.reshape(blocks, bins, pixels)
    flat_context = context.reshape(blocks, pixels, channels)
    owner = block_owner.reshape(blocks)
    local = block_local.reshape(blocks)
    cells = block_cell.reshape(blocks, 1, bins).astype(F32)
    cells = jnp.concatenate([cells, cells], axis=2)

    sent = pack(owner, local, cells, depth, flat_context, owners)
    message = lax.all_to_all(sent, axes, split_axis=0, concat_axis=0, tiled=True)

    cot = with_sides(with_sides(cotangent, "tile", 1, EXT), "cam", 0, LAYERS)
    turned_weight = conv_weight[:, ::-1, ::-1].swapaxes(3, 4)
    weights = jnp.concatenate([paired_weights(conv_weight), paired_weights(turned_weight)], axis=0)
    cam = lax.axis_index("cam")
    tile = lax.axis_index("tile")
    edges = jnp.stack(
        [cam == 0, cam == lax.axis_size("cam") - 1, tile == 0, tile == lax.axis_size("tile") - 1]
    ).astype(jnp.int32)

    tiles = message[:, 2 * bins + 1, :: bins].astype(jnp.int32).reshape(2 * owners)
    middle = splat(tiles, message, rows, cols)

    down, up = ring("cam")
    east, west = ring("tile")
    above = lax.ppermute(middle[rows - EXT :], "cam", down)
    below = lax.ppermute(middle[:EXT], "cam", up)
    left = lax.ppermute(middle[:, cols - EXT :], "tile", east)
    right = lax.ppermute(middle[:, :EXT], "tile", west)
    sides = jnp.concatenate([left, right], axis=1)
    corner_above = lax.ppermute(sides[rows - EXT :], "cam", down)
    corner_below = lax.ppermute(sides[:EXT], "cam", up)

    bev, grad = convs(
        edges, middle, above, below, left, right, corner_above, corner_below, cot, weights
    )
    rows_back = gather(tiles, message, grad)
    returned = lax.all_to_all(rows_back, axes, split_axis=0, concat_axis=0, tiled=True)
    grad_depth, grad_context = final(owner, returned, depth, flat_context)
    return (
        bev,
        grad_depth.reshape(depth_weights.shape),
        grad_context.reshape(context.shape),
    )


def solution(mesh):
    placed = (
        P(("cam", "tile"), None, None, None),
        P(("cam", "tile"), None, None, None),
        P(("cam", "tile"), None, None),
        P(("cam", "tile"), None),
        P(("cam", "tile"), None, None),
        P(),
        P("cam", "tile", None),
    )
    return jax.shard_map(
        per_device,
        mesh=mesh,
        in_specs=placed,
        out_specs=(
            P("cam", "tile", None),
            P(("cam", "tile"), None, None, None),
            P(("cam", "tile"), None, None, None),
        ),
        check_vma=False,
    )
```

```python
import jax
import jax.numpy as jnp
from jax import lax
from jax.experimental import pallas as pl
from jax.experimental.pallas import tpu as pltpu
from jax.sharding import PartitionSpec as P

TS = 16
LAYERS = 4
EXT = 2 * LAYERS
PAIRS = 8
CHUNK = 4
EMPTY = 256.0
ABSENT = 255
BF = jnp.bfloat16
F32 = jnp.float32


def ring(axis):
    count = lax.axis_size(axis)
    ends = count - 1
    down = [(i, i + 1) for i in range(ends)]
    up = [(i + 1, i) for i in range(ends)]
    return down, up


def with_sides(cells, axis, dim, width):
    down, up = ring(axis)
    size = cells.shape[dim]
    head = lax.slice_in_dim(cells, 0, width, axis=dim)
    tail = lax.slice_in_dim(cells, size - width, size, axis=dim)
    return jnp.concatenate(
        [lax.ppermute(tail, axis, down), cells, lax.ppermute(head, axis, up)], axis=dim
    )


def take_slot(owner, count):
    rank = count[owner]
    count[owner] = rank + 1
    return rank


def clear_counts(count, size):
    @pl.loop(0, size)
    def _(i):
        count[i] = 0


def pair_cells(cells):
    return (cells // TS) * TS + (cells % 2) * (TS // 2) + (cells % TS) // 2


def pack_kernel(owner, local, cells, depth, context, out, count, wide, lifted, meta, sems):
    step = pl.program_id(0)
    blocks, bins, _ = depth.shape
    owners = out.shape[0]
    channels = context.shape[2]

    @pl.when(step == 0)
    def _():
        clear_counts(count, owners)
        kind = lax.broadcasted_iota(jnp.int32, meta.shape, 1)
        meta[...] = jnp.where(kind == 0, EMPTY, ABSENT)
        numbers = pair_cells(cells[...]).astype(F32)
        wide[...] = jnp.concatenate([numbers, numbers], axis=1)

    lane = lax.broadcasted_iota(jnp.int32, (1, 2 * bins), 1)

    def block(b, carry):
        at = step * blocks + b
        to = owner[at]
        rank = take_slot(to, count)
        product = jnp.dot(depth[b], context[b], preferred_element_type=F32)
        lifted[at // 2, pl.ds(pl.multiple_of((at % 2) * bins, bins), bins), :] = product.astype(BF)
        mine = (lane // bins) == rank
        row = wide[pl.ds(at, 1), :]
        meta[to, pl.ds(0, 1), :] = jnp.where(mine, row, meta[to, pl.ds(0, 1), :])
        tile = local[at].astype(F32)
        meta[to, pl.ds(1, 1), :] = jnp.where(mine, tile, meta[to, pl.ds(1, 1), :])
        pltpu.make_async_copy(
            lifted.at[at // 2, pl.ds(pl.multiple_of((at % 2) * bins, bins), bins), :],
            out.at[to, pl.ds(pl.multiple_of(rank * bins, bins), bins), :],
            sems.at[0],
        ).start()
        return carry

    lax.fori_loop(0, blocks, block, 0, unroll=4)

    @pl.when(step == pl.num_programs(0) - 1)
    def _():
        wide_meta = lifted.shape[0]
        def put_meta(small):
            small[...] = meta[...].astype(BF)
            copy = pltpu.make_async_copy(
                small, out.at[:, pl.ds(2 * bins, 8), :], sems.at[1]
            )
            copy.start()
            copy.wait()
        pl.run_scoped(put_meta, pltpu.VMEM(meta.shape, BF))
        pltpu.make_async_copy(
            lifted, out.at[pl.ds(0, wide_meta), pl.ds(0, 2 * bins), :], sems.at[0]
        ).wait()


def pack(owner, local, cells, depth, context, owners):
    blocks, bins, pixels = depth.shape
    channels = context.shape[2]
    chunk = blocks // 4
    smem = pl.BlockSpec(memory_space=pltpu.SMEM)
    return pl.pallas_call(
        pack_kernel,
        out_shape=jax.ShapeDtypeStruct((owners, 2 * bins + 8, channels), BF),
        grid=(blocks // chunk,),
        in_specs=[
            smem,
            smem,
            pl.BlockSpec(cells.shape, lambda i: (0, 0)),
            pl.BlockSpec((chunk, bins, pixels), lambda i: (i, 0, 0)),
            pl.BlockSpec((chunk, pixels, channels), lambda i: (i, 0, 0)),
        ],
        out_specs=pl.BlockSpec(memory_space=pltpu.HBM),
        scratch_shapes=[
            pltpu.SMEM((owners,), jnp.int32),
            pltpu.VMEM((blocks, 2 * bins), F32),
            pltpu.VMEM((blocks // 2, 2 * bins, channels), BF),
            pltpu.VMEM((owners, 8, 2 * bins), F32),
            pltpu.SemaphoreType.DMA((2,)),
        ],
        compiler_params=pltpu.CompilerParams(vmem_limit_bytes=40 << 20),
        name="pack",
    )(owner, local, cells, depth, context)


def cell_onehot(cell_row, cells):
    number = lax.broadcasted_iota(jnp.int32, (cells, cell_row.shape[1]), 0)
    return jnp.where(number == cell_row, 1.0, 0.0).astype(BF)


def splat_kernel(meta_all, message, out, tiles_out, even, odd, turned, tiles, sem):
    step = pl.program_id(0)
    sources, rows, channels = message.shape
    bins = (rows - 8) // 2
    cells = TS * TS

    @pl.when(step == 0)
    def _():
        numbers = meta_all[:, 0:8, :].astype(F32)
        flat = numbers[:, 1, :].T
        turned[0:1, :] = flat[0:1].astype(jnp.int32)
        turned[1:2, :] = flat[bins : bins + 1].astype(jnp.int32)
        copy = pltpu.make_async_copy(turned, tiles, sem)
        copy.start()
        even[...] = jnp.zeros(even.shape, F32)
        odd[...] = jnp.zeros(odd.shape, F32)
        copy.wait()

    def source(s, carry):
        meta = message[s, pl.ds(2 * bins, 8), :].astype(jnp.int32)
        hot = cell_onehot(meta[0:1], cells)
        tile = [tiles[rank, step * sources + s] for rank in range(2)]
        nothing = jnp.zeros((bins, channels), BF)
        first = jnp.where(tile[0] < ABSENT, message[s, 0:bins, :], nothing)
        second = jnp.where(tile[1] < ABSENT, message[s, bins : 2 * bins, :], nothing)
        both = jnp.concatenate(
            [
                jnp.concatenate([first, nothing], axis=0),
                jnp.concatenate([nothing, second], axis=0),
            ],
            axis=1,
        )
        sums = jnp.dot(hot, both, preferred_element_type=F32)
        for rank, acc in enumerate((even, odd)):
            here = jnp.minimum(tile[rank], acc.shape[1] // 8 - 1)
            at = pl.ds(pl.multiple_of(here * 8, 8), 8)
            part = sums[:, rank * channels : (rank + 1) * channels].reshape(TS, 2, 8, channels)
            for side in range(2):
                lanes = slice(side * channels, (side + 1) * channels)
                acc[:, at, lanes] += part[:, side]
        return carry

    lax.fori_loop(0, sources, source, 0, unroll=4)

    @pl.when(step == pl.num_programs(0) - 1)
    def _():
        out[...] = (even[...] + odd[...]).astype(BF)
        tiles_out[...] = turned[...]


def splat(message, rows, cols):
    owners, height, channels = message.shape
    chunk = owners // 8
    shape = (rows, cols // 2, 2 * channels)
    return pl.pallas_call(
        splat_kernel,
        out_shape=(
            jax.ShapeDtypeStruct(shape, BF),
            jax.ShapeDtypeStruct((2, owners), jnp.int32),
        ),
        grid=(owners // chunk,),
        in_specs=[
            pl.BlockSpec((owners, 8, channels), lambda i: (0, height // 8 - 1, 0)),
            pl.BlockSpec((chunk, height, channels), lambda i: (i, 0, 0)),
        ],
        out_specs=(
            pl.BlockSpec(shape, lambda i: (0, 0, 0)),
            pl.BlockSpec((2, owners), lambda i: (0, 0)),
        ),
        scratch_shapes=[
            pltpu.VMEM(shape, F32),
            pltpu.VMEM(shape, F32),
            pltpu.VMEM((2, owners), jnp.int32),
            pltpu.SMEM((2, owners), jnp.int32),
            pltpu.SemaphoreType.DMA,
        ],
        compiler_params=pltpu.CompilerParams(vmem_limit_bytes=40 << 20),
        name="splat",
    )(message, message)


def conv_kernel(
    edges, middle, above, below, left, right, corner_above, corner_below, cot, weights,
    bev, grad, ping, pong, slopes, half,
):
    rows, mid, double = middle.shape
    channels = double // 2
    wide = mid + 2 * PAIRS
    tall = rows + 2 * EXT
    column = lax.broadcasted_iota(jnp.int32, (wide, double), 0)
    gone = ((column < PAIRS) & (edges[2] == 1)) | ((column >= wide - PAIRS) & (edges[3] == 1))
    half[0] = jnp.zeros((wide, double), F32)
    half[1] = jnp.where(gone, 0.0, 0.5)

    def put(ref, row, value):
        first = value[:, :channels]
        second = value[:, channels:]
        ref[row, :, 0:channels] = pltpu.roll(second, 1, 0).astype(BF)
        ref[row, :, channels : 3 * channels] = value.astype(BF)
        ref[row, :, 3 * channels :] = pltpu.roll(first, wide - 1, 0).astype(BF)

    def load(row, west, center, east):
        put(
            ping, row,
            jnp.concatenate([west.astype(F32), center.astype(F32), east.astype(F32)], axis=0),
        )

    def load_outer(k, carry):
        load(k, corner_above[k, 0:PAIRS], above[k], corner_above[k, PAIRS:])
        load(EXT + rows + k, corner_below[k, 0:PAIRS], below[k], corner_below[k, PAIRS:])
        return carry

    def load_inner(k, carry):
        load(EXT + k, left[k], middle[k], right[k])
        return carry

    lax.fori_loop(0, EXT, load_outer, 0)
    lax.fori_loop(0, rows, load_inner, 0)

    def conv(ref, row, layer, chunk):
        taps = [
            ref[pl.ds(row + tap, chunk)].reshape(chunk * wide, 2 * double) for tap in range(3)
        ]
        return jnp.dot(
            jnp.concatenate(taps, axis=1), weights[layer], preferred_element_type=F32
        ).reshape(chunk, wide, double)

    source, target = ping, pong
    offset = 0
    offsets = []
    for layer in range(LAYERS):
        count = tall - 2 - 2 * layer
        offsets.append(offset)

        def forward(k, carry, layer=layer, source=source, target=target, offset=offset, count=count):
            start = jnp.minimum(k * CHUNK, count - CHUNK)
            total = conv(source, start, layer, CHUNK)
            for side in range(CHUNK):
                here = start + side
                row = layer + 1 + here
                inside = jnp.where(
                    ((row < EXT) & (edges[0] == 1)) | ((row >= EXT + rows) & (edges[1] == 1)), 0, 1
                )
                preact = total[side]
                scale = half[inside]
                sigma = scale + scale * jnp.tanh(0.5 * preact)
                active = preact * sigma
                slope = sigma + (active - active * sigma)
                if layer < LAYERS - 1:
                    put(target, here, active)
                    slopes[offset + here] = slope
                else:
                    @pl.when((row >= EXT) & (row < EXT + rows))
                    def _(row=row, active=active):
                        bev[row - EXT] = active[PAIRS : PAIRS + mid].astype(BF)

                    put(target, here, cot[here].astype(F32) * slope)
            return carry

        lax.fori_loop(0, -(-count // CHUNK), forward, 0)
        offset += count
        source, target = target, source

    for step in range(LAYERS):
        layer = LAYERS - 1 - step
        count = rows + 2 * layer

        def backward(k, carry, layer=layer, source=source, target=target, step=step, count=count):
            start = jnp.minimum(k * CHUNK, count - CHUNK)
            total = conv(source, start, LAYERS + layer, CHUNK)
            for side in range(CHUNK):
                here = start + side
                if layer > 0:
                    put(target, here, total[side] * slopes[offsets[layer - 1] + here + 2 * (step + 1)])
                else:
                    grad[here] = total[side, PAIRS : PAIRS + mid].astype(BF)
            return carry

        lax.fori_loop(0, -(-count // CHUNK), backward, 0)
        source, target = target, source


def convs(edges, middle, above, below, left, right, corner_above, corner_below, cot, weights):
    rows, mid, double = middle.shape
    wide = mid + 2 * PAIRS
    tall = rows + 2 * EXT
    kept = sum(tall - 2 - 2 * layer for layer in range(LAYERS - 1))
    vmem = pl.BlockSpec(memory_space=pltpu.VMEM)
    buffer = pltpu.VMEM((tall, wide, 2 * double), BF)
    return pl.pallas_call(
        conv_kernel,
        out_shape=(
            jax.ShapeDtypeStruct(middle.shape, BF),
            jax.ShapeDtypeStruct(middle.shape, BF),
        ),
        in_specs=[pl.BlockSpec(memory_space=pltpu.SMEM)] + [vmem] * 9,
        out_specs=(vmem, vmem),
        scratch_shapes=[
            buffer,
            buffer,
            pltpu.VMEM((kept, wide, double), F32),
            pltpu.VMEM((2, wide, double), F32),
        ],
        compiler_params=pltpu.CompilerParams(vmem_limit_bytes=60 << 20),
        name="convs",
    )(edges, middle, above, below, left, right, corner_above, corner_below, cot, weights)


def gather_kernel(tiles, message, grad, out, turned):
    step = pl.program_id(0)
    sources, _, channels = message.shape
    rows, mid, double = grad.shape
    cells = TS * TS
    bins = out.shape[2] // 2

    @pl.when(step == 0)
    def _():
        for tile in range(mid // 8):
            piece = grad[:, tile * 8 : (tile + 1) * 8, :].astype(F32)
            piece = jnp.stack([piece[:, :, :channels], piece[:, :, channels:]], axis=1)
            turned[tile] = piece.reshape(cells, channels).T.astype(BF)

    lane = lax.broadcasted_iota(jnp.int32, (1, 2 * bins), 1)
    lift = (lane // bins) * cells

    def source(s, carry):
        meta = message[s].astype(jnp.int32)[0:1]
        hot = cell_onehot(jnp.where(meta < cells, meta + lift, 2 * cells), 2 * cells)
        at = step * sources + s
        here = [jnp.minimum(tiles[rank, at], mid // 8 - 1) for rank in range(2)]
        both = jnp.concatenate([turned[here[0]], turned[here[1]]], axis=1)
        out[s] = jnp.dot(both, hot, preferred_element_type=F32).astype(BF)
        return carry

    lax.fori_loop(0, sources, source, 0, unroll=4)


def gather(tiles, message, grad):
    owners, height, channels = message.shape
    chunk = owners // 8
    return pl.pallas_call(
        gather_kernel,
        out_shape=jax.ShapeDtypeStruct((owners, channels, height - 8), BF),
        grid=(owners // chunk,),
        in_specs=[
            pl.BlockSpec(memory_space=pltpu.SMEM),
            pl.BlockSpec((chunk, 8, channels), lambda i: (i, height // 8 - 1, 0)),
            pl.BlockSpec(grad.shape, lambda i: (0, 0, 0)),
        ],
        out_specs=pl.BlockSpec((chunk, channels, height - 8), lambda i: (i, 0, 0)),
        scratch_shapes=[pltpu.VMEM((grad.shape[1] // 8, channels, TS * TS), BF)],
        compiler_params=pltpu.CompilerParams(vmem_limit_bytes=40 << 20),
        name="gather",
    )(tiles, message, grad)


def final_kernel(owner, returned, depth, context, grad_depth, grad_context, count):
    step = pl.program_id(0)
    blocks, bins, _ = depth.shape

    @pl.when(step == 0)
    def _():
        clear_counts(count, returned.shape[0])

    def block(b, carry):
        to = owner[step * blocks + b]
        rank = take_slot(to, count)
        turned = returned[to].astype(F32).T
        rows = jnp.where(rank == 0, turned[0:bins], turned[bins : 2 * bins]).astype(BF)
        grad_depth[b] = lax.dot_general(
            rows, context[b], (((1,), (1,)), ((), ())), preferred_element_type=F32
        ).astype(BF)
        grad_context[b] = lax.dot_general(
            depth[b], rows, (((0,), (0,)), ((), ())), preferred_element_type=F32
        ).astype(BF)
        return carry

    lax.fori_loop(0, blocks, block, 0, unroll=4)


def final(owner, returned, depth, context):
    blocks, bins, pixels = depth.shape
    channels = context.shape[2]
    chunk = blocks // 4
    whole = pl.BlockSpec(returned.shape, lambda i: (0, 0, 0))
    depth_block = pl.BlockSpec((chunk, bins, pixels), lambda i: (i, 0, 0))
    context_block = pl.BlockSpec((chunk, pixels, channels), lambda i: (i, 0, 0))
    return pl.pallas_call(
        final_kernel,
        out_shape=(
            jax.ShapeDtypeStruct(depth.shape, BF),
            jax.ShapeDtypeStruct(context.shape, BF),
        ),
        grid=(blocks // chunk,),
        in_specs=[pl.BlockSpec(memory_space=pltpu.SMEM), whole, depth_block, context_block],
        out_specs=(depth_block, context_block),
        scratch_shapes=[pltpu.SMEM((returned.shape[0],), jnp.int32)],
        compiler_params=pltpu.CompilerParams(vmem_limit_bytes=40 << 20),
        name="final",
    )(owner, returned, depth, context)


def paired_weights(kernel):
    layers, taps, _, inner, outer = kernel.shape
    first = jnp.pad(kernel, ((0, 0), (0, 0), (0, 1), (0, 0), (0, 0)))
    second = jnp.pad(kernel, ((0, 0), (0, 0), (1, 0), (0, 0), (0, 0)))
    return jnp.concatenate([first, second], axis=4).reshape(layers, 4 * taps * inner, 2 * outer)


def per_device(
    depth_weights, context, block_owner, block_local, block_cell, conv_weight, cotangent
):
    cams_here, blocks_cam, bins, pixels = depth_weights.shape
    channels = context.shape[3]
    rows, cols, _ = cotangent.shape
    mid = cols // 2
    axes = ("cam", "tile")
    owners = lax.axis_size(axes)
    blocks = cams_here * blocks_cam
    depth = depth_weights.reshape(blocks, bins, pixels)
    flat_context = context.reshape(blocks, pixels, channels)
    owner = block_owner.reshape(blocks)
    local = block_local.reshape(blocks)

    sent = pack(owner, local, block_cell.reshape(blocks, bins), depth, flat_context, owners)
    message = lax.all_to_all(sent, axes, split_axis=0, concat_axis=0, tiled=True)

    cot = cotangent.reshape(rows, mid, 2 * channels)
    cot = with_sides(with_sides(cot, "tile", 1, PAIRS), "cam", 0, LAYERS)
    turned_weight = conv_weight[:, ::-1, ::-1].swapaxes(3, 4)
    weights = jnp.concatenate([paired_weights(conv_weight), paired_weights(turned_weight)], axis=0)
    cam = lax.axis_index("cam")
    tile = lax.axis_index("tile")
    edges = jnp.stack(
        [cam == 0, cam == lax.axis_size("cam") - 1, tile == 0, tile == lax.axis_size("tile") - 1]
    ).astype(jnp.int32)

    middle, tiles = splat(message, rows, cols)

    down, up = ring("cam")
    east, west = ring("tile")
    above = lax.ppermute(middle[rows - EXT :], "cam", down)
    below = lax.ppermute(middle[:EXT], "cam", up)
    left = lax.ppermute(middle[:, mid - PAIRS :], "tile", east)
    right = lax.ppermute(middle[:, :PAIRS], "tile", west)
    sides = jnp.concatenate([left, right], axis=1)
    corner_above = lax.ppermute(sides[rows - EXT :], "cam", down)
    corner_below = lax.ppermute(sides[:EXT], "cam", up)

    bev, grad = convs(
        edges, middle, above, below, left, right, corner_above, corner_below, cot, weights
    )
    rows_back = gather(tiles, message, grad)
    returned = lax.all_to_all(rows_back, axes, split_axis=0, concat_axis=0, tiled=True)
    grad_depth, grad_context = final(owner, returned, depth, flat_context)
    return (
        bev.reshape(cotangent.shape),
        grad_depth.reshape(depth_weights.shape),
        grad_context.reshape(context.shape),
    )


def solution(mesh):
    placed = (
        P(("cam", "tile"), None, None, None),
        P(("cam", "tile"), None, None, None),
        P(("cam", "tile"), None, None),
        P(("cam", "tile"), None),
        P(("cam", "tile"), None, None),
        P(),
        P("cam", "tile", None),
    )
    return jax.shard_map(
        per_device,
        mesh=mesh,
        in_specs=placed,
        out_specs=(
            P("cam", "tile", None),
            P(("cam", "tile"), None, None, None),
            P(("cam", "tile"), None, None, None),
        ),
        check_vma=False,
    )
```

```python
import functools

import jax
import jax.numpy as jnp
from jax import lax
from jax.experimental import pallas as pl
from jax.experimental.pallas import tpu as pltpu
from jax.sharding import PartitionSpec as P

TS = 16
LAYERS = 4
EXT = 2 * LAYERS
PAIRS = 8
EMPTY = 256.0
ABSENT = 255
BF = jnp.bfloat16
F32 = jnp.float32


def ring(axis):
    count = lax.axis_size(axis)
    ends = count - 1
    down = [(i, i + 1) for i in range(ends)]
    up = [(i + 1, i) for i in range(ends)]
    return down, up


def with_sides(cells, axis, dim, width):
    down, up = ring(axis)
    size = cells.shape[dim]
    head = lax.slice_in_dim(cells, 0, width, axis=dim)
    tail = lax.slice_in_dim(cells, size - width, size, axis=dim)
    return jnp.concatenate(
        [lax.ppermute(tail, axis, down), cells, lax.ppermute(head, axis, up)], axis=dim
    )


def take_slot(owner, count):
    rank = count[owner]
    count[owner] = rank + 1
    return rank


def clear_counts(count, size):
    for i in range(size):
        count[i] = 0


def in_hbm(x):
    return pltpu.with_memory_space_constraint(x, pltpu.HBM)


def spot_of(spots, at, tiles):
    value = spots[at // spots.shape[1], at % spots.shape[1]]
    return value // tiles, value % tiles


def pair_cells(cells):
    return (cells // TS) * TS + (cells % 2) * (TS // 2) + (cells % TS) // 2


def pack_kernel(tile_count, spots, cells, depth, context, out, count, wide, lifted, meta, sems):
    step = pl.program_id(0)
    blocks, bins, _ = depth.shape
    owners = out.shape[0]
    channels = context.shape[2]

    @pl.when(step == 0)
    def _():
        clear_counts(count, owners)
        kind = lax.broadcasted_iota(jnp.int32, meta.shape, 1)
        meta[...] = jnp.where(kind == 0, EMPTY, ABSENT)
        numbers = pair_cells(cells[...]).astype(F32)
        wide[...] = jnp.concatenate([numbers, numbers], axis=1)

    lane = lax.broadcasted_iota(jnp.int32, (1, 2 * bins), 1)

    def block(b, carry):
        at = step * blocks + b
        to, local = spot_of(spots, at, tile_count)
        rank = take_slot(to, count)
        product = jnp.dot(depth[b], context[b], preferred_element_type=F32)
        lifted[at // 2, pl.ds(pl.multiple_of((at % 2) * bins, bins), bins), :] = product.astype(BF)
        mine = (lane // bins) == rank
        row = wide[pl.ds(at, 1), :]
        meta[to, pl.ds(0, 1), :] = jnp.where(mine, row, meta[to, pl.ds(0, 1), :])
        tile = local.astype(F32)
        meta[to, pl.ds(1, 1), :] = jnp.where(mine, tile, meta[to, pl.ds(1, 1), :])
        pltpu.make_async_copy(
            lifted.at[at // 2, pl.ds(pl.multiple_of((at % 2) * bins, bins), bins), :],
            out.at[to, pl.ds(pl.multiple_of(rank * bins, bins), bins), :],
            sems.at[0],
        ).start()
        return carry

    lax.fori_loop(0, blocks, block, 0, unroll=4)

    @pl.when(step == pl.num_programs(0) - 1)
    def _():
        wide_meta = lifted.shape[0]
        def put_meta(small):
            small[...] = meta[...].astype(BF)
            copy = pltpu.make_async_copy(
                small, out.at[:, pl.ds(2 * bins, 8), :], sems.at[1]
            )
            copy.start()
            copy.wait()
        pl.run_scoped(put_meta, pltpu.VMEM(meta.shape, BF))
        pltpu.make_async_copy(
            lifted, out.at[pl.ds(0, wide_meta), pl.ds(0, 2 * bins), :], sems.at[0]
        ).wait()


def pack(spots, cells, depth, context, owners, tile_count):
    blocks, bins, pixels = depth.shape
    channels = context.shape[2]
    chunk = blocks // 4
    return pl.pallas_call(
        functools.partial(pack_kernel, tile_count),
        out_shape=pltpu.HBM((owners, 2 * bins + 8, channels), BF),
        grid=(blocks // chunk,),
        in_specs=[
            pl.BlockSpec(memory_space=pltpu.SMEM),
            pl.BlockSpec(cells.shape, lambda i: (0, 0)),
            pl.BlockSpec((chunk, bins, pixels), lambda i: (i, 0, 0)),
            pl.BlockSpec((chunk, pixels, channels), lambda i: (i, 0, 0)),
        ],
        out_specs=pl.BlockSpec(memory_space=pltpu.HBM),
        scratch_shapes=[
            pltpu.SMEM((owners,), jnp.int32),
            pltpu.VMEM((blocks, 2 * bins), F32),
            pltpu.VMEM((blocks // 2, 2 * bins, channels), BF),
            pltpu.VMEM((owners, 8, 2 * bins), F32),
            pltpu.SemaphoreType.DMA((2,)),
        ],
        compiler_params=pltpu.CompilerParams(vmem_limit_bytes=24 << 20),
        name="pack",
    )(spots, cells, depth, context)


def cell_onehot(cell_row, cells):
    number = lax.broadcasted_iota(jnp.int32, (cells, cell_row.shape[1]), 0)
    return jnp.where(number == cell_row, 1.0, 0.0).astype(BF)


def splat_kernel(meta_all, message, out, tiles_out, even, odd, turned, tiles, sem):
    step = pl.program_id(0)
    sources, rows, channels = message.shape
    bins = (rows - 8) // 2
    cells = TS * TS

    @pl.when(step == 0)
    def _():
        numbers = meta_all[:, 0:8, :].astype(F32)
        flat = numbers[:, 1, :].T
        turned[0:1, :] = flat[0:1].astype(jnp.int32)
        turned[1:2, :] = flat[bins : bins + 1].astype(jnp.int32)
        copy = pltpu.make_async_copy(turned, tiles, sem)
        copy.start()
        even[...] = jnp.zeros(even.shape, F32)
        odd[...] = jnp.zeros(odd.shape, F32)
        copy.wait()

    def source(s, carry):
        meta = message[s, pl.ds(2 * bins, 8), :].astype(jnp.int32)
        hot = cell_onehot(meta[0:1], cells)
        tile = [tiles[rank, step * sources + s] for rank in range(2)]
        nothing = jnp.zeros((bins, channels), BF)
        first = jnp.where(tile[0] < ABSENT, message[s, 0:bins, :], nothing)
        second = jnp.where(tile[1] < ABSENT, message[s, bins : 2 * bins, :], nothing)
        both = jnp.concatenate(
            [
                jnp.concatenate([first, nothing], axis=0),
                jnp.concatenate([nothing, second], axis=0),
            ],
            axis=1,
        )
        sums = jnp.dot(hot, both, preferred_element_type=F32)
        for rank, acc in enumerate((even, odd)):
            here = jnp.minimum(tile[rank], acc.shape[1] // 8 - 1)
            at = pl.ds(pl.multiple_of(here * 8, 8), 8)
            part = sums[:, rank * channels : (rank + 1) * channels].reshape(TS, 2, 8, channels)
            for side in range(2):
                lanes = slice(side * channels, (side + 1) * channels)
                acc[:, at, lanes] += part[:, side]
        return carry

    lax.fori_loop(0, sources, source, 0, unroll=4)

    @pl.when(step == pl.num_programs(0) - 1)
    def _():
        out[...] = (even[...] + odd[...]).astype(BF)
        tiles_out[...] = turned[...]


def splat(message, rows, cols):
    owners, height, channels = message.shape
    chunk = owners // 8
    shape = (rows, cols // 2, 2 * channels)
    return pl.pallas_call(
        splat_kernel,
        out_shape=(
            jax.ShapeDtypeStruct(shape, BF),
            jax.ShapeDtypeStruct((2, owners), jnp.int32),
        ),
        grid=(owners // chunk,),
        in_specs=[
            pl.BlockSpec((owners, 8, channels), lambda i: (0, height // 8 - 1, 0)),
            pl.BlockSpec((chunk, height, channels), lambda i: (i, 0, 0)),
        ],
        out_specs=(
            pl.BlockSpec(shape, lambda i: (0, 0, 0)),
            pl.BlockSpec((2, owners), lambda i: (0, 0)),
        ),
        scratch_shapes=[
            pltpu.VMEM(shape, F32),
            pltpu.VMEM(shape, F32),
            pltpu.VMEM((2, owners), jnp.int32),
            pltpu.SMEM((2, owners), jnp.int32),
            pltpu.SemaphoreType.DMA,
        ],
        compiler_params=pltpu.CompilerParams(vmem_limit_bytes=40 << 20),
        name="splat",
    )(message, message)


def chunks_of(count):
    parts = -(-count // 7)
    size = -(-count // parts)
    return size, [min(i * size, count - size) for i in range(parts)]


def conv_kernel(
    edges, middle, above, below, left, right, corner_above, corner_below, cot_far, weights_far,
    bev, grad, ping, pong, slopes, mask, sums, weights, cot, sems,
):
    rows, mid, double = middle.shape
    channels = double // 2
    wide = mid + 2 * PAIRS
    tall = rows + 2 * EXT
    arrivals = [
        pltpu.make_async_copy(weights_far.at[i], weights.at[i], sems.at[i])
        for i in range(2 * LAYERS)
    ]
    cot_arrival = pltpu.make_async_copy(cot_far, cot, sems.at[2 * LAYERS])
    for copy in arrivals[:LAYERS]:
        copy.start()
    cot_arrival.start()
    for copy in arrivals[: LAYERS - 1 : -1]:
        copy.start()
    column = lax.broadcasted_iota(jnp.int32, (wide, double), 0)
    gone = ((column < PAIRS) & (edges[2] == 1)) | ((column >= wide - PAIRS) & (edges[3] == 1))
    mask[0] = jnp.zeros((wide, double), F32)
    mask[1] = jnp.where(gone, 0.0, 1.0)

    def put(ref, row, value):
        first = value[:, :channels]
        second = value[:, channels:]
        ref[row, :, 0:channels] = pltpu.roll(second, 1, 0).astype(BF)
        ref[row, :, channels : 3 * channels] = value.astype(BF)
        ref[row, :, 3 * channels :] = pltpu.roll(first, wide - 1, 0).astype(BF)

    def load(row, west, center, east):
        put(
            ping, row,
            jnp.concatenate([west.astype(F32), center.astype(F32), east.astype(F32)], axis=0),
        )

    def load_outer(k, carry):
        load(k, corner_above[k, 0:PAIRS], above[k], corner_above[k, PAIRS:])
        load(EXT + rows + k, corner_below[k, 0:PAIRS], below[k], corner_below[k, PAIRS:])
        return carry

    def load_inner(k, carry):
        load(EXT + k, left[k], middle[k], right[k])
        return carry

    lax.fori_loop(0, EXT, load_outer, 0)
    lax.fori_loop(0, rows, load_inner, 0)

    def matmul(ref, index, start, size):
        taps = [ref[pl.ds(start + tap, size)].reshape(size * wide, 2 * double) for tap in range(3)]
        total = jnp.dot(
            jnp.concatenate(taps, axis=1), weights[index], preferred_element_type=F32
        )
        sums[0:size] = total.reshape(size, wide, double)

    kept = [tall - 2 - 2 * layer for layer in range(LAYERS)]
    offsets = [sum(kept[:layer]) for layer in range(LAYERS)]

    def forward(layer, target, start, size):
        for side in range(size):
            here = start + side
            row = layer + 1 + here
            inside = jnp.where(
                ((row < EXT) & (edges[0] == 1)) | ((row >= EXT + rows) & (edges[1] == 1)), 0, 1
            )
            part = sums[side]
            flag = mask[inside]
            twice = flag + flag * jnp.tanh(part)
            active = part * twice
            slope = twice + active * (2.0 - twice)
            if layer < LAYERS - 1:
                put(target, here, active)
                slopes[offsets[layer] + here] = slope.astype(slopes.dtype)
            else:
                bev[here] = active[PAIRS : PAIRS + mid].astype(BF)
                put(target, here, cot[here].astype(F32) * slope)

    def backward(step, target, start, size):
        layer = LAYERS - 1 - step
        for side in range(size):
            here = start + side
            if layer > 0:
                slope = slopes[offsets[layer - 1] + here + 2 * (step + 1)].astype(F32)
                put(target, here, sums[side] * slope)
            else:
                grad[here] = sums[side, PAIRS : PAIRS + mid].astype(BF)

    stages = []
    for layer in range(LAYERS):
        stages.append((layer, kept[layer], functools.partial(forward, layer)))
    for step in range(LAYERS):
        layer = LAYERS - 1 - step
        stages.append((LAYERS + layer, rows + 2 * layer, functools.partial(backward, step)))

    source, target = ping, pong
    finish = None
    for index, count, epilogue in stages:
        size, starts = chunks_of(count)
        arrivals[index].wait()
        if finish is not None:
            finish()
        matmul(source, index, 0, size)
        if index == LAYERS - 1:
            cot_arrival.wait()

        def steady(k, carry, index=index, count=count, size=size, source=source, target=target, epilogue=epilogue):
            epilogue(target, (k - 1) * size, size)
            matmul(source, index, jnp.minimum(k * size, count - size), size)
            return carry

        lax.fori_loop(1, len(starts), steady, 0)
        finish = functools.partial(epilogue, target, starts[-1], size)
        source, target = target, source
    finish()


def convs(edges, middle, above, below, left, right, corner_above, corner_below, cot, weights):
    rows, mid, double = middle.shape
    wide = mid + 2 * PAIRS
    tall = rows + 2 * EXT
    kept = sum(tall - 2 - 2 * layer for layer in range(LAYERS - 1))
    vmem = pl.BlockSpec(memory_space=pltpu.VMEM)
    hbm = pl.BlockSpec(memory_space=pltpu.HBM)
    buffer = pltpu.VMEM((tall, wide, 2 * double), BF)
    return pl.pallas_call(
        conv_kernel,
        out_shape=(
            jax.ShapeDtypeStruct((rows + 2 * LAYERS, mid, double), BF),
            jax.ShapeDtypeStruct(middle.shape, BF),
        ),
        in_specs=[pl.BlockSpec(memory_space=pltpu.SMEM)] + [vmem] * 7 + [hbm] * 2,
        out_specs=(vmem, vmem),
        scratch_shapes=[
            buffer,
            buffer,
            pltpu.VMEM((kept, wide, double), F32),
            pltpu.VMEM((2, wide, double), F32),
            pltpu.VMEM((7, wide, double), F32),
            pltpu.VMEM(weights.shape, BF),
            pltpu.VMEM(cot.shape, BF),
            pltpu.SemaphoreType.DMA((2 * LAYERS + 1,)),
        ],
        compiler_params=pltpu.CompilerParams(vmem_limit_bytes=48 << 20),
        name="convs",
    )(
        edges, middle, above, below, left, right, corner_above, corner_below,
        in_hbm(cot), in_hbm(weights),
    )


def gather_kernel(tiles, message, grad, out, turned):
    step = pl.program_id(0)
    sources, _, channels = message.shape
    rows, mid, double = grad.shape
    cells = TS * TS
    bins = out.shape[2] // 2

    @pl.when(step == 0)
    def _():
        for tile in range(mid // 8):
            piece = grad[:, tile * 8 : (tile + 1) * 8, :].astype(F32)
            piece = jnp.stack([piece[:, :, :channels], piece[:, :, channels:]], axis=1)
            turned[tile] = piece.reshape(cells, channels).T.astype(BF)

    lane = lax.broadcasted_iota(jnp.int32, (1, 2 * bins), 1)
    lift = (lane // bins) * cells

    def source(s, carry):
        meta = message[s].astype(jnp.int32)[0:1]
        hot = cell_onehot(jnp.where(meta < cells, meta + lift, 2 * cells), 2 * cells)
        at = step * sources + s
        here = [jnp.minimum(tiles[rank, at], mid // 8 - 1) for rank in range(2)]
        both = jnp.concatenate([turned[here[0]], turned[here[1]]], axis=1)
        out[s] = jnp.dot(both, hot, preferred_element_type=F32).astype(BF)
        return carry

    lax.fori_loop(0, sources, source, 0, unroll=4)


def gather(tiles, message, grad):
    owners, height, channels = message.shape
    chunk = owners // 8
    return pl.pallas_call(
        gather_kernel,
        out_shape=pltpu.HBM((owners, channels, height - 8), BF),
        grid=(owners // chunk,),
        in_specs=[
            pl.BlockSpec(memory_space=pltpu.SMEM),
            pl.BlockSpec((chunk, 8, channels), lambda i: (i, height // 8 - 1, 0)),
            pl.BlockSpec(grad.shape, lambda i: (0, 0, 0)),
        ],
        out_specs=pl.BlockSpec((chunk, channels, height - 8), lambda i: (i, 0, 0)),
        scratch_shapes=[pltpu.VMEM((grad.shape[1] // 8, channels, TS * TS), BF)],
        compiler_params=pltpu.CompilerParams(vmem_limit_bytes=40 << 20),
        name="gather",
    )(tiles, message, grad)


def final_kernel(tile_count, spots, returned, depth, context, grad_depth, grad_context, count):
    step = pl.program_id(0)
    blocks, bins, _ = depth.shape

    @pl.when(step == 0)
    def _():
        clear_counts(count, returned.shape[0])

    def block(b, carry):
        to, _ = spot_of(spots, step * blocks + b, tile_count)
        rank = take_slot(to, count)
        turned = returned[to].T
        rows = jnp.where(rank == 0, turned[0:bins], turned[bins : 2 * bins])
        grad_depth[b] = lax.dot_general(
            rows, context[b], (((1,), (1,)), ((), ())), preferred_element_type=F32
        ).astype(BF)
        grad_context[b] = lax.dot_general(
            depth[b], rows, (((0,), (0,)), ((), ())), preferred_element_type=F32
        ).astype(BF)
        return carry

    lax.fori_loop(0, blocks, block, 0, unroll=4)


def final(spots, returned, depth, context, tile_count):
    blocks, bins, pixels = depth.shape
    channels = context.shape[2]
    chunk = blocks // 4
    whole = pl.BlockSpec(returned.shape, lambda i: (0, 0, 0))
    depth_block = pl.BlockSpec((chunk, bins, pixels), lambda i: (i, 0, 0))
    context_block = pl.BlockSpec((chunk, pixels, channels), lambda i: (i, 0, 0))
    return pl.pallas_call(
        functools.partial(final_kernel, tile_count),
        out_shape=(
            jax.ShapeDtypeStruct(depth.shape, BF),
            jax.ShapeDtypeStruct(context.shape, BF),
        ),
        grid=(blocks // chunk,),
        in_specs=[pl.BlockSpec(memory_space=pltpu.SMEM), whole, depth_block, context_block],
        out_specs=(depth_block, context_block),
        scratch_shapes=[pltpu.SMEM((returned.shape[0],), jnp.int32)],
        compiler_params=pltpu.CompilerParams(vmem_limit_bytes=40 << 20),
        name="final",
    )(spots, in_hbm(returned), depth, context)


def paired_weights(kernel):
    layers, taps, _, inner, outer = kernel.shape
    first = jnp.pad(kernel, ((0, 0), (0, 0), (0, 1), (0, 0), (0, 0)))
    second = jnp.pad(kernel, ((0, 0), (0, 0), (1, 0), (0, 0), (0, 0)))
    return jnp.concatenate([first, second], axis=4).reshape(layers, 4 * taps * inner, 2 * outer)


def per_device(
    depth_weights, context, block_owner, block_local, block_cell, conv_weight, cotangent
):
    cams_here, blocks_cam, bins, pixels = depth_weights.shape
    channels = context.shape[3]
    rows, cols, _ = cotangent.shape
    mid = cols // 2
    axes = ("cam", "tile")
    owners = lax.axis_size(axes)
    blocks = cams_here * blocks_cam
    depth = depth_weights.reshape(blocks, bins, pixels)
    flat_context = context.reshape(blocks, pixels, channels)
    tile_count = cols // TS
    spots = block_owner[:, :, 0] * tile_count + block_local

    sent = pack(
        spots, block_cell.reshape(blocks, bins), in_hbm(depth), in_hbm(flat_context), owners, tile_count
    )
    message = lax.all_to_all(sent, axes, split_axis=0, concat_axis=0, tiled=True)

    cot = cotangent.reshape(rows, mid, 2 * channels)
    cot = with_sides(with_sides(cot, "tile", 1, PAIRS), "cam", 0, LAYERS)
    turned_weight = conv_weight[:, ::-1, ::-1].swapaxes(3, 4)
    weights = jnp.concatenate([paired_weights(conv_weight), paired_weights(turned_weight)], axis=0)
    weights = weights * jnp.asarray(0.5, BF)
    cam = lax.axis_index("cam")
    tile = lax.axis_index("tile")
    edges = jnp.stack(
        [cam == 0, cam == lax.axis_size("cam") - 1, tile == 0, tile == lax.axis_size("tile") - 1]
    ).astype(jnp.int32)

    middle, tiles = splat(message, rows, cols)

    down, up = ring("cam")
    east, west = ring("tile")
    above = lax.ppermute(middle[rows - EXT :], "cam", down)
    below = lax.ppermute(middle[:EXT], "cam", up)
    left = lax.ppermute(middle[:, mid - PAIRS :], "tile", east)
    right = lax.ppermute(middle[:, :PAIRS], "tile", west)
    sides = jnp.concatenate([left, right], axis=1)
    corner_above = lax.ppermute(sides[rows - EXT :], "cam", down)
    corner_below = lax.ppermute(sides[:EXT], "cam", up)

    bev, grad = convs(
        edges, middle, above, below, left, right, corner_above, corner_below, cot, weights
    )
    rows_back = gather(tiles, message, grad)
    returned = lax.all_to_all(rows_back, axes, split_axis=0, concat_axis=0, tiled=True)
    grad_depth, grad_context = final(
        spots, returned, in_hbm(depth), in_hbm(flat_context), tile_count
    )
    return (
        bev[LAYERS : LAYERS + rows].reshape(cotangent.shape),
        grad_depth.reshape(depth_weights.shape),
        grad_context.reshape(context.shape),
    )


def solution(mesh):
    placed = (
        P(("cam", "tile"), None, None, None),
        P(("cam", "tile"), None, None, None),
        P(("cam", "tile"), None, None),
        P(("cam", "tile"), None),
        P(("cam", "tile"), None, None),
        P(),
        P("cam", "tile", None),
    )
    return jax.shard_map(
        per_device,
        mesh=mesh,
        in_specs=placed,
        out_specs=(
            P("cam", "tile", None),
            P(("cam", "tile"), None, None, None),
            P(("cam", "tile"), None, None, None),
        ),
        check_vma=False,
    )
```

```python
import functools

import jax
import jax.numpy as jnp
from jax import lax
from jax.experimental import pallas as pl
from jax.experimental.pallas import tpu as pltpu
from jax.sharding import PartitionSpec as P

TS = 16
LAYERS = 4
EXT = 2 * LAYERS
PAIRS = 8
EMPTY = 256.0
ABSENT = 255
BF = jnp.bfloat16
F32 = jnp.float32


def ring(axis):
    count = lax.axis_size(axis)
    ends = count - 1
    down = [(i, i + 1) for i in range(ends)]
    up = [(i + 1, i) for i in range(ends)]
    return down, up


def take_slot(owner, count):
    rank = count[owner]
    count[owner] = rank + 1
    return rank


def clear_counts(count, size):
    for i in range(size):
        count[i] = 0


def in_hbm(x):
    return pltpu.with_memory_space_constraint(x, pltpu.HBM)


def owner_of(owner, at):
    each = owner.shape[2]
    return owner[lax.div(at, each), 0, lax.rem(at, each)]


def pair_cells(cells):
    return (cells // TS) * TS + (cells % 2) * (TS // 2) + (cells % TS) // 2


def pack_kernel(owner, local, cells, depth, context, out, count, wide, lifted, meta, sems):
    step = pl.program_id(0)
    blocks, bins, _ = depth.shape
    owners = out.shape[0]

    @pl.when(step == 0)
    def _():
        clear_counts(count, owners)
        kind = lax.broadcasted_iota(jnp.int32, meta.shape, 1)
        meta[...] = jnp.where(kind == 0, EMPTY, ABSENT)
        numbers = pair_cells(cells[...]).astype(F32).reshape(wide.shape[0], bins)
        wide[...] = jnp.concatenate([numbers, numbers], axis=1)

    lane = lax.broadcasted_iota(jnp.int32, (1, 2 * bins), 1)

    def block(b, carry):
        at = step * blocks + b
        to = owner_of(owner, at)
        each = local.shape[1]
        tile = local[lax.div(at, each), lax.rem(at, each)].astype(F32)
        rank = take_slot(to, count)
        product = jnp.dot(depth[b], context[b], preferred_element_type=F32)
        lifted[lax.div(at, 2), pl.ds(pl.multiple_of(lax.rem(at, 2) * bins, bins), bins), :] = product.astype(BF)
        mine = (lane // bins) == rank
        row = wide[pl.ds(at, 1), :]
        meta[to, pl.ds(0, 1), :] = jnp.where(mine, row, meta[to, pl.ds(0, 1), :])
        meta[to, pl.ds(1, 1), :] = jnp.where(mine, tile, meta[to, pl.ds(1, 1), :])
        pltpu.make_async_copy(
            lifted.at[lax.div(at, 2), pl.ds(pl.multiple_of(lax.rem(at, 2) * bins, bins), bins), :],
            out.at[to, pl.ds(pl.multiple_of(rank * bins, bins), bins), :],
            sems.at[0],
        ).start()
        return carry

    lax.fori_loop(0, blocks, block, 0, unroll=4)

    @pl.when(step == pl.num_programs(0) - 1)
    def _():
        wide_meta = lifted.shape[0]

        def put_meta(small):
            small[...] = meta[...].astype(BF)
            copy = pltpu.make_async_copy(
                small, out.at[:, pl.ds(2 * bins, 8), :], sems.at[1]
            )
            copy.start()
            copy.wait()

        pl.run_scoped(put_meta, pltpu.VMEM(meta.shape, BF))
        pltpu.make_async_copy(
            lifted, out.at[pl.ds(0, wide_meta), pl.ds(0, 2 * bins), :], sems.at[0]
        ).wait()


def pack(owner, local, cells, depth, context, owners):
    blocks, bins, pixels = depth.shape
    channels = context.shape[2]
    chunk = blocks // 4
    return pl.pallas_call(
        pack_kernel,
        out_shape=pltpu.HBM((owners, 2 * bins + 8, channels), BF),
        grid=(blocks // chunk,),
        in_specs=[
            pl.BlockSpec(memory_space=pltpu.SMEM),
            pl.BlockSpec(memory_space=pltpu.SMEM),
            pl.BlockSpec(cells.shape, lambda i: (0, 0, 0)),
            pl.BlockSpec((chunk, bins, pixels), lambda i: (i, 0, 0)),
            pl.BlockSpec((chunk, pixels, channels), lambda i: (i, 0, 0)),
        ],
        out_specs=pl.BlockSpec(memory_space=pltpu.HBM),
        scratch_shapes=[
            pltpu.SMEM((owners,), jnp.int32),
            pltpu.VMEM((blocks, 2 * bins), F32),
            pltpu.VMEM((blocks // 2, 2 * bins, channels), BF),
            pltpu.VMEM((owners, 8, 2 * bins), F32),
            pltpu.SemaphoreType.DMA((2,)),
        ],
        compiler_params=pltpu.CompilerParams(vmem_limit_bytes=24 << 20),
        name="pack",
    )(owner, local, cells, depth, context)


def cell_onehot(cell_row, cells):
    number = lax.broadcasted_iota(jnp.int32, (cells, cell_row.shape[1]), 0)
    return jnp.where(number == cell_row, 1.0, 0.0).astype(BF)


def splat_kernel(meta_all, message, out, tiles_out, even, odd, turned, tiles, sem):
    step = pl.program_id(0)
    sources, rows, channels = message.shape
    bins = (rows - 8) // 2
    cells = TS * TS

    @pl.when(step == 0)
    def _():
        numbers = meta_all[:, 0:8, :].astype(F32)
        flat = numbers[:, 1, :].T
        turned[0:1, :] = flat[0:1].astype(jnp.int32)
        turned[1:2, :] = flat[bins : bins + 1].astype(jnp.int32)
        copy = pltpu.make_async_copy(turned, tiles, sem)
        copy.start()
        even[...] = jnp.zeros(even.shape, F32)
        odd[...] = jnp.zeros(odd.shape, F32)
        copy.wait()

    def source(s, carry):
        meta = message[s, pl.ds(2 * bins, 8), :].astype(jnp.int32)
        hot = cell_onehot(meta[0:1], cells)
        tile = [tiles[rank, step * sources + s] for rank in range(2)]
        nothing = jnp.zeros((bins, channels), BF)
        first = jnp.where(tile[0] < ABSENT, message[s, 0:bins, :], nothing)
        second = jnp.where(tile[1] < ABSENT, message[s, bins : 2 * bins, :], nothing)
        both = jnp.concatenate(
            [
                jnp.concatenate([first, nothing], axis=0),
                jnp.concatenate([nothing, second], axis=0),
            ],
            axis=1,
        )
        sums = jnp.dot(hot, both, preferred_element_type=F32)
        for rank, acc in enumerate((even, odd)):
            here = jnp.minimum(tile[rank], acc.shape[1] // 8 - 1)
            at = pl.ds(pl.multiple_of(here * 8, 8), 8)
            part = sums[:, rank * channels : (rank + 1) * channels].reshape(TS, 2, 8, channels)
            for side in range(2):
                lanes = slice(side * channels, (side + 1) * channels)
                acc[:, at, lanes] += part[:, side]
        return carry

    lax.fori_loop(0, sources, source, 0, unroll=8)

    @pl.when(step == pl.num_programs(0) - 1)
    def _():
        out[...] = (even[...] + odd[...]).astype(BF)
        tiles_out[...] = turned[...]


def splat(message, rows, cols):
    owners, height, channels = message.shape
    chunk = owners // 8
    shape = (rows, cols // 2, 2 * channels)
    return pl.pallas_call(
        splat_kernel,
        out_shape=(
            jax.ShapeDtypeStruct(shape, BF),
            jax.ShapeDtypeStruct((2, owners), jnp.int32),
        ),
        grid=(owners // chunk,),
        in_specs=[
            pl.BlockSpec((owners, 8, channels), lambda i: (0, height // 8 - 1, 0)),
            pl.BlockSpec((chunk, height, channels), lambda i: (i, 0, 0)),
        ],
        out_specs=(
            pl.BlockSpec(shape, lambda i: (0, 0, 0)),
            pl.BlockSpec((2, owners), lambda i: (0, 0)),
        ),
        scratch_shapes=[
            pltpu.VMEM(shape, F32),
            pltpu.VMEM(shape, F32),
            pltpu.VMEM((2, owners), jnp.int32),
            pltpu.SMEM((2, owners), jnp.int32),
            pltpu.SemaphoreType.DMA,
        ],
        compiler_params=pltpu.CompilerParams(vmem_limit_bytes=40 << 20),
        name="splat",
    )(message, message)


def chunks_of(count):
    parts = -(-count // 7)
    size = -(-count // parts)
    return size, [min(i * size, count - size) for i in range(parts)]


def conv_kernel(
    edges, middle, above, below, left, right, corner_above, corner_below,
    cot_middle, cot_above, cot_below, cot_left, cot_right, weights_far,
    bev, grad, ping, pong, slopes, mask, sums, weights, cot, sems,
):
    rows, mid, double = middle.shape
    channels = double // 2
    wide = mid + 2 * PAIRS
    tall = rows + 2 * EXT
    arrivals = [
        pltpu.make_async_copy(weights_far.at[i], weights.at[i], sems.at[i])
        for i in range(2 * LAYERS)
    ]
    for copy in arrivals[:LAYERS]:
        copy.start()
    for copy in arrivals[: LAYERS - 1 : -1]:
        copy.start()
    column = lax.broadcasted_iota(jnp.int32, (wide, double), 0)
    gone = ((column < PAIRS) & (edges[2] == 1)) | ((column >= wide - PAIRS) & (edges[3] == 1))
    mask[0] = jnp.zeros((wide, double), F32)
    mask[1] = jnp.where(gone, 0.0, 1.0)

    def put(ref, row, value):
        first = value[:, :channels]
        second = value[:, channels:]
        ref[row, :, 0:channels] = pltpu.roll(second, 1, 0).astype(BF)
        ref[row, :, channels : 3 * channels] = value.astype(BF)
        ref[row, :, 3 * channels :] = pltpu.roll(first, wide - 1, 0).astype(BF)

    def joined(west, center, east):
        return jnp.concatenate([west.astype(F32), center.astype(F32), east.astype(F32)], axis=0)

    def load(row, west, center, east):
        put(ping, row, joined(west, center, east))

    def load_outer(k, carry):
        load(k, corner_above[k, 0:PAIRS], above[k], corner_above[k, PAIRS:])
        load(EXT + rows + k, corner_below[k, 0:PAIRS], below[k], corner_below[k, PAIRS:])
        return carry

    def load_inner(k, carry):
        load(EXT + k, left[k], middle[k], right[k])
        return carry

    lax.fori_loop(0, EXT, load_outer, 0)

    def load_cot(k, carry):
        cot[LAYERS + k] = joined(cot_left[k], cot_middle[k], cot_right[k]).astype(BF)
        return carry

    lax.fori_loop(0, rows, load_inner, 0)
    lax.fori_loop(0, rows, load_cot, 0)
    for k in range(LAYERS):
        for corner, field, base in (
            (corner_above, cot_above, 0), (corner_below, cot_below, LAYERS + rows)
        ):
            west, east = corner[EXT + k, 0:PAIRS], corner[EXT + k, PAIRS:]
            cot[base + k] = joined(west, field[k], east).astype(BF)

    def matmul(ref, index, start, size):
        taps = [ref[pl.ds(start + tap, size)].reshape(size * wide, 2 * double) for tap in range(3)]
        total = jnp.dot(
            jnp.concatenate(taps, axis=1), weights[index], preferred_element_type=F32
        )
        sums[0:size] = total.reshape(size, wide, double)

    kept = [tall - 2 - 2 * layer for layer in range(LAYERS)]
    offsets = [sum(kept[:layer]) for layer in range(LAYERS)]

    def forward(layer, target, start, size):
        for side in range(size):
            here = start + side
            row = layer + 1 + here
            inside = jnp.where(
                ((row < EXT) & (edges[0] == 1)) | ((row >= EXT + rows) & (edges[1] == 1)), 0, 1
            )
            part = sums[side]
            flag = mask[inside]
            twice = flag + flag * jnp.tanh(part)
            active = part * twice
            slope = twice + active * (2.0 - twice)
            if layer < LAYERS - 1:
                put(target, here, active)
                slopes[offsets[layer] + here] = slope.astype(slopes.dtype)
            else:
                bev[here] = active[PAIRS : PAIRS + mid].astype(BF)
                put(target, here, cot[here].astype(F32) * slope)

    def backward(step, target, start, size):
        layer = LAYERS - 1 - step
        for side in range(size):
            here = start + side
            if layer > 0:
                slope = slopes[offsets[layer - 1] + here + 2 * (step + 1)].astype(F32)
                put(target, here, sums[side] * slope)
            else:
                grad[here] = sums[side, PAIRS : PAIRS + mid].astype(BF)

    stages = []
    for layer in range(LAYERS):
        stages.append((layer, kept[layer], functools.partial(forward, layer)))
    for step in range(LAYERS):
        layer = LAYERS - 1 - step
        stages.append((LAYERS + layer, rows + 2 * layer, functools.partial(backward, step)))

    source, target = ping, pong
    finish = None
    for index, count, epilogue in stages:
        size, starts = chunks_of(count)
        arrivals[index].wait()
        if finish is not None:
            finish()
        matmul(source, index, 0, size)

        def steady(k, carry, index=index, count=count, size=size, source=source, target=target, epilogue=epilogue):
            epilogue(target, (k - 1) * size, size)
            matmul(source, index, jnp.minimum(k * size, count - size), size)
            return carry

        lax.fori_loop(1, len(starts), steady, 0)
        finish = functools.partial(epilogue, target, starts[-1], size)
        source, target = target, source
    finish()


def convs(edges, weights, *fields):
    middle = fields[0]
    rows, mid, double = middle.shape
    wide = mid + 2 * PAIRS
    tall = rows + 2 * EXT
    kept = sum(tall - 2 - 2 * layer for layer in range(LAYERS - 1))
    vmem = pl.BlockSpec(memory_space=pltpu.VMEM)
    hbm = pl.BlockSpec(memory_space=pltpu.HBM)
    buffer = pltpu.VMEM((tall, wide, 2 * double), BF)
    return pl.pallas_call(
        conv_kernel,
        out_shape=(
            jax.ShapeDtypeStruct((rows + 2 * LAYERS, mid, double), BF),
            jax.ShapeDtypeStruct(middle.shape, BF),
        ),
        in_specs=[pl.BlockSpec(memory_space=pltpu.SMEM)] + [vmem] * len(fields) + [hbm],
        out_specs=(vmem, vmem),
        scratch_shapes=[
            buffer,
            buffer,
            pltpu.VMEM((kept, wide, double), F32),
            pltpu.VMEM((2, wide, double), F32),
            pltpu.VMEM((7, wide, double), F32),
            pltpu.VMEM(weights.shape, BF),
            pltpu.VMEM((rows + 2 * LAYERS, wide, double), BF),
            pltpu.SemaphoreType.DMA((2 * LAYERS,)),
        ],
        compiler_params=pltpu.CompilerParams(vmem_limit_bytes=48 << 20),
        name="convs",
    )(edges, *fields, in_hbm(weights))


def gather_kernel(tiles, message, grad, out, turned):
    step = pl.program_id(0)
    sources, _, channels = message.shape
    _, mid, _ = grad.shape
    cells = TS * TS
    bins = out.shape[2] // 2

    @pl.when(step == 0)
    def _():
        for tile in range(mid // 8):
            piece = grad[:, tile * 8 : (tile + 1) * 8, :].astype(F32)
            piece = jnp.stack([piece[:, :, :channels], piece[:, :, channels:]], axis=1)
            turned[tile] = piece.reshape(cells, channels).T.astype(BF)

    lane = lax.broadcasted_iota(jnp.int32, (1, 2 * bins), 1)

    def source(s, carry):
        hot = cell_onehot(message[s].astype(jnp.int32)[0:1], cells)
        at = step * sources + s
        here = [jnp.minimum(tiles[rank, at], mid // 8 - 1) for rank in range(2)]
        both = jnp.concatenate([turned[here[0]], turned[here[1]]], axis=0)
        picked = jnp.dot(both, hot, preferred_element_type=F32)
        out[s] = jnp.where(lane < bins, picked[:channels], picked[channels:]).astype(BF)
        return carry

    lax.fori_loop(0, sources, source, 0, unroll=8)


def gather(tiles, message, grad):
    owners, height, channels = message.shape
    chunk = owners // 8
    return pl.pallas_call(
        gather_kernel,
        out_shape=pltpu.HBM((owners, channels, height - 8), BF),
        grid=(owners // chunk,),
        in_specs=[
            pl.BlockSpec(memory_space=pltpu.SMEM),
            pl.BlockSpec((chunk, 8, channels), lambda i: (i, height // 8 - 1, 0)),
            pl.BlockSpec(grad.shape, lambda i: (0, 0, 0)),
        ],
        out_specs=pl.BlockSpec((chunk, channels, height - 8), lambda i: (i, 0, 0)),
        scratch_shapes=[pltpu.VMEM((grad.shape[1] // 8, channels, TS * TS), BF)],
        compiler_params=pltpu.CompilerParams(vmem_limit_bytes=40 << 20),
        name="gather",
    )(tiles, message, grad)


def final_kernel(owner, returned, depth, context, grad_depth, grad_context, count):
    step = pl.program_id(0)
    blocks, bins, _ = depth.shape

    @pl.when(step == 0)
    def _():
        clear_counts(count, returned.shape[0])

    def block(b, carry):
        to = owner_of(owner, step * blocks + b)
        rank = take_slot(to, count)
        turned = returned[to].T
        rows = jnp.where(rank == 0, turned[0:bins], turned[bins : 2 * bins])
        grad_depth[b] = lax.dot_general(
            rows, context[b], (((1,), (1,)), ((), ())), preferred_element_type=F32
        ).astype(BF)
        grad_context[b] = lax.dot_general(
            depth[b], rows, (((0,), (0,)), ((), ())), preferred_element_type=F32
        ).astype(BF)
        return carry

    lax.fori_loop(0, blocks, block, 0, unroll=8)


def final(owner, returned, depth, context):
    blocks, bins, pixels = depth.shape
    channels = context.shape[2]
    chunk = blocks // 4
    whole = pl.BlockSpec(returned.shape, lambda i: (0, 0, 0))
    depth_block = pl.BlockSpec((chunk, bins, pixels), lambda i: (i, 0, 0))
    context_block = pl.BlockSpec((chunk, pixels, channels), lambda i: (i, 0, 0))
    return pl.pallas_call(
        final_kernel,
        out_shape=(
            jax.ShapeDtypeStruct(depth.shape, BF),
            jax.ShapeDtypeStruct(context.shape, BF),
        ),
        grid=(blocks // chunk,),
        in_specs=[pl.BlockSpec(memory_space=pltpu.SMEM), whole, depth_block, context_block],
        out_specs=(depth_block, context_block),
        scratch_shapes=[pltpu.SMEM((returned.shape[0],), jnp.int32)],
        compiler_params=pltpu.CompilerParams(vmem_limit_bytes=40 << 20),
        name="final",
    )(owner, in_hbm(returned), depth, context)


def paired_weights(kernel):
    layers, taps, _, inner, outer = kernel.shape
    first = jnp.pad(kernel, ((0, 0), (0, 0), (0, 1), (0, 0), (0, 0)))
    second = jnp.pad(kernel, ((0, 0), (0, 0), (1, 0), (0, 0), (0, 0)))
    return jnp.concatenate([first, second], axis=4).reshape(layers, 4 * taps * inner, 2 * outer)


def per_device(
    depth_weights, context, block_owner, block_local, block_cell, conv_weight, cotangent
):
    cams_here, blocks_cam, bins, pixels = depth_weights.shape
    channels = context.shape[3]
    rows, cols, _ = cotangent.shape
    mid = cols // 2
    axes = ("cam", "tile")
    owners = lax.axis_size(axes)
    blocks = cams_here * blocks_cam
    depth = depth_weights.reshape(blocks, bins, pixels)
    flat_context = context.reshape(blocks, pixels, channels)
    owner = block_owner.transpose(0, 2, 1)

    sent = pack(
        in_hbm(owner), in_hbm(block_local), in_hbm(block_cell), in_hbm(depth),
        in_hbm(flat_context), owners,
    )
    message = lax.all_to_all(sent, axes, split_axis=0, concat_axis=0, tiled=True)

    cot = cotangent.reshape(rows, mid, 2 * channels)
    down, up = ring("cam")
    east, west = ring("tile")
    cot_above = lax.ppermute(cot[rows - LAYERS :], "cam", down)
    cot_below = lax.ppermute(cot[:LAYERS], "cam", up)
    cot_left = lax.ppermute(cot[:, mid - PAIRS :], "tile", east)
    cot_right = lax.ppermute(cot[:, :PAIRS], "tile", west)
    turned_weight = conv_weight[:, ::-1, ::-1].swapaxes(3, 4)
    weights = jnp.concatenate([paired_weights(conv_weight), paired_weights(turned_weight)], axis=0)
    weights = weights * jnp.asarray(0.5, BF)
    cam = lax.axis_index("cam")
    tile = lax.axis_index("tile")
    edges = jnp.stack(
        [cam == 0, cam == lax.axis_size("cam") - 1, tile == 0, tile == lax.axis_size("tile") - 1]
    ).astype(jnp.int32)

    middle, tiles = splat(message, rows, cols)

    above = lax.ppermute(middle[rows - EXT :], "cam", down)
    below = lax.ppermute(middle[:EXT], "cam", up)
    left = lax.ppermute(middle[:, mid - PAIRS :], "tile", east)
    right = lax.ppermute(middle[:, :PAIRS], "tile", west)
    sides = jnp.concatenate([left, right], axis=1)
    cot_sides = jnp.concatenate([cot_left, cot_right], axis=1)
    corner_above = lax.ppermute(
        jnp.concatenate([sides[rows - EXT :], cot_sides[rows - LAYERS :]], axis=0), "cam", down
    )
    corner_below = lax.ppermute(
        jnp.concatenate([sides[:EXT], cot_sides[:LAYERS]], axis=0), "cam", up
    )

    bev, grad = convs(
        edges, weights, middle, above, below, left, right, corner_above, corner_below,
        cot, cot_above, cot_below, cot_left, cot_right,
    )
    rows_back = gather(tiles, message, grad)
    returned = lax.all_to_all(rows_back, axes, split_axis=0, concat_axis=0, tiled=True)
    grad_depth, grad_context = final(owner, returned, in_hbm(depth), in_hbm(flat_context))
    return (
        bev[LAYERS : LAYERS + rows].reshape(cotangent.shape),
        grad_depth.reshape(depth_weights.shape),
        grad_context.reshape(context.shape),
    )


def solution(mesh):
    placed = (
        P(("cam", "tile"), None, None, None),
        P(("cam", "tile"), None, None, None),
        P(("cam", "tile"), None, None),
        P(("cam", "tile"), None),
        P(("cam", "tile"), None, None),
        P(),
        P("cam", "tile", None),
    )
    return jax.shard_map(
        per_device,
        mesh=mesh,
        in_specs=placed,
        out_specs=(
            P("cam", "tile", None),
            P(("cam", "tile"), None, None, None),
            P(("cam", "tile"), None, None, None),
        ),
        check_vma=False,
    )
```

```python
import functools

import jax
import jax.numpy as jnp
from jax import lax
from jax.experimental import pallas as pl
from jax.experimental.pallas import tpu as pltpu
from jax.sharding import PartitionSpec as P

TS = 16
LAYERS = 4
EXT = 2 * LAYERS
PAIRS = 8
EMPTY = 256.0
ABSENT = 255
BF = jnp.bfloat16
F32 = jnp.float32


def ring(axis):
    count = lax.axis_size(axis)
    ends = count - 1
    down = [(i, i + 1) for i in range(ends)]
    up = [(i + 1, i) for i in range(ends)]
    return down, up


def take_slot(owner, count):
    rank = count[owner]
    count[owner] = rank + 1
    return rank


def clear_counts(count, size):
    for i in range(size):
        count[i] = 0


def in_hbm(x):
    return pltpu.with_memory_space_constraint(x, pltpu.HBM)


def owner_of(owner, at):
    each = owner.shape[2]
    return owner[lax.div(at, each), 0, lax.rem(at, each)]


def pair_cells(cells):
    return (cells // TS) * TS + (cells % 2) * (TS // 2) + (cells % TS) // 2


def pack_kernel(
    owner, local, cells, depth, context, out, slots, count, wide, lifted, meta, sems
):
    step = pl.program_id(0)
    blocks, bins, _ = depth.shape
    owners = out.shape[0]

    @pl.when(step == 0)
    def _():
        clear_counts(count, owners)
        kind = lax.broadcasted_iota(jnp.int32, meta.shape, 1)
        meta[...] = jnp.where(kind == 0, EMPTY, ABSENT)
        numbers = pair_cells(cells[...]).astype(F32).reshape(wide.shape[0], bins)
        wide[...] = jnp.concatenate([numbers, numbers], axis=1)

    lane = lax.broadcasted_iota(jnp.int32, (1, 2 * bins), 1)

    def block(b, carry):
        at = step * blocks + b
        to = owner_of(owner, at)
        each = local.shape[1]
        tile = local[lax.div(at, each), lax.rem(at, each)].astype(F32)
        rank = take_slot(to, count)
        slots[at] = 2 * to + rank
        product = jnp.dot(depth[b], context[b], preferred_element_type=F32)
        lifted[lax.div(at, 2), pl.ds(pl.multiple_of(lax.rem(at, 2) * bins, bins), bins), :] = product.astype(BF)
        mine = (lane // bins) == rank
        row = wide[pl.ds(at, 1), :]
        meta[to, pl.ds(0, 1), :] = jnp.where(mine, row, meta[to, pl.ds(0, 1), :])
        meta[to, pl.ds(1, 1), :] = jnp.where(mine, tile, meta[to, pl.ds(1, 1), :])
        pltpu.make_async_copy(
            lifted.at[lax.div(at, 2), pl.ds(pl.multiple_of(lax.rem(at, 2) * bins, bins), bins), :],
            out.at[to, pl.ds(pl.multiple_of(rank * bins, bins), bins), :],
            sems.at[0],
        ).start()
        return carry

    lax.fori_loop(0, blocks, block, 0, unroll=4)

    @pl.when(step == pl.num_programs(0) - 1)
    def _():
        wide_meta = lifted.shape[0]

        def put_meta(small):
            small[...] = meta[...].astype(BF)
            copy = pltpu.make_async_copy(
                small, out.at[:, pl.ds(2 * bins, 8), :], sems.at[1]
            )
            copy.start()
            copy.wait()

        pl.run_scoped(put_meta, pltpu.VMEM(meta.shape, BF))
        pltpu.make_async_copy(
            lifted, out.at[pl.ds(0, wide_meta), pl.ds(0, 2 * bins), :], sems.at[0]
        ).wait()


def pack(owner, local, cells, depth, context, owners):
    blocks, bins, pixels = depth.shape
    channels = context.shape[2]
    chunk = blocks // 4
    return pl.pallas_call(
        pack_kernel,
        out_shape=(
            pltpu.HBM((owners, 2 * bins + 8, channels), BF),
            jax.ShapeDtypeStruct((blocks,), jnp.int32),
        ),
        grid=(blocks // chunk,),
        in_specs=[
            pl.BlockSpec(memory_space=pltpu.SMEM),
            pl.BlockSpec(memory_space=pltpu.SMEM),
            pl.BlockSpec(cells.shape, lambda i: (0, 0, 0)),
            pl.BlockSpec((chunk, bins, pixels), lambda i: (i, 0, 0)),
            pl.BlockSpec((chunk, pixels, channels), lambda i: (i, 0, 0)),
        ],
        out_specs=(
            pl.BlockSpec(memory_space=pltpu.HBM),
            pl.BlockSpec(memory_space=pltpu.SMEM),
        ),
        scratch_shapes=[
            pltpu.SMEM((owners,), jnp.int32),
            pltpu.VMEM((blocks, 2 * bins), F32),
            pltpu.VMEM((blocks // 2, 2 * bins, channels), BF),
            pltpu.VMEM((owners, 8, 2 * bins), F32),
            pltpu.SemaphoreType.DMA((2,)),
        ],
        compiler_params=pltpu.CompilerParams(vmem_limit_bytes=24 << 20),
        name="pack",
    )(owner, local, cells, depth, context)


def cell_onehot(cell_row, cells):
    number = lax.broadcasted_iota(jnp.int32, (cells, cell_row.shape[1]), 0)
    return jnp.where(number == cell_row, 1.0, 0.0).astype(BF)


def splat_kernel(meta_all, message, out, tiles_out, even, odd, turned, tiles, sem):
    step = pl.program_id(0)
    sources, rows, channels = message.shape
    bins = (rows - 8) // 2
    cells = TS * TS

    @pl.when(step == 0)
    def _():
        numbers = meta_all[:, 0:8, :].astype(F32)
        flat = numbers[:, 1, :].T
        turned[0:1, :] = flat[0:1].astype(jnp.int32)
        turned[1:2, :] = flat[bins : bins + 1].astype(jnp.int32)
        copy = pltpu.make_async_copy(turned, tiles, sem)
        copy.start()
        even[...] = jnp.zeros(even.shape, F32)
        odd[...] = jnp.zeros(odd.shape, F32)
        copy.wait()

    def source(s, carry):
        meta = message[s, pl.ds(2 * bins, 8), :].astype(jnp.int32)
        hot = cell_onehot(meta[0:1], cells)
        tile = [tiles[rank, step * sources + s] for rank in range(2)]
        nothing = jnp.zeros((bins, channels), BF)
        first = jnp.where(tile[0] < ABSENT, message[s, 0:bins, :], nothing)
        second = jnp.where(tile[1] < ABSENT, message[s, bins : 2 * bins, :], nothing)
        both = jnp.concatenate(
            [
                jnp.concatenate([first, nothing], axis=0),
                jnp.concatenate([nothing, second], axis=0),
            ],
            axis=1,
        )
        sums = jnp.dot(hot, both, preferred_element_type=F32)
        for rank, acc in enumerate((even, odd)):
            here = jnp.minimum(tile[rank], acc.shape[1] // 8 - 1)
            at = pl.ds(pl.multiple_of(here * 8, 8), 8)
            part = sums[:, rank * channels : (rank + 1) * channels].reshape(TS, 2, 8, channels)
            for side in range(2):
                lanes = slice(side * channels, (side + 1) * channels)
                acc[:, at, lanes] += part[:, side]
        return carry

    lax.fori_loop(0, sources, source, 0, unroll=8)

    @pl.when(step == pl.num_programs(0) - 1)
    def _():
        out[...] = (even[...] + odd[...]).astype(BF)
        tiles_out[...] = turned[...]


def splat(message, rows, cols):
    owners, height, channels = message.shape
    chunk = owners // 8
    shape = (rows, cols // 2, 2 * channels)
    return pl.pallas_call(
        splat_kernel,
        out_shape=(
            jax.ShapeDtypeStruct(shape, BF),
            jax.ShapeDtypeStruct((2, owners), jnp.int32),
        ),
        grid=(owners // chunk,),
        in_specs=[
            pl.BlockSpec((owners, 8, channels), lambda i: (0, height // 8 - 1, 0)),
            pl.BlockSpec((chunk, height, channels), lambda i: (i, 0, 0)),
        ],
        out_specs=(
            pl.BlockSpec(shape, lambda i: (0, 0, 0)),
            pl.BlockSpec((2, owners), lambda i: (0, 0)),
        ),
        scratch_shapes=[
            pltpu.VMEM(shape, F32),
            pltpu.VMEM(shape, F32),
            pltpu.VMEM((2, owners), jnp.int32),
            pltpu.SMEM((2, owners), jnp.int32),
            pltpu.SemaphoreType.DMA,
        ],
        compiler_params=pltpu.CompilerParams(vmem_limit_bytes=40 << 20),
        name="splat",
    )(message, message)


def chunks_of(count):
    parts = -(-count // 7)
    size = -(-count // parts)
    return size, [min(i * size, count - size) for i in range(parts)]


def conv_kernel(
    edges, middle, above, below, left, right, corner_above, corner_below,
    cot_above, cot_below, cot_far, weights_far,
    bev, grad, ping, pong, slopes, mask, sums, weights, cot, sems,
):
    rows, mid, double = middle.shape
    channels = double // 2
    wide = mid + 2 * PAIRS
    tall = rows + 2 * EXT
    arrivals = [
        pltpu.make_async_copy(weights_far.at[i], weights.at[i], sems.at[i])
        for i in range(2 * LAYERS)
    ]
    cot_arrival = pltpu.make_async_copy(
        cot_far, cot.at[pl.ds(LAYERS, rows)], sems.at[2 * LAYERS]
    )
    for copy in arrivals[:LAYERS]:
        copy.start()
    cot_arrival.start()
    for copy in arrivals[: LAYERS - 1 : -1]:
        copy.start()
    column = lax.broadcasted_iota(jnp.int32, (wide, double), 0)
    gone = ((column < PAIRS) & (edges[2] == 1)) | ((column >= wide - PAIRS) & (edges[3] == 1))
    mask[0] = jnp.zeros((wide, double), F32)
    mask[1] = jnp.where(gone, 0.0, 1.0)

    def put(ref, row, value):
        first = value[:, :channels]
        second = value[:, channels:]
        ref[row, :, 0:channels] = pltpu.roll(second, 1, 0).astype(BF)
        ref[row, :, channels : 3 * channels] = value.astype(BF)
        ref[row, :, 3 * channels :] = pltpu.roll(first, wide - 1, 0).astype(BF)

    def joined(west, center, east):
        return jnp.concatenate([west.astype(F32), center.astype(F32), east.astype(F32)], axis=0)

    def load(row, west, center, east):
        put(ping, row, joined(west, center, east))

    def load_outer(k, carry):
        load(k, corner_above[k, 0:PAIRS], above[k], corner_above[k, PAIRS:])
        load(EXT + rows + k, corner_below[k, 0:PAIRS], below[k], corner_below[k, PAIRS:])
        return carry

    def load_inner(k, carry):
        load(EXT + k, left[k], middle[k], right[k])
        return carry

    lax.fori_loop(0, EXT, load_outer, 0)
    lax.fori_loop(0, rows, load_inner, 0)
    for k in range(LAYERS):
        for corner, field, base in (
            (corner_above, cot_above, 0), (corner_below, cot_below, LAYERS + rows)
        ):
            west, east = corner[EXT + k, 0:PAIRS], corner[EXT + k, PAIRS:]
            cot[base + k] = joined(west, field[k], east).astype(BF)

    def matmul(ref, index, start, size):
        taps = [ref[pl.ds(start + tap, size)].reshape(size * wide, 2 * double) for tap in range(3)]
        total = jnp.dot(
            jnp.concatenate(taps, axis=1), weights[index], preferred_element_type=F32
        )
        sums[0:size] = total.reshape(size, wide, double)

    kept = [tall - 2 - 2 * layer for layer in range(LAYERS)]
    offsets = [sum(kept[:layer]) for layer in range(LAYERS)]

    def forward(layer, target, start, size):
        for side in range(size):
            here = start + side
            row = layer + 1 + here
            inside = jnp.where(
                ((row < EXT) & (edges[0] == 1)) | ((row >= EXT + rows) & (edges[1] == 1)), 0, 1
            )
            part = sums[side]
            flag = mask[inside]
            twice = flag + flag * jnp.tanh(part)
            active = part * twice
            slope = twice + active * (2.0 - twice)
            if layer < LAYERS - 1:
                put(target, here, active)
                slopes[offsets[layer] + here] = slope.astype(slopes.dtype)
            else:
                bev[here] = active[PAIRS : PAIRS + mid].astype(BF)
                put(target, here, cot[here].astype(F32) * slope)

    def backward(step, target, start, size):
        layer = LAYERS - 1 - step
        for side in range(size):
            here = start + side
            if layer > 0:
                slope = slopes[offsets[layer - 1] + here + 2 * (step + 1)].astype(F32)
                put(target, here, sums[side] * slope)
            else:
                value = sums[side, PAIRS : PAIRS + mid]
                for tile in range(mid // 8):
                    piece = value[tile * 8 : (tile + 1) * 8]
                    piece = jnp.concatenate([piece[:, :channels], piece[:, channels:]], axis=0)
                    at = pl.ds(pl.multiple_of(here * TS, TS), TS)
                    grad[tile, at, :] = piece.astype(BF)

    stages = []
    for layer in range(LAYERS):
        stages.append((layer, kept[layer], functools.partial(forward, layer)))
    for step in range(LAYERS):
        layer = LAYERS - 1 - step
        stages.append((LAYERS + layer, rows + 2 * layer, functools.partial(backward, step)))

    source, target = ping, pong
    finish = None
    for index, count, epilogue in stages:
        size, starts = chunks_of(count)
        arrivals[index].wait()
        if index == LAYERS - 1:
            cot_arrival.wait()
        if finish is not None:
            finish()
        matmul(source, index, 0, size)

        def steady(k, carry, index=index, count=count, size=size, source=source, target=target, epilogue=epilogue):
            epilogue(target, (k - 1) * size, size)
            matmul(source, index, jnp.minimum(k * size, count - size), size)
            return carry

        lax.fori_loop(1, len(starts), steady, 0)
        finish = functools.partial(epilogue, target, starts[-1], size)
        source, target = target, source
    finish()


def convs(edges, weights, cot, *fields):
    middle = fields[0]
    rows, mid, double = middle.shape
    wide = mid + 2 * PAIRS
    tall = rows + 2 * EXT
    kept = sum(tall - 2 - 2 * layer for layer in range(LAYERS - 1))
    vmem = pl.BlockSpec(memory_space=pltpu.VMEM)
    hbm = pl.BlockSpec(memory_space=pltpu.HBM)
    buffer = pltpu.VMEM((tall, wide, 2 * double), BF)
    return pl.pallas_call(
        conv_kernel,
        out_shape=(
            jax.ShapeDtypeStruct((rows + 2 * LAYERS, mid, double), BF),
            jax.ShapeDtypeStruct((mid // 8, rows * TS, double // 2), BF),
        ),
        in_specs=[pl.BlockSpec(memory_space=pltpu.SMEM)] + [vmem] * len(fields) + [hbm] * 2,
        out_specs=(vmem, vmem),
        scratch_shapes=[
            buffer,
            buffer,
            pltpu.VMEM((kept, wide, double), F32),
            pltpu.VMEM((2, wide, double), F32),
            pltpu.VMEM((7, wide, double), F32),
            pltpu.VMEM(weights.shape, BF),
            pltpu.VMEM((rows + 2 * LAYERS, wide, double), BF),
            pltpu.SemaphoreType.DMA((2 * LAYERS + 1,)),
        ],
        compiler_params=pltpu.CompilerParams(vmem_limit_bytes=48 << 20),
        name="convs",
    )(edges, *fields, in_hbm(cot), in_hbm(weights))


def gather_kernel(tiles, meta_all, grad, out, columns):
    step = pl.program_id(0)
    owners = meta_all.shape[0]
    sources, slots, channels = out.shape
    bins = slots // 2
    count, cells, _ = grad.shape

    @pl.when(step == 0)
    def _():
        columns[...] = meta_all[...].astype(F32)[:, 0, :].T.astype(jnp.int32)

    mine = pltpu.roll(columns[...], lax.rem(owners - step * sources, owners), 1)
    number = lax.broadcasted_iota(jnp.int32, (slots, cells), 1)
    for s in range(sources):
        hot = jnp.where(mine[:, s : s + 1] == number, 1.0, 0.0).astype(BF)
        here = [jnp.minimum(tiles[rank, step * sources + s], count - 1) for rank in range(2)]
        both = jnp.concatenate([grad[here[0]], grad[here[1]]], axis=1)
        picked = jnp.dot(hot, both, preferred_element_type=F32)
        out[s, 0:bins, :] = picked[:bins, :channels].astype(BF)
        out[s, bins:, :] = picked[bins:, channels:].astype(BF)


def gather(tiles, message, grad):
    owners, height, channels = message.shape
    chunk = owners // 8
    return pl.pallas_call(
        gather_kernel,
        out_shape=pltpu.HBM((owners, height - 8, channels), BF),
        grid=(owners // chunk,),
        in_specs=[
            pl.BlockSpec(memory_space=pltpu.SMEM),
            pl.BlockSpec((owners, 8, channels), lambda i: (0, height // 8 - 1, 0)),
            pl.BlockSpec(grad.shape, lambda i: (0, 0, 0)),
        ],
        out_specs=pl.BlockSpec((chunk, height - 8, channels), lambda i: (i, 0, 0)),
        scratch_shapes=[pltpu.VMEM((height - 8, owners), jnp.int32)],
        compiler_params=pltpu.CompilerParams(vmem_limit_bytes=24 << 20),
        name="gather",
    )(tiles, message, grad)


def final_kernel(slots, returned, depth, context, grad_depth, grad_context, fetched, sems):
    step = pl.program_id(0)
    blocks, bins, _ = depth.shape
    halves = blocks // 2

    @pl.when(step == 0)
    def _():
        for b in range(2 * fetched.shape[0]):
            slot = slots[b]
            start = pl.multiple_of(lax.rem(slot, 2) * bins, bins)
            pltpu.make_async_copy(
                returned.at[lax.div(slot, 2), pl.ds(start, bins), :],
                fetched.at[b // 2, pl.ds((b % 2) * bins, bins), :],
                sems.at[b // blocks],
            ).start()

    pltpu.make_async_copy(
        returned.at[pl.ds(0, halves)],
        fetched.at[pl.ds(pl.multiple_of(step * halves, halves), halves)],
        sems.at[step],
    ).wait()

    for b in range(blocks):
        rows = fetched[step * halves + b // 2, (b % 2) * bins : (b % 2 + 1) * bins, :]
        grad_depth[b] = lax.dot_general(
            rows, context[b], (((1,), (1,)), ((), ())), preferred_element_type=F32
        ).astype(BF)
        grad_context[b] = lax.dot_general(
            depth[b], rows, (((0,), (0,)), ((), ())), preferred_element_type=F32
        ).astype(BF)


def final(slots, returned, depth, context):
    blocks, bins, pixels = depth.shape
    channels = context.shape[2]
    steps = 4
    chunk = blocks // steps
    depth_block = pl.BlockSpec((chunk, bins, pixels), lambda i: (i, 0, 0))
    context_block = pl.BlockSpec((chunk, pixels, channels), lambda i: (i, 0, 0))
    return pl.pallas_call(
        final_kernel,
        out_shape=(
            jax.ShapeDtypeStruct(depth.shape, BF),
            jax.ShapeDtypeStruct(context.shape, BF),
        ),
        grid=(steps,),
        in_specs=[
            pl.BlockSpec(memory_space=pltpu.SMEM),
            pl.BlockSpec(memory_space=pltpu.HBM),
            depth_block,
            context_block,
        ],
        out_specs=(depth_block, context_block),
        scratch_shapes=[
            pltpu.VMEM((blocks // 2,) + returned.shape[1:], BF),
            pltpu.SemaphoreType.DMA((steps,)),
        ],
        compiler_params=pltpu.CompilerParams(vmem_limit_bytes=24 << 20),
        name="final",
    )(slots, in_hbm(returned), depth, context)


def paired_weights(kernel):
    layers, taps, _, inner, outer = kernel.shape
    first = jnp.pad(kernel, ((0, 0), (0, 0), (0, 1), (0, 0), (0, 0)))
    second = jnp.pad(kernel, ((0, 0), (0, 0), (1, 0), (0, 0), (0, 0)))
    return jnp.concatenate([first, second], axis=4).reshape(layers, 4 * taps * inner, 2 * outer)


def per_device(
    depth_weights, context, block_owner, block_local, block_cell, conv_weight, cotangent
):
    cams_here, blocks_cam, bins, pixels = depth_weights.shape
    channels = context.shape[3]
    rows, cols, _ = cotangent.shape
    mid = cols // 2
    axes = ("cam", "tile")
    owners = lax.axis_size(axes)
    blocks = cams_here * blocks_cam
    depth = depth_weights.reshape(blocks, bins, pixels)
    flat_context = context.reshape(blocks, pixels, channels)
    owner = block_owner.transpose(0, 2, 1)

    sent, slots = pack(
        in_hbm(owner), in_hbm(block_local), in_hbm(block_cell), in_hbm(depth),
        in_hbm(flat_context), owners,
    )
    message = lax.all_to_all(sent, axes, split_axis=0, concat_axis=0, tiled=True)

    cot = cotangent.reshape(rows, mid, 2 * channels)
    down, up = ring("cam")
    east, west = ring("tile")
    cot_above = lax.ppermute(cot[rows - LAYERS :], "cam", down)
    cot_below = lax.ppermute(cot[:LAYERS], "cam", up)
    cot_left = lax.ppermute(cot[:, mid - PAIRS :], "tile", east)
    cot_right = lax.ppermute(cot[:, :PAIRS], "tile", west)
    cot_middle = jnp.concatenate([cot_left, cot, cot_right], axis=1)
    turned_weight = conv_weight[:, ::-1, ::-1].swapaxes(3, 4)
    weights = jnp.concatenate([paired_weights(conv_weight), paired_weights(turned_weight)], axis=0)
    weights = weights * jnp.asarray(0.5, BF)
    cam = lax.axis_index("cam")
    tile = lax.axis_index("tile")
    edges = jnp.stack(
        [cam == 0, cam == lax.axis_size("cam") - 1, tile == 0, tile == lax.axis_size("tile") - 1]
    ).astype(jnp.int32)

    middle, tiles = splat(message, rows, cols)

    above = lax.ppermute(middle[rows - EXT :], "cam", down)
    below = lax.ppermute(middle[:EXT], "cam", up)
    left = lax.ppermute(middle[:, mid - PAIRS :], "tile", east)
    right = lax.ppermute(middle[:, :PAIRS], "tile", west)
    sides = jnp.concatenate([left, right], axis=1)
    cot_sides = jnp.concatenate([cot_middle[:, :PAIRS], cot_middle[:, PAIRS + mid :]], axis=1)
    lower = jnp.concatenate([sides[rows - EXT :], cot_sides[rows - LAYERS :]], axis=0)
    upper = jnp.concatenate([sides[:EXT], cot_sides[:LAYERS]], axis=0)
    corner_above = lax.ppermute(lower, "cam", down)
    corner_below = lax.ppermute(upper, "cam", up)

    bev, grad = convs(
        edges, weights, cot_middle, middle, above, below, left, right, corner_above,
        corner_below, cot_above, cot_below,
    )
    rows_back = gather(tiles, message, grad)
    returned = lax.all_to_all(rows_back, axes, split_axis=0, concat_axis=0, tiled=True)
    grad_depth, grad_context = final(slots, returned, in_hbm(depth), in_hbm(flat_context))
    return (
        bev[LAYERS : LAYERS + rows].reshape(cotangent.shape),
        grad_depth.reshape(depth_weights.shape),
        grad_context.reshape(context.shape),
    )


def solution(mesh):
    placed = (
        P(("cam", "tile"), None, None, None),
        P(("cam", "tile"), None, None, None),
        P(("cam", "tile"), None, None),
        P(("cam", "tile"), None),
        P(("cam", "tile"), None, None),
        P(),
        P("cam", "tile", None),
    )
    return jax.shard_map(
        per_device,
        mesh=mesh,
        in_specs=placed,
        out_specs=(
            P("cam", "tile", None),
            P(("cam", "tile"), None, None, None),
            P(("cam", "tile"), None, None, None),
        ),
        check_vma=False,
    )
```

```python
import functools

import jax
import jax.numpy as jnp
from jax import lax
from jax.experimental import pallas as pl
from jax.experimental.pallas import tpu as pltpu
from jax.sharding import PartitionSpec as P

TS = 16
LAYERS = 4
EXT = 2 * LAYERS
PAIRS = 8
EMPTY = 256.0
ABSENT = 255
BF = jnp.bfloat16
F32 = jnp.float32


def ring(axis):
    count = lax.axis_size(axis)
    ends = count - 1
    down = [(i, i + 1) for i in range(ends)]
    up = [(i + 1, i) for i in range(ends)]
    return down, up


def take_slot(owner, count):
    rank = count[owner]
    count[owner] = rank + 1
    return rank


def clear_counts(count, size):
    for i in range(size):
        count[i] = 0


def in_hbm(x):
    return pltpu.with_memory_space_constraint(x, pltpu.HBM)


def owner_of(owner, at):
    each = owner.shape[2]
    return owner[lax.div(at, each), 0, lax.rem(at, each)]


def pair_cells(cells):
    return (cells // TS) * TS + (cells % 2) * (TS // 2) + (cells % TS) // 2


def pack_kernel(
    owner, local, cells, depth, context, out, slots, count, wide, lifted, meta, sems
):
    step = pl.program_id(0)
    blocks, bins, _ = depth.shape
    owners = out.shape[0]

    @pl.when(step == 0)
    def _():
        clear_counts(count, owners)
        kind = lax.broadcasted_iota(jnp.int32, meta.shape, 1)
        meta[...] = jnp.where(kind == 0, EMPTY, ABSENT)
        numbers = pair_cells(cells[...]).astype(F32).reshape(wide.shape[0], bins)
        wide[...] = jnp.concatenate([numbers, numbers], axis=1)

    lane = lax.broadcasted_iota(jnp.int32, (1, 2 * bins), 1)

    def block(b, carry):
        at = step * blocks + b
        to = owner_of(owner, at)
        each = local.shape[1]
        tile = local[lax.div(at, each), lax.rem(at, each)].astype(F32)
        rank = take_slot(to, count)
        slots[at] = 2 * to + rank
        product = jnp.dot(depth[b], context[b], preferred_element_type=F32)
        lifted[lax.div(at, 2), pl.ds(pl.multiple_of(lax.rem(at, 2) * bins, bins), bins), :] = product.astype(BF)
        mine = (lane // bins) == rank
        row = wide[pl.ds(at, 1), :]
        meta[to, pl.ds(0, 1), :] = jnp.where(mine, row, meta[to, pl.ds(0, 1), :])
        meta[to, pl.ds(1, 1), :] = jnp.where(mine, tile, meta[to, pl.ds(1, 1), :])
        pltpu.make_async_copy(
            lifted.at[lax.div(at, 2), pl.ds(pl.multiple_of(lax.rem(at, 2) * bins, bins), bins), :],
            out.at[to, pl.ds(pl.multiple_of(rank * bins, bins), bins), :],
            sems.at[0],
        ).start()
        return carry

    lax.fori_loop(0, blocks, block, 0, unroll=4)

    @pl.when(step == pl.num_programs(0) - 1)
    def _():
        wide_meta = lifted.shape[0]

        def put_meta(small):
            small[...] = meta[...].astype(BF)
            copy = pltpu.make_async_copy(
                small, out.at[:, pl.ds(2 * bins, 8), :], sems.at[1]
            )
            copy.start()
            copy.wait()

        pl.run_scoped(put_meta, pltpu.VMEM(meta.shape, BF))
        pltpu.make_async_copy(
            lifted, out.at[pl.ds(0, wide_meta), pl.ds(0, 2 * bins), :], sems.at[0]
        ).wait()


def pack(owner, local, cells, depth, context, owners):
    blocks, bins, pixels = depth.shape
    channels = context.shape[2]
    chunk = blocks // 4
    return pl.pallas_call(
        pack_kernel,
        out_shape=(
            pltpu.HBM((owners, 2 * bins + 8, channels), BF),
            jax.ShapeDtypeStruct((blocks,), jnp.int32),
        ),
        grid=(blocks // chunk,),
        in_specs=[
            pl.BlockSpec(memory_space=pltpu.SMEM),
            pl.BlockSpec(memory_space=pltpu.SMEM),
            pl.BlockSpec(cells.shape, lambda i: (0, 0, 0)),
            pl.BlockSpec((chunk, bins, pixels), lambda i: (i, 0, 0)),
            pl.BlockSpec((chunk, pixels, channels), lambda i: (i, 0, 0)),
        ],
        out_specs=(
            pl.BlockSpec(memory_space=pltpu.HBM),
            pl.BlockSpec(memory_space=pltpu.SMEM),
        ),
        scratch_shapes=[
            pltpu.SMEM((owners,), jnp.int32),
            pltpu.VMEM((blocks, 2 * bins), F32),
            pltpu.VMEM((blocks // 2, 2 * bins, channels), BF),
            pltpu.VMEM((owners, 8, 2 * bins), F32),
            pltpu.SemaphoreType.DMA((2,)),
        ],
        compiler_params=pltpu.CompilerParams(vmem_limit_bytes=24 << 20),
        name="pack",
    )(owner, local, cells, depth, context)


def cell_onehot(cell_row, cells):
    number = lax.broadcasted_iota(jnp.int32, (cells, cell_row.shape[1]), 0)
    return jnp.where(number == cell_row, 1.0, 0.0).astype(BF)


def splat_kernel(
    meta_all, message, out, tiles_out, acc, rows, cells, codes, numbers, group, group_tile, sems
):
    owners, _, channels = meta_all.shape
    bins = channels // 2
    tile_count = acc.shape[1] // 8
    groups = group_tile.shape[0] - owners // 2
    arrival = pltpu.make_async_copy(
        message.at[:, pl.ds(0, 2 * bins), :], rows.at[pl.ds(0, owners)], sems.at[0]
    )
    arrival.start()
    meta = meta_all[...].astype(F32)
    cells[0:owners, :] = meta[:, 0, :].astype(jnp.int32)
    cells[owners:, :] = jnp.full((8, channels), TS * TS, jnp.int32)
    rows[owners] = jnp.zeros((2 * bins, channels), BF)
    lane = lax.broadcasted_iota(jnp.int32, (owners, channels), 1)
    line = lax.broadcasted_iota(jnp.int32, (owners, channels), 0)
    named = meta[:, 1, :]
    swapped = pltpu.roll(named, bins, 1)
    across, place, amount = [], [], []
    for rank in range(2):
        down = jnp.where((lane < bins) == (rank == 0), named, swapped).astype(jnp.int32)
        tile = down.T
        earlier = (down == tile) & (line < lane)
        across.append(tile)
        place.append(jnp.sum(earlier.astype(jnp.int32), axis=0, keepdims=True))
        amount.append(jnp.sum((line == tile).astype(jnp.int32), axis=1, keepdims=True))
    needed = lax.shift_right_logical(jnp.maximum(amount[0], amount[1]) + 1, 1)
    needed = jnp.where(line < tile_count, needed, 0)
    for rank in range(2):
        tile = across[rank][0:1]
        base = jnp.sum(jnp.where(line < across[rank], needed, 0), axis=0, keepdims=True)
        at = jnp.where(tile < tile_count, base, groups) + lax.shift_right_logical(place[rank], 1)
        codes[rank : rank + 1, :] = 4 * at + 2 * rank + (place[rank] & 1)
        codes[2 + rank : 3 + rank, :] = tile
        tiles_out[rank : rank + 1, :] = jnp.minimum(tile, tile_count - 1)
    codes[4:5, :] = jnp.sum(needed, axis=0, keepdims=True)
    copy = pltpu.make_async_copy(codes, numbers, sems.at[1])
    copy.start()
    acc[...] = jnp.zeros(acc.shape, F32)
    for i in range(4 * groups):
        group[i] = owners
    for i in range(groups):
        group_tile[i] = 0
    copy.wait()
    total = numbers[4, 0]

    def place_source(s, carry):
        for rank in range(2):
            at = numbers[rank, s]
            group[at] = s
            group_tile[lax.shift_right_logical(at, 2)] = numbers[2 + rank, s]
        return carry

    lax.fori_loop(0, owners, place_source, 0, unroll=16)
    arrival.wait()
    low = lax.broadcasted_iota(jnp.int32, (1, channels), 1) < bins

    def batch(b, carry):
        for q in range(8):
            at = 8 * b + q
            ids = [group[4 * at + slot] for slot in range(4)]
            hot = [
                cell_onehot(
                    jnp.where(low, cells[pl.ds(ids[k], 1), :], cells[pl.ds(ids[2 + k], 1), :]),
                    TS * TS,
                )
                for k in range(2)
            ]
            parts = []
            for k in range(2):
                parts += [rows[ids[k], 0:bins, :], rows[ids[2 + k], bins : 2 * bins, :]]
            sums = jnp.dot(
                jnp.concatenate(hot, axis=1),
                jnp.concatenate(parts, axis=0),
                preferred_element_type=F32,
            ).reshape(TS, 2, 8, channels)
            here = pl.ds(pl.multiple_of(group_tile[at] * 8, 8), 8)
            for side in range(2):
                acc[:, here, side * channels : (side + 1) * channels] += sums[:, side]
        return carry

    lax.fori_loop(0, lax.div(total + 7, 8), batch, 0)
    out[...] = acc[...].astype(BF)


def splat(message, rows, cols):
    owners, height, channels = message.shape
    shape = (rows, cols // 2, 2 * channels)
    groups = owners + cols // TS
    spare = groups + owners // 2
    return pl.pallas_call(
        splat_kernel,
        out_shape=(
            jax.ShapeDtypeStruct(shape, BF),
            jax.ShapeDtypeStruct((2, owners), jnp.int32),
        ),
        grid=(1,),
        in_specs=[
            pl.BlockSpec((owners, 8, channels), lambda i: (0, height // 8 - 1, 0)),
            pl.BlockSpec(memory_space=pltpu.HBM),
        ],
        out_specs=(
            pl.BlockSpec(shape, lambda i: (0, 0, 0)),
            pl.BlockSpec((2, owners), lambda i: (0, 0)),
        ),
        scratch_shapes=[
            pltpu.VMEM(shape, F32),
            pltpu.VMEM((owners + 1, height - 8, channels), BF),
            pltpu.VMEM((owners + 8, channels), jnp.int32),
            pltpu.VMEM((8, owners), jnp.int32),
            pltpu.SMEM((8, owners), jnp.int32),
            pltpu.SMEM((4 * spare,), jnp.int32),
            pltpu.SMEM((spare,), jnp.int32),
            pltpu.SemaphoreType.DMA((2,)),
        ],
        compiler_params=pltpu.CompilerParams(vmem_limit_bytes=24 << 20),
        name="splat",
    )(in_hbm(message), in_hbm(message))


def chunks_of(count):
    parts = -(-count // 7)
    size = -(-count // parts)
    return size, [min(i * size, count - size) for i in range(parts)]


def conv_kernel(
    edges, middle, above, below, left, right, corner_above, corner_below,
    cot_above, cot_below, cot_far, weights_far,
    bev, grad, ping, pong, slopes, sums, weights, cot, sems,
):
    rows, mid, double = middle.shape
    channels = double // 2
    wide = mid + 2 * PAIRS
    tall = rows + 2 * EXT
    arrivals = [
        pltpu.make_async_copy(weights_far.at[i], weights.at[i], sems.at[i])
        for i in range(2 * LAYERS)
    ]
    cot_arrival = pltpu.make_async_copy(
        cot_far, cot.at[pl.ds(LAYERS, rows)], sems.at[2 * LAYERS]
    )
    for copy in arrivals[:LAYERS]:
        copy.start()
    cot_arrival.start()
    for copy in arrivals[: LAYERS - 1 : -1]:
        copy.start()

    def put(ref, row, value):
        first = value[:, :channels]
        second = value[:, channels:]
        ref[row, :, 0:channels] = pltpu.roll(second, 1, 0).astype(BF)
        ref[row, :, channels : 3 * channels] = value.astype(BF)
        ref[row, :, 3 * channels :] = pltpu.roll(first, wide - 1, 0).astype(BF)

    def joined(west, center, east):
        return jnp.concatenate([west.astype(F32), center.astype(F32), east.astype(F32)], axis=0)

    def load(row, west, center, east):
        put(ping, row, joined(west, center, east))

    def load_outer(k, carry):
        load(k, corner_above[k, 0:PAIRS], above[k], corner_above[k, PAIRS:])
        load(EXT + rows + k, corner_below[k, 0:PAIRS], below[k], corner_below[k, PAIRS:])
        return carry

    def load_inner(k, carry):
        load(EXT + k, left[k], middle[k], right[k])
        return carry

    lax.fori_loop(0, EXT, load_outer, 0)
    lax.fori_loop(0, rows, load_inner, 0)
    for k in range(LAYERS):
        for corner, field, base in (
            (corner_above, cot_above, 0), (corner_below, cot_below, LAYERS + rows)
        ):
            west, east = corner[EXT + k, 0:PAIRS], corner[EXT + k, PAIRS:]
            cot[base + k] = joined(west, field[k], east).astype(BF)

    def matmul(ref, index, start, size):
        taps = [ref[pl.ds(start + tap, size)].reshape(size * wide, 2 * double) for tap in range(3)]
        total = jnp.dot(
            jnp.concatenate(taps, axis=1), weights[index], preferred_element_type=F32
        )
        sums[0:size] = total.reshape(size, wide, double)

    kept = [tall - 2 - 2 * layer for layer in range(LAYERS)]
    offsets = [sum(kept[:layer]) for layer in range(LAYERS)]

    def forward(layer, target, start, size):
        for side in range(size):
            here = start + side
            row = layer + 1 + here
            inside = jnp.where(
                ((row < EXT) & (edges[0] == 1)) | ((row >= EXT + rows) & (edges[1] == 1)), 0.0, 1.0
            )
            part = sums[side]
            twice = 1.0 + jnp.tanh(part)
            twice = jnp.concatenate(
                [
                    twice[:PAIRS] * jnp.where(edges[2] == 1, 0.0, inside),
                    twice[PAIRS : PAIRS + mid] * inside,
                    twice[PAIRS + mid :] * jnp.where(edges[3] == 1, 0.0, inside),
                ],
                axis=0,
            )
            active = part * twice
            slope = twice + active * (2.0 - twice)
            if layer < LAYERS - 1:
                put(target, here, active)
                slopes[offsets[layer] + here] = slope.astype(slopes.dtype)
            else:
                bev[here] = active[PAIRS : PAIRS + mid].astype(BF)
                put(target, here, cot[here].astype(F32) * slope)

    def backward(step, target, start, size):
        layer = LAYERS - 1 - step
        for side in range(size):
            here = start + side
            if layer > 0:
                slope = slopes[offsets[layer - 1] + here + 2 * (step + 1)].astype(F32)
                put(target, here, sums[side] * slope)
            else:
                value = sums[side, PAIRS : PAIRS + mid]
                for tile in range(mid // 8):
                    piece = value[tile * 8 : (tile + 1) * 8]
                    piece = jnp.concatenate([piece[:, :channels], piece[:, channels:]], axis=0)
                    at = pl.ds(pl.multiple_of(here * TS, TS), TS)
                    grad[tile, at, :] = piece.astype(BF)

    stages = []
    for layer in range(LAYERS):
        stages.append((layer, kept[layer], functools.partial(forward, layer)))
    for step in range(LAYERS):
        layer = LAYERS - 1 - step
        stages.append((LAYERS + layer, rows + 2 * layer, functools.partial(backward, step)))

    source, target = ping, pong
    finish = None
    for index, count, epilogue in stages:
        size, starts = chunks_of(count)
        arrivals[index].wait()
        if index == LAYERS - 1:
            cot_arrival.wait()
        if finish is not None:
            finish()
        matmul(source, index, 0, size)

        def steady(k, carry, index=index, count=count, size=size, source=source, target=target, epilogue=epilogue):
            epilogue(target, (k - 1) * size, size)
            matmul(source, index, jnp.minimum(k * size, count - size), size)
            return carry

        lax.fori_loop(1, len(starts), steady, 0)
        finish = functools.partial(epilogue, target, starts[-1], size)
        source, target = target, source
    finish()


def convs(edges, weights, cot, *fields):
    middle = fields[0]
    rows, mid, double = middle.shape
    wide = mid + 2 * PAIRS
    tall = rows + 2 * EXT
    kept = sum(tall - 2 - 2 * layer for layer in range(LAYERS - 1))
    vmem = pl.BlockSpec(memory_space=pltpu.VMEM)
    hbm = pl.BlockSpec(memory_space=pltpu.HBM)
    buffer = pltpu.VMEM((tall, wide, 2 * double), BF)
    return pl.pallas_call(
        conv_kernel,
        out_shape=(
            jax.ShapeDtypeStruct((rows + 2 * LAYERS, mid, double), BF),
            jax.ShapeDtypeStruct((mid // 8, rows * TS, double // 2), BF),
        ),
        in_specs=[pl.BlockSpec(memory_space=pltpu.SMEM)] + [vmem] * len(fields) + [hbm] * 2,
        out_specs=(vmem, vmem),
        scratch_shapes=[
            buffer,
            buffer,
            pltpu.VMEM((kept, wide, double), F32),
            pltpu.VMEM((7, wide, double), F32),
            pltpu.VMEM(weights.shape, BF),
            pltpu.VMEM((rows + 2 * LAYERS, wide, double), BF),
            pltpu.SemaphoreType.DMA((2 * LAYERS + 1,)),
        ],
        compiler_params=pltpu.CompilerParams(vmem_limit_bytes=48 << 20),
        name="convs",
    )(edges, *fields, in_hbm(cot), in_hbm(weights))


def gather_kernel(tiles, meta_all, grad, out, columns):
    step = pl.program_id(0)
    owners = meta_all.shape[0]
    sources, slots, channels = out.shape
    bins = slots // 2
    count, cells, _ = grad.shape

    @pl.when(step == 0)
    def _():
        columns[...] = meta_all[...].astype(F32)[:, 0, :].T.astype(jnp.int32)

    mine = pltpu.roll(columns[...], lax.rem(owners - step * sources, owners), 1)
    number = lax.broadcasted_iota(jnp.int32, (slots, cells), 1)
    for s in range(sources):
        hot = jnp.where(mine[:, s : s + 1] == number, 1.0, 0.0).astype(BF)
        here = [jnp.minimum(tiles[rank, step * sources + s], count - 1) for rank in range(2)]
        both = jnp.concatenate([grad[here[0]], grad[here[1]]], axis=1)
        picked = jnp.dot(hot, both, preferred_element_type=F32)
        out[s, 0:bins, :] = picked[:bins, :channels].astype(BF)
        out[s, bins:, :] = picked[bins:, channels:].astype(BF)


def gather(tiles, message, grad):
    owners, height, channels = message.shape
    chunk = owners // 8
    return pl.pallas_call(
        gather_kernel,
        out_shape=pltpu.HBM((owners, height - 8, channels), BF),
        grid=(owners // chunk,),
        in_specs=[
            pl.BlockSpec(memory_space=pltpu.SMEM),
            pl.BlockSpec((owners, 8, channels), lambda i: (0, height // 8 - 1, 0)),
            pl.BlockSpec(grad.shape, lambda i: (0, 0, 0)),
        ],
        out_specs=pl.BlockSpec((chunk, height - 8, channels), lambda i: (i, 0, 0)),
        scratch_shapes=[pltpu.VMEM((height - 8, owners), jnp.int32)],
        compiler_params=pltpu.CompilerParams(vmem_limit_bytes=24 << 20),
        name="gather",
    )(tiles, message, grad)


def final_kernel(slots, returned, depth, context, grad_depth, grad_context, fetched, sems):
    step = pl.program_id(0)
    blocks, bins, _ = depth.shape
    halves = blocks // 2

    def fetch(first, group):
        for b in range(blocks):
            slot = slots[first + b]
            pltpu.make_async_copy(
                returned.at[
                    lax.shift_right_logical(slot, 1),
                    pl.ds(pl.multiple_of((slot & 1) * bins, bins), bins),
                    :,
                ],
                fetched.at[group * halves + b // 2, pl.ds((b % 2) * bins, bins), :],
                sems.at[group],
            ).start()

    @pl.when(step == 0)
    def _():
        fetch(0, 0)

    @pl.when(step + 1 < pl.num_programs(0))
    def _():
        fetch((step + 1) * blocks, step + 1)

    pltpu.make_async_copy(
        returned.at[pl.ds(0, halves)],
        fetched.at[pl.ds(pl.multiple_of(step * halves, halves), halves)],
        sems.at[step],
    ).wait()

    for b in range(blocks):
        rows = fetched[step * halves + b // 2, (b % 2) * bins : (b % 2 + 1) * bins, :]
        grad_depth[b] = lax.dot_general(
            rows, context[b], (((1,), (1,)), ((), ())), preferred_element_type=F32
        ).astype(BF)
        grad_context[b] = lax.dot_general(
            depth[b], rows, (((0,), (0,)), ((), ())), preferred_element_type=F32
        ).astype(BF)


def final(slots, returned, depth, context):
    blocks, bins, pixels = depth.shape
    channels = context.shape[2]
    steps = 4
    chunk = blocks // steps
    depth_block = pl.BlockSpec((chunk, bins, pixels), lambda i: (i, 0, 0))
    context_block = pl.BlockSpec((chunk, pixels, channels), lambda i: (i, 0, 0))
    return pl.pallas_call(
        final_kernel,
        out_shape=(
            jax.ShapeDtypeStruct(depth.shape, BF),
            jax.ShapeDtypeStruct(context.shape, BF),
        ),
        grid=(steps,),
        in_specs=[
            pl.BlockSpec(memory_space=pltpu.SMEM),
            pl.BlockSpec(memory_space=pltpu.HBM),
            depth_block,
            context_block,
        ],
        out_specs=(depth_block, context_block),
        scratch_shapes=[
            pltpu.VMEM((blocks // 2,) + returned.shape[1:], BF),
            pltpu.SemaphoreType.DMA((steps,)),
        ],
        compiler_params=pltpu.CompilerParams(vmem_limit_bytes=24 << 20),
        name="final",
    )(slots, in_hbm(returned), depth, context)


def paired_weights(kernel):
    layers, taps, _, inner, outer = kernel.shape
    first = jnp.pad(kernel, ((0, 0), (0, 0), (0, 1), (0, 0), (0, 0)))
    second = jnp.pad(kernel, ((0, 0), (0, 0), (1, 0), (0, 0), (0, 0)))
    return jnp.concatenate([first, second], axis=4).reshape(layers, 4 * taps * inner, 2 * outer)


def per_device(
    depth_weights, context, block_owner, block_local, block_cell, conv_weight, cotangent
):
    cams_here, blocks_cam, bins, pixels = depth_weights.shape
    channels = context.shape[3]
    rows, cols, _ = cotangent.shape
    mid = cols // 2
    axes = ("cam", "tile")
    owners = lax.axis_size(axes)
    blocks = cams_here * blocks_cam
    depth = depth_weights.reshape(blocks, bins, pixels)
    flat_context = context.reshape(blocks, pixels, channels)
    owner = block_owner.transpose(0, 2, 1)

    sent, slots = pack(
        in_hbm(owner), in_hbm(block_local), in_hbm(block_cell), in_hbm(depth),
        in_hbm(flat_context), owners,
    )
    message = lax.all_to_all(sent, axes, split_axis=0, concat_axis=0, tiled=True)

    cot = cotangent.reshape(rows, mid, 2 * channels)
    down, up = ring("cam")
    east, west = ring("tile")
    cot_above = lax.ppermute(cot[rows - LAYERS :], "cam", down)
    cot_below = lax.ppermute(cot[:LAYERS], "cam", up)
    cot_left = lax.ppermute(cot[:, mid - PAIRS :], "tile", east)
    cot_right = lax.ppermute(cot[:, :PAIRS], "tile", west)
    cot_middle = jnp.concatenate([cot_left, cot, cot_right], axis=1)
    turned_weight = conv_weight[:, ::-1, ::-1].swapaxes(3, 4)
    weights = jnp.concatenate([paired_weights(conv_weight), paired_weights(turned_weight)], axis=0)
    weights = weights * jnp.asarray(0.5, BF)
    cam = lax.axis_index("cam")
    tile = lax.axis_index("tile")
    edges = jnp.stack(
        [cam == 0, cam == lax.axis_size("cam") - 1, tile == 0, tile == lax.axis_size("tile") - 1]
    ).astype(jnp.int32)

    middle, tiles = splat(message, rows, cols)

    above = lax.ppermute(middle[rows - EXT :], "cam", down)
    below = lax.ppermute(middle[:EXT], "cam", up)
    left = lax.ppermute(middle[:, mid - PAIRS :], "tile", east)
    right = lax.ppermute(middle[:, :PAIRS], "tile", west)
    sides = jnp.concatenate([left, right], axis=1)
    cot_sides = jnp.concatenate([cot_middle[:, :PAIRS], cot_middle[:, PAIRS + mid :]], axis=1)
    lower = jnp.concatenate([sides[rows - EXT :], cot_sides[rows - LAYERS :]], axis=0)
    upper = jnp.concatenate([sides[:EXT], cot_sides[:LAYERS]], axis=0)
    corner_above = lax.ppermute(lower, "cam", down)
    corner_below = lax.ppermute(upper, "cam", up)

    bev, grad = convs(
        edges, weights, cot_middle, middle, above, below, left, right, corner_above,
        corner_below, cot_above, cot_below,
    )
    rows_back = gather(tiles, message, grad)
    returned = lax.all_to_all(rows_back, axes, split_axis=0, concat_axis=0, tiled=True)
    grad_depth, grad_context = final(slots, returned, in_hbm(depth), in_hbm(flat_context))
    return (
        bev[LAYERS : LAYERS + rows].reshape(cotangent.shape),
        grad_depth.reshape(depth_weights.shape),
        grad_context.reshape(context.shape),
    )


def solution(mesh):
    placed = (
        P(("cam", "tile"), None, None, None),
        P(("cam", "tile"), None, None, None),
        P(("cam", "tile"), None, None),
        P(("cam", "tile"), None),
        P(("cam", "tile"), None, None),
        P(),
        P("cam", "tile", None),
    )
    return jax.shard_map(
        per_device,
        mesh=mesh,
        in_specs=placed,
        out_specs=(
            P("cam", "tile", None),
            P(("cam", "tile"), None, None, None),
            P(("cam", "tile"), None, None, None),
        ),
        check_vma=False,
    )
```

```python
import functools

import jax
import jax.numpy as jnp
from jax import lax
from jax.experimental import pallas as pl
from jax.experimental.pallas import tpu as pltpu
from jax.sharding import PartitionSpec as P

TS = 16
LAYERS = 4
EXT = 2 * LAYERS
PAIRS = 8
PARTS = 4
CHUNK = 16
EMPTY = 256.0
ABSENT = 255
BF = jnp.bfloat16
F32 = jnp.float32


def ring(axis):
    count = lax.axis_size(axis)
    ends = count - 1
    down = [(i, i + 1) for i in range(ends)]
    up = [(i + 1, i) for i in range(ends)]
    return down, up


def take_slot(owner, count):
    rank = count[owner]
    count[owner] = rank + 1
    return rank


def clear_counts(count, size):
    for i in range(size):
        count[i] = 0


def in_hbm(x):
    return pltpu.with_memory_space_constraint(x, pltpu.HBM)


def owner_of(owner, at):
    each = owner.shape[2]
    return owner[lax.div(at, each), 0, lax.rem(at, each)]


def pair_cells(cells):
    return (cells // TS) * TS + (cells % 2) * (TS // 2) + (cells % TS) // 2


def pack_kernel(
    owner, local, cells, depth_far, context_far, out, slots,
    count, depth, context, wide, lifted, meta, small, sems,
):
    blocks, bins, _ = depth.shape
    owners = out.shape[0]
    chunk = blocks // PARTS
    arrivals = []
    for part in range(PARTS):
        here = pl.ds(part * chunk, chunk)
        for k, (far, near) in enumerate(((depth_far, depth), (context_far, context))):
            copy = pltpu.make_async_copy(far.at[here], near.at[here], sems.at[2 * part + k])
            copy.start()
            arrivals.append(copy)
    clear_counts(count, owners)
    kind = lax.broadcasted_iota(jnp.int32, meta.shape, 1)
    meta[...] = jnp.where(kind == 0, EMPTY, ABSENT)
    numbers = pair_cells(cells[...]).astype(F32).reshape(blocks, bins)
    wide[...] = jnp.concatenate([numbers, numbers], axis=1)
    lane = lax.broadcasted_iota(jnp.int32, (1, 2 * bins), 1)
    each = local.shape[1]

    def describe(b, carry):
        to = owner_of(owner, b)
        tile = local[lax.div(b, each), lax.rem(b, each)].astype(F32)
        rank = take_slot(to, count)
        slots[b] = 2 * to + rank
        mine = (lane // bins) == rank
        row = wide[pl.ds(b, 1), :]
        meta[to, pl.ds(0, 1), :] = jnp.where(mine, row, meta[to, pl.ds(0, 1), :])
        meta[to, pl.ds(1, 1), :] = jnp.where(mine, tile, meta[to, pl.ds(1, 1), :])
        return carry

    lax.fori_loop(0, blocks, describe, 0, unroll=8)
    small[...] = meta[...].astype(BF)
    meta_copy = pltpu.make_async_copy(
        small, out.at[:, pl.ds(2 * bins, 8), :], sems.at[2 * PARTS]
    )
    meta_copy.start()

    for part in range(PARTS):
        for copy in arrivals[2 * part : 2 * part + 2]:
            copy.wait()
        for b in range(part * chunk, (part + 1) * chunk):
            product = jnp.dot(depth[b], context[b], preferred_element_type=F32)
            half = pl.ds((b % 2) * bins, bins)
            lifted[b // 2, half, :] = product.astype(BF)
        for b in range(part * chunk, (part + 1) * chunk):
            slot = slots[b]
            pltpu.make_async_copy(
                lifted.at[b // 2, pl.ds((b % 2) * bins, bins), :],
                out.at[
                    lax.shift_right_logical(slot, 1),
                    pl.ds(pl.multiple_of((slot & 1) * bins, bins), bins),
                    :,
                ],
                sems.at[2 * PARTS + 1],
            ).start()
    meta_copy.wait()
    pltpu.make_async_copy(
        lifted, out.at[pl.ds(0, blocks // 2), pl.ds(0, 2 * bins), :], sems.at[2 * PARTS + 1]
    ).wait()


def pack(owner, local, cells, depth, context, owners):
    blocks, bins, _ = depth.shape
    channels = context.shape[2]
    smem = pl.BlockSpec(memory_space=pltpu.SMEM)
    hbm = pl.BlockSpec(memory_space=pltpu.HBM)
    return pl.pallas_call(
        pack_kernel,
        out_shape=(
            pltpu.HBM((owners, 2 * bins + 8, channels), BF),
            jax.ShapeDtypeStruct((blocks,), jnp.int32),
        ),
        in_specs=[smem, smem, pl.BlockSpec(memory_space=pltpu.VMEM), hbm, hbm],
        out_specs=(hbm, smem),
        scratch_shapes=[
            pltpu.SMEM((owners,), jnp.int32),
            pltpu.VMEM(depth.shape, BF),
            pltpu.VMEM(context.shape, BF),
            pltpu.VMEM((blocks, 2 * bins), F32),
            pltpu.VMEM((blocks // 2, 2 * bins, channels), BF),
            pltpu.VMEM((owners, 8, 2 * bins), F32),
            pltpu.VMEM((owners, 8, 2 * bins), BF),
            pltpu.SemaphoreType.DMA((2 * PARTS + 2,)),
        ],
        compiler_params=pltpu.CompilerParams(vmem_limit_bytes=24 << 20),
        name="pack",
    )(owner, local, cells, depth, context)


def cell_onehot(cell_row, cells):
    number = lax.broadcasted_iota(jnp.int32, (cells, cell_row.shape[1]), 0)
    return jnp.where(number == cell_row, 1.0, 0.0).astype(BF)


def splat_kernel(
    meta_all, message, out, tiles_out, acc, rows, cells, codes, numbers, group, group_tile, sems
):
    owners, _, channels = meta_all.shape
    bins = channels // 2
    tile_count = acc.shape[1] // 8
    groups = group_tile.shape[0] - owners // 2
    arrival = pltpu.make_async_copy(
        message.at[:, pl.ds(0, 2 * bins), :], rows.at[pl.ds(0, owners)], sems.at[0]
    )
    arrival.start()
    meta = meta_all[...].astype(F32)
    cells[0:owners, :] = meta[:, 0, :].astype(jnp.int32)
    cells[owners:, :] = jnp.full((8, channels), TS * TS, jnp.int32)
    rows[owners] = jnp.zeros((2 * bins, channels), BF)
    lane = lax.broadcasted_iota(jnp.int32, (owners, channels), 1)
    line = lax.broadcasted_iota(jnp.int32, (owners, channels), 0)
    named = meta[:, 1, :]
    swapped = pltpu.roll(named, bins, 1)
    across, place, amount = [], [], []
    for rank in range(2):
        down = jnp.where((lane < bins) == (rank == 0), named, swapped).astype(jnp.int32)
        tile = down.T
        earlier = (down == tile) & (line < lane)
        across.append(tile)
        place.append(jnp.sum(earlier.astype(jnp.int32), axis=0, keepdims=True))
        amount.append(jnp.sum((line == tile).astype(jnp.int32), axis=1, keepdims=True))
    needed = lax.shift_right_logical(jnp.maximum(amount[0], amount[1]) + 1, 1)
    needed = jnp.where(line < tile_count, needed, 0)
    for rank in range(2):
        tile = across[rank][0:1]
        base = jnp.sum(jnp.where(line < across[rank], needed, 0), axis=0, keepdims=True)
        at = jnp.where(tile < tile_count, base, groups) + lax.shift_right_logical(place[rank], 1)
        codes[rank : rank + 1, :] = 4 * at + 2 * rank + (place[rank] & 1)
        codes[2 + rank : 3 + rank, :] = tile
        tiles_out[rank : rank + 1, :] = jnp.minimum(tile, tile_count - 1)
    codes[4:5, :] = jnp.sum(needed, axis=0, keepdims=True)
    copy = pltpu.make_async_copy(codes, numbers, sems.at[1])
    copy.start()
    acc[...] = jnp.zeros(acc.shape, F32)
    for i in range(4 * groups):
        group[i] = owners
    for i in range(groups):
        group_tile[i] = 0
    copy.wait()
    total = numbers[4, 0]

    def place_source(s, carry):
        for rank in range(2):
            at = numbers[rank, s]
            group[at] = s
            group_tile[lax.shift_right_logical(at, 2)] = numbers[2 + rank, s]
        return carry

    lax.fori_loop(0, owners, place_source, 0, unroll=16)
    arrival.wait()
    low = lax.broadcasted_iota(jnp.int32, (1, channels), 1) < bins

    def batch(b, carry):
        for q in range(8):
            at = 8 * b + q
            ids = [group[4 * at + slot] for slot in range(4)]
            hot = [
                cell_onehot(
                    jnp.where(low, cells[pl.ds(ids[k], 1), :], cells[pl.ds(ids[2 + k], 1), :]),
                    TS * TS,
                )
                for k in range(2)
            ]
            parts = []
            for k in range(2):
                parts += [rows[ids[k], 0:bins, :], rows[ids[2 + k], bins : 2 * bins, :]]
            sums = jnp.dot(
                jnp.concatenate(hot, axis=1),
                jnp.concatenate(parts, axis=0),
                preferred_element_type=F32,
            ).reshape(TS, 2, 8, channels)
            here = pl.ds(pl.multiple_of(group_tile[at] * 8, 8), 8)
            for side in range(2):
                acc[:, here, side * channels : (side + 1) * channels] += sums[:, side]
        return carry

    lax.fori_loop(0, lax.div(total + 7, 8), batch, 0)
    out[...] = acc[...].astype(BF)


def splat(message, rows, cols):
    owners, height, channels = message.shape
    shape = (rows, cols // 2, 2 * channels)
    groups = owners + cols // TS
    spare = groups + owners // 2
    return pl.pallas_call(
        splat_kernel,
        out_shape=(
            jax.ShapeDtypeStruct(shape, BF),
            jax.ShapeDtypeStruct((2, owners), jnp.int32),
        ),
        grid=(1,),
        in_specs=[
            pl.BlockSpec((owners, 8, channels), lambda i: (0, height // 8 - 1, 0)),
            pl.BlockSpec(memory_space=pltpu.HBM),
        ],
        out_specs=(
            pl.BlockSpec(shape, lambda i: (0, 0, 0)),
            pl.BlockSpec((2, owners), lambda i: (0, 0)),
        ),
        scratch_shapes=[
            pltpu.VMEM(shape, F32),
            pltpu.VMEM((owners + 1, height - 8, channels), BF),
            pltpu.VMEM((owners + 8, channels), jnp.int32),
            pltpu.VMEM((8, owners), jnp.int32),
            pltpu.SMEM((8, owners), jnp.int32),
            pltpu.SMEM((4 * spare,), jnp.int32),
            pltpu.SMEM((spare,), jnp.int32),
            pltpu.SemaphoreType.DMA((2,)),
        ],
        compiler_params=pltpu.CompilerParams(vmem_limit_bytes=24 << 20),
        name="splat",
    )(in_hbm(message), in_hbm(message))


def chunks_of(count):
    parts = -(-count // 7)
    size = -(-count // parts)
    return size, [min(i * size, count - size) for i in range(parts)]


def conv_kernel(
    edges, middle, above, below, left, right, corner_above, corner_below,
    cot_above, cot_below, tiles, meta_far, cot_far, weights_far,
    bev_far, back_far, ping, pong, slopes, sums, weights, cot, bev, grad, back, meta, columns, sems,
):
    rows, mid, double = middle.shape
    channels = double // 2
    wide = mid + 2 * PAIRS
    tall = rows + 2 * EXT
    arrivals = [
        pltpu.make_async_copy(weights_far.at[i], weights.at[i], sems.at[i])
        for i in range(2 * LAYERS)
    ]
    cot_arrival = pltpu.make_async_copy(
        cot_far, cot.at[pl.ds(LAYERS, rows)], sems.at[2 * LAYERS]
    )
    slots = back.shape[1]
    meta_arrival = pltpu.make_async_copy(
        meta_far.at[:, pl.ds(slots, 8), :], meta, sems.at[2 * LAYERS + 1]
    )
    for copy in arrivals[:LAYERS]:
        copy.start()
    cot_arrival.start()
    meta_arrival.start()
    for copy in arrivals[: LAYERS - 1 : -1]:
        copy.start()

    def put(ref, row, value):
        first = value[:, :channels]
        second = value[:, channels:]
        ref[row, :, 0:channels] = pltpu.roll(second, 1, 0).astype(BF)
        ref[row, :, channels : 3 * channels] = value.astype(BF)
        ref[row, :, 3 * channels :] = pltpu.roll(first, wide - 1, 0).astype(BF)

    def joined(west, center, east):
        return jnp.concatenate([west.astype(F32), center.astype(F32), east.astype(F32)], axis=0)

    def load(row, west, center, east):
        put(ping, row, joined(west, center, east))

    def load_outer(k, carry):
        load(k, corner_above[k, 0:PAIRS], above[k], corner_above[k, PAIRS:])
        load(EXT + rows + k, corner_below[k, 0:PAIRS], below[k], corner_below[k, PAIRS:])
        return carry

    def load_inner(k, carry):
        load(EXT + k, left[k], middle[k], right[k])
        return carry

    lax.fori_loop(0, EXT, load_outer, 0)
    lax.fori_loop(0, rows, load_inner, 0)
    for k in range(LAYERS):
        for corner, field, base in (
            (corner_above, cot_above, 0), (corner_below, cot_below, LAYERS + rows)
        ):
            west, east = corner[EXT + k, 0:PAIRS], corner[EXT + k, PAIRS:]
            cot[base + k] = joined(west, field[k], east).astype(BF)

    def matmul(ref, index, start, size):
        taps = [ref[pl.ds(start + tap, size)].reshape(size * wide, 2 * double) for tap in range(3)]
        total = jnp.dot(
            jnp.concatenate(taps, axis=1), weights[index], preferred_element_type=F32
        )
        sums[0:size] = total.reshape(size, wide, double)

    kept = [tall - 2 - 2 * layer for layer in range(LAYERS)]
    offsets = [sum(kept[:layer]) for layer in range(LAYERS)]

    def forward(layer, target, start, size):
        for side in range(size):
            here = start + side
            row = layer + 1 + here
            inside = jnp.where(
                ((row < EXT) & (edges[0] == 1)) | ((row >= EXT + rows) & (edges[1] == 1)), 0.0, 1.0
            )
            part = sums[side]
            twice = 1.0 + jnp.tanh(part)
            twice = jnp.concatenate(
                [
                    twice[:PAIRS] * jnp.where(edges[2] == 1, 0.0, inside),
                    twice[PAIRS : PAIRS + mid] * inside,
                    twice[PAIRS + mid :] * jnp.where(edges[3] == 1, 0.0, inside),
                ],
                axis=0,
            )
            active = part * twice
            slope = twice + active * (2.0 - twice)
            if layer < LAYERS - 1:
                put(target, here, active)
                slopes[offsets[layer] + here] = slope.astype(slopes.dtype)
            else:
                bev[here] = active[PAIRS : PAIRS + mid].astype(BF)
                put(target, here, cot[here].astype(F32) * slope)

    def backward(step, target, start, size):
        layer = LAYERS - 1 - step
        for side in range(size):
            here = start + side
            if layer > 0:
                slope = slopes[offsets[layer - 1] + here + 2 * (step + 1)].astype(F32)
                put(target, here, sums[side] * slope)
            else:
                value = sums[side, PAIRS : PAIRS + mid]
                for tile in range(mid // 8):
                    piece = value[tile * 8 : (tile + 1) * 8]
                    piece = jnp.concatenate([piece[:, :channels], piece[:, channels:]], axis=0)
                    at = pl.ds(pl.multiple_of(here * TS, TS), TS)
                    grad[tile, at, :] = piece.astype(BF)

    stages = []
    for layer in range(LAYERS):
        stages.append((layer, kept[layer], functools.partial(forward, layer)))
    for step in range(LAYERS):
        layer = LAYERS - 1 - step
        stages.append((LAYERS + layer, rows + 2 * layer, functools.partial(backward, step)))

    source, target = ping, pong
    finish = None
    for index, count, epilogue in stages:
        size, starts = chunks_of(count)
        arrivals[index].wait()
        if index == LAYERS - 1:
            cot_arrival.wait()
        if finish is not None:
            finish()
        matmul(source, index, 0, size)

        def steady(k, carry, index=index, count=count, size=size, source=source, target=target, epilogue=epilogue):
            epilogue(target, (k - 1) * size, size)
            matmul(source, index, jnp.minimum(k * size, count - size), size)
            return carry

        lax.fori_loop(1, len(starts), steady, 0)
        finish = functools.partial(epilogue, target, starts[-1], size)
        source, target = target, source
        if index == 2 * LAYERS - 1:
            bev_copy = pltpu.make_async_copy(
                bev.at[pl.ds(LAYERS, rows)], bev_far, sems.at[2 * LAYERS + 2]
            )
            bev_copy.start()
            meta_arrival.wait()
            columns[...] = meta[...].astype(F32)[:, 0, :].T.astype(jnp.int32)
    finish()

    owners = back.shape[0]
    bins = slots // 2
    _, cells, _ = grad.shape
    number = lax.broadcasted_iota(jnp.int32, (slots, cells), 1)

    def answer(chunk, carry):
        first = chunk * CHUNK
        mine = pltpu.roll(columns[...], lax.rem(owners - first, owners), 1)
        for s in range(CHUNK):
            hot = jnp.where(mine[:, s : s + 1] == number, 1.0, 0.0).astype(BF)
            both = jnp.concatenate(
                [grad[tiles[0, first + s]], grad[tiles[1, first + s]]], axis=1
            )
            picked = jnp.dot(hot, both, preferred_element_type=F32)
            back[first + s, 0:bins, :] = picked[:bins, :channels].astype(BF)
            back[first + s, bins:, :] = picked[bins:, channels:].astype(BF)
        here = pl.ds(pl.multiple_of(first, CHUNK), CHUNK)
        pltpu.make_async_copy(back.at[here], back_far.at[here], sems.at[2 * LAYERS + 3]).start()
        return carry

    lax.fori_loop(0, owners // CHUNK, answer, 0)
    bev_copy.wait()
    pltpu.make_async_copy(back, back_far, sems.at[2 * LAYERS + 3]).wait()


def convs(edges, tiles, message, cot, weights, *fields):
    middle = fields[0]
    rows, mid, double = middle.shape
    wide = mid + 2 * PAIRS
    tall = rows + 2 * EXT
    owners, height, channels = message.shape
    kept = sum(tall - 2 - 2 * layer for layer in range(LAYERS - 1))
    vmem = pl.BlockSpec(memory_space=pltpu.VMEM)
    smem = pl.BlockSpec(memory_space=pltpu.SMEM)
    hbm = pl.BlockSpec(memory_space=pltpu.HBM)
    buffer = pltpu.VMEM((tall, wide, 2 * double), BF)
    return pl.pallas_call(
        conv_kernel,
        out_shape=(
            pltpu.HBM(middle.shape, BF),
            pltpu.HBM((owners, height - 8, channels), BF),
        ),
        in_specs=[smem] + [vmem] * len(fields) + [smem] + [hbm] * 3,
        out_specs=(hbm, hbm),
        scratch_shapes=[
            buffer,
            buffer,
            pltpu.VMEM((kept, wide, double), F32),
            pltpu.VMEM((7, wide, double), F32),
            pltpu.VMEM(weights.shape, BF),
            pltpu.VMEM((rows + 2 * LAYERS, wide, double), BF),
            pltpu.VMEM((rows + 2 * LAYERS, mid, double), BF),
            pltpu.VMEM((mid // 8, rows * TS, channels), BF),
            pltpu.VMEM((owners, height - 8, channels), BF),
            pltpu.VMEM((owners, 8, channels), BF),
            pltpu.VMEM((height - 8, owners), jnp.int32),
            pltpu.SemaphoreType.DMA((2 * LAYERS + 4,)),
        ],
        compiler_params=pltpu.CompilerParams(vmem_limit_bytes=50 << 20),
        name="convs",
    )(edges, *fields, tiles, in_hbm(message), in_hbm(cot), in_hbm(weights))


def final_kernel(slots, returned, depth, context, grad_depth, grad_context, fetched, sems):
    step = pl.program_id(0)
    blocks, bins, _ = depth.shape
    halves = blocks // 2

    def fetch(first, group):
        for b in range(blocks):
            slot = slots[first + b]
            pltpu.make_async_copy(
                returned.at[
                    lax.shift_right_logical(slot, 1),
                    pl.ds(pl.multiple_of((slot & 1) * bins, bins), bins),
                    :,
                ],
                fetched.at[group * halves + b // 2, pl.ds((b % 2) * bins, bins), :],
                sems.at[group],
            ).start()

    @pl.when(step == 0)
    def _():
        fetch(0, 0)

    @pl.when(step + 1 < pl.num_programs(0))
    def _():
        fetch((step + 1) * blocks, step + 1)

    pltpu.make_async_copy(
        returned.at[pl.ds(0, halves)],
        fetched.at[pl.ds(pl.multiple_of(step * halves, halves), halves)],
        sems.at[step],
    ).wait()

    for b in range(blocks):
        rows = fetched[step * halves + b // 2, (b % 2) * bins : (b % 2 + 1) * bins, :]
        grad_depth[b] = lax.dot_general(
            rows, context[b], (((1,), (1,)), ((), ())), preferred_element_type=F32
        ).astype(BF)
        grad_context[b] = lax.dot_general(
            depth[b], rows, (((0,), (0,)), ((), ())), preferred_element_type=F32
        ).astype(BF)


def final(slots, returned, depth, context):
    blocks, bins, pixels = depth.shape
    channels = context.shape[2]
    steps = 4
    chunk = blocks // steps
    depth_block = pl.BlockSpec((chunk, bins, pixels), lambda i: (i, 0, 0))
    context_block = pl.BlockSpec((chunk, pixels, channels), lambda i: (i, 0, 0))
    return pl.pallas_call(
        final_kernel,
        out_shape=(
            jax.ShapeDtypeStruct(depth.shape, BF),
            jax.ShapeDtypeStruct(context.shape, BF),
        ),
        grid=(steps,),
        in_specs=[
            pl.BlockSpec(memory_space=pltpu.SMEM),
            pl.BlockSpec(memory_space=pltpu.HBM),
            depth_block,
            context_block,
        ],
        out_specs=(depth_block, context_block),
        scratch_shapes=[
            pltpu.VMEM((blocks // 2,) + returned.shape[1:], BF),
            pltpu.SemaphoreType.DMA((steps,)),
        ],
        compiler_params=pltpu.CompilerParams(vmem_limit_bytes=24 << 20),
        name="final",
    )(slots, in_hbm(returned), depth, context)


def paired_weights(kernel):
    layers, taps, _, inner, outer = kernel.shape
    first = jnp.pad(kernel, ((0, 0), (0, 0), (0, 1), (0, 0), (0, 0)))
    second = jnp.pad(kernel, ((0, 0), (0, 0), (1, 0), (0, 0), (0, 0)))
    return jnp.concatenate([first, second], axis=4).reshape(layers, 4 * taps * inner, 2 * outer)


def per_device(
    depth_weights, context, block_owner, block_local, block_cell, conv_weight, cotangent
):
    cams_here, blocks_cam, bins, pixels = depth_weights.shape
    channels = context.shape[3]
    rows, cols, _ = cotangent.shape
    mid = cols // 2
    axes = ("cam", "tile")
    owners = lax.axis_size(axes)
    blocks = cams_here * blocks_cam
    depth = depth_weights.reshape(blocks, bins, pixels)
    flat_context = context.reshape(blocks, pixels, channels)
    owner = block_owner.transpose(0, 2, 1)

    sent, slots = pack(
        in_hbm(owner), in_hbm(block_local), in_hbm(block_cell), in_hbm(depth),
        in_hbm(flat_context), owners,
    )
    message = lax.all_to_all(sent, axes, split_axis=0, concat_axis=0, tiled=True)

    cot = cotangent.reshape(rows, mid, 2 * channels)
    down, up = ring("cam")
    east, west = ring("tile")
    cot_above = lax.ppermute(cot[rows - LAYERS :], "cam", down)
    cot_below = lax.ppermute(cot[:LAYERS], "cam", up)
    cot_left = lax.ppermute(cot[:, mid - PAIRS :], "tile", east)
    cot_right = lax.ppermute(cot[:, :PAIRS], "tile", west)
    cot_middle = jnp.concatenate([cot_left, cot, cot_right], axis=1)
    turned_weight = conv_weight[:, ::-1, ::-1].swapaxes(3, 4)
    weights = jnp.concatenate([paired_weights(conv_weight), paired_weights(turned_weight)], axis=0)
    weights = weights * jnp.asarray(0.5, BF)
    cam = lax.axis_index("cam")
    tile = lax.axis_index("tile")
    edges = jnp.stack(
        [cam == 0, cam == lax.axis_size("cam") - 1, tile == 0, tile == lax.axis_size("tile") - 1]
    ).astype(jnp.int32)

    middle, tiles = splat(message, rows, cols)

    above = lax.ppermute(middle[rows - EXT :], "cam", down)
    below = lax.ppermute(middle[:EXT], "cam", up)
    left = lax.ppermute(middle[:, mid - PAIRS :], "tile", east)
    right = lax.ppermute(middle[:, :PAIRS], "tile", west)
    sides = jnp.concatenate([left, right], axis=1)
    cot_sides = jnp.concatenate([cot_middle[:, :PAIRS], cot_middle[:, PAIRS + mid :]], axis=1)
    lower = jnp.concatenate([sides[rows - EXT :], cot_sides[rows - LAYERS :]], axis=0)
    upper = jnp.concatenate([sides[:EXT], cot_sides[:LAYERS]], axis=0)
    corner_above = lax.ppermute(lower, "cam", down)
    corner_below = lax.ppermute(upper, "cam", up)

    bev, rows_back = convs(
        edges, tiles, message, cot_middle, weights, middle, above, below, left, right, corner_above,
        corner_below, cot_above, cot_below,
    )
    returned = lax.all_to_all(rows_back, axes, split_axis=0, concat_axis=0, tiled=True)
    grad_depth, grad_context = final(slots, returned, depth, flat_context)
    return (
        bev.reshape(cotangent.shape),
        grad_depth.reshape(depth_weights.shape),
        grad_context.reshape(context.shape),
    )


def solution(mesh):
    placed = (
        P(("cam", "tile"), None, None, None),
        P(("cam", "tile"), None, None, None),
        P(("cam", "tile"), None, None),
        P(("cam", "tile"), None),
        P(("cam", "tile"), None, None),
        P(),
        P("cam", "tile", None),
    )
    return jax.shard_map(
        per_device,
        mesh=mesh,
        in_specs=placed,
        out_specs=(
            P("cam", "tile", None),
            P(("cam", "tile"), None, None, None),
            P(("cam", "tile"), None, None, None),
        ),
        check_vma=False,
    )
```

```python
import functools

import jax
import jax.numpy as jnp
from jax import lax
from jax.experimental import pallas as pl
from jax.experimental.pallas import tpu as pltpu
from jax.sharding import PartitionSpec as P

TS = 16
LAYERS = 4
EXT = 2 * LAYERS
PAIRS = 8
PARTS = 4
CHUNK = 16
EMPTY = 256.0
ABSENT = 255
BF = jnp.bfloat16
F32 = jnp.float32


def ring(axis):
    count = lax.axis_size(axis)
    ends = count - 1
    down = [(i, i + 1) for i in range(ends)]
    up = [(i + 1, i) for i in range(ends)]
    return down, up


def take_slot(owner, count):
    rank = count[owner]
    count[owner] = rank + 1
    return rank


def clear_counts(count, size):
    for i in range(size):
        count[i] = 0


def in_hbm(x):
    return pltpu.with_memory_space_constraint(x, pltpu.HBM)


def owner_of(owner, at):
    each = owner.shape[2]
    return owner[lax.div(at, each), 0, lax.rem(at, each)]


def pair_cells(cells):
    return (cells // TS) * TS + (cells % 2) * (TS // 2) + (cells % TS) // 2


def pack_kernel(
    owner, local, cells, depth_far, context_far, out, slots,
    count, depth, context, wide, lifted, meta, small, sems,
):
    blocks, bins, _ = depth.shape
    owners = out.shape[0]
    chunk = blocks // PARTS
    arrivals = []
    for part in range(PARTS):
        here = pl.ds(part * chunk, chunk)
        for k, (far, near) in enumerate(((depth_far, depth), (context_far, context))):
            copy = pltpu.make_async_copy(far.at[here], near.at[here], sems.at[2 * part + k])
            copy.start()
            arrivals.append(copy)
    clear_counts(count, owners)
    kind = lax.broadcasted_iota(jnp.int32, meta.shape, 1)
    meta[...] = jnp.where(kind == 0, EMPTY, ABSENT)
    numbers = pair_cells(cells[...]).astype(F32).reshape(blocks, bins)
    wide[...] = jnp.concatenate([numbers, numbers], axis=1)
    lane = lax.broadcasted_iota(jnp.int32, (1, 2 * bins), 1)
    each = local.shape[1]

    def describe(b, carry):
        to = owner_of(owner, b)
        tile = local[lax.div(b, each), lax.rem(b, each)].astype(F32)
        rank = take_slot(to, count)
        slots[b] = 2 * to + rank
        mine = (lane // bins) == rank
        row = wide[pl.ds(b, 1), :]
        meta[to, pl.ds(0, 1), :] = jnp.where(mine, row, meta[to, pl.ds(0, 1), :])
        meta[to, pl.ds(1, 1), :] = jnp.where(mine, tile, meta[to, pl.ds(1, 1), :])
        return carry

    lax.fori_loop(0, blocks, describe, 0, unroll=8)
    small[...] = meta[...].astype(BF)
    meta_copy = pltpu.make_async_copy(
        small, out.at[:, pl.ds(2 * bins, 8), :], sems.at[2 * PARTS]
    )
    meta_copy.start()

    for part in range(PARTS):
        for copy in arrivals[2 * part : 2 * part + 2]:
            copy.wait()
        for b in range(part * chunk, (part + 1) * chunk):
            product = jnp.dot(depth[b], context[b], preferred_element_type=F32)
            half = pl.ds((b % 2) * bins, bins)
            lifted[b // 2, half, :] = product.astype(BF)
        for b in range(part * chunk, (part + 1) * chunk):
            slot = slots[b]
            pltpu.make_async_copy(
                lifted.at[b // 2, pl.ds((b % 2) * bins, bins), :],
                out.at[
                    lax.shift_right_logical(slot, 1),
                    pl.ds(pl.multiple_of((slot & 1) * bins, bins), bins),
                    :,
                ],
                sems.at[2 * PARTS + 1],
            ).start()
    meta_copy.wait()
    pltpu.make_async_copy(
        lifted, out.at[pl.ds(0, blocks // 2), pl.ds(0, 2 * bins), :], sems.at[2 * PARTS + 1]
    ).wait()


def pack(owner, local, cells, depth, context, owners):
    blocks, bins, _ = depth.shape
    channels = context.shape[2]
    smem = pl.BlockSpec(memory_space=pltpu.SMEM)
    hbm = pl.BlockSpec(memory_space=pltpu.HBM)
    return pl.pallas_call(
        pack_kernel,
        out_shape=(
            pltpu.HBM((owners, 2 * bins + 8, channels), BF),
            jax.ShapeDtypeStruct((blocks,), jnp.int32),
        ),
        in_specs=[smem, smem, pl.BlockSpec(memory_space=pltpu.VMEM), hbm, hbm],
        out_specs=(hbm, smem),
        scratch_shapes=[
            pltpu.SMEM((owners,), jnp.int32),
            pltpu.VMEM(depth.shape, BF),
            pltpu.VMEM(context.shape, BF),
            pltpu.VMEM((blocks, 2 * bins), F32),
            pltpu.VMEM((blocks // 2, 2 * bins, channels), BF),
            pltpu.VMEM((owners, 8, 2 * bins), F32),
            pltpu.VMEM((owners, 8, 2 * bins), BF),
            pltpu.SemaphoreType.DMA((2 * PARTS + 2,)),
        ],
        compiler_params=pltpu.CompilerParams(vmem_limit_bytes=24 << 20),
        name="pack",
    )(owner, local, cells, depth, context)


def cell_onehot(cell_row, cells):
    number = lax.broadcasted_iota(jnp.int32, (cells, cell_row.shape[1]), 0)
    return jnp.where(number == cell_row, 1.0, 0.0).astype(BF)


def splat_kernel(
    meta_all, message, out, tiles_out, acc, rows, cells, codes, numbers, group, sems
):
    owners, _, channels = meta_all.shape
    bins = channels // 2
    tile_count = acc.shape[1] // 8
    groups = group.shape[0] // 4 - owners // 2
    arrival = pltpu.make_async_copy(
        message.at[:, pl.ds(0, 2 * bins), :], rows.at[pl.ds(0, owners)], sems.at[0]
    )
    arrival.start()
    meta = meta_all[...].astype(F32)
    cells[0:owners, :] = meta[:, 0, :].astype(jnp.int32)
    cells[owners:, :] = jnp.full((8, channels), TS * TS, jnp.int32)
    rows[owners] = jnp.zeros((2 * bins, channels), BF)
    lane = lax.broadcasted_iota(jnp.int32, (owners, channels), 1)
    line = lax.broadcasted_iota(jnp.int32, (owners, channels), 0)
    named = meta[:, 1, :]
    swapped = pltpu.roll(named, bins, 1)
    across, place, amount = [], [], []
    for rank in range(2):
        down = jnp.where((lane < bins) == (rank == 0), named, swapped).astype(jnp.int32)
        tile = down.T
        earlier = (down == tile) & (line < lane)
        across.append(tile)
        place.append(jnp.sum(earlier.astype(jnp.int32), axis=0, keepdims=True))
        amount.append(jnp.sum((line == tile).astype(jnp.int32), axis=1, keepdims=True))
    needed = lax.shift_right_logical(jnp.maximum(amount[0], amount[1]) + 1, 1)
    needed = jnp.where(line < tile_count, needed, 0)
    for rank in range(2):
        tile = across[rank][0:1]
        base = jnp.sum(jnp.where(line < across[rank], needed, 0), axis=0, keepdims=True)
        at = jnp.where(tile < tile_count, base, groups) + lax.shift_right_logical(place[rank], 1)
        codes[rank : rank + 1, :] = 4 * at + 2 * rank + (place[rank] & 1)
        codes[2 + rank : 3 + rank, :] = 256 * tile + lane[0:1]
        tiles_out[rank : rank + 1, :] = jnp.minimum(tile, tile_count - 1)
    codes[4:5, :] = jnp.sum(needed, axis=0, keepdims=True)
    copy = pltpu.make_async_copy(codes, numbers, sems.at[1])
    copy.start()
    acc[...] = jnp.zeros(acc.shape, F32)
    for i in range(4 * groups):
        group[i] = owners
    copy.wait()
    total = numbers[4, 0]

    for s in range(owners):
        for rank in range(2):
            group[numbers[rank, s]] = numbers[2 + rank, s]
    arrival.wait()
    low = lax.broadcasted_iota(jnp.int32, (1, channels), 1) < bins

    def batch(b, carry):
        for q in range(8):
            named_slots = [group[4 * (8 * b + q) + slot] for slot in range(4)]
            ids = [slot & 255 for slot in named_slots]
            tile = lax.shift_right_logical(jnp.maximum(named_slots[0], named_slots[2]), 8)
            hot = [
                cell_onehot(
                    jnp.where(low, cells[pl.ds(ids[k], 1), :], cells[pl.ds(ids[2 + k], 1), :]),
                    TS * TS,
                )
                for k in range(2)
            ]
            parts = []
            for k in range(2):
                parts += [rows[ids[k], 0:bins, :], rows[ids[2 + k], bins : 2 * bins, :]]
            sums = jnp.dot(
                jnp.concatenate(hot, axis=1),
                jnp.concatenate(parts, axis=0),
                preferred_element_type=F32,
            ).reshape(TS, 2, 8, channels)
            here = pl.ds(pl.multiple_of(tile * 8, 8), 8)
            for side in range(2):
                acc[:, here, side * channels : (side + 1) * channels] += sums[:, side]
        return carry

    lax.fori_loop(0, lax.div(total + 7, 8), batch, 0)
    out[...] = acc[...].astype(BF)


def splat(message, rows, cols):
    owners, height, channels = message.shape
    shape = (rows, cols // 2, 2 * channels)
    groups = owners + cols // TS
    spare = groups + owners // 2
    return pl.pallas_call(
        splat_kernel,
        out_shape=(
            jax.ShapeDtypeStruct(shape, BF),
            jax.ShapeDtypeStruct((2, owners), jnp.int32),
        ),
        grid=(1,),
        in_specs=[
            pl.BlockSpec((owners, 8, channels), lambda i: (0, height // 8 - 1, 0)),
            pl.BlockSpec(memory_space=pltpu.HBM),
        ],
        out_specs=(
            pl.BlockSpec(shape, lambda i: (0, 0, 0)),
            pl.BlockSpec((2, owners), lambda i: (0, 0)),
        ),
        scratch_shapes=[
            pltpu.VMEM(shape, F32),
            pltpu.VMEM((owners + 1, height - 8, channels), BF),
            pltpu.VMEM((owners + 8, channels), jnp.int32),
            pltpu.VMEM((8, owners), jnp.int32),
            pltpu.SMEM((8, owners), jnp.int32),
            pltpu.SMEM((4 * spare,), jnp.int32),
            pltpu.SemaphoreType.DMA((2,)),
        ],
        compiler_params=pltpu.CompilerParams(vmem_limit_bytes=24 << 20),
        name="splat",
    )(in_hbm(message), in_hbm(message))


def chunks_of(count):
    parts = -(-count // 7)
    size = -(-count // parts)
    return size, [min(i * size, count - size) for i in range(parts)]


def conv_kernel(
    edges, middle, above, below, left, right, corner_above, corner_below,
    cot_above, cot_below, tiles, meta_far, cot_far, weights_far,
    bev_far, back_far, ping, pong, slopes, sums, weights, cot, bev, grad, back, meta, columns, sems,
):
    rows, mid, double = middle.shape
    channels = double // 2
    wide = mid + 2 * PAIRS
    tall = rows + 2 * EXT
    arrivals = [
        pltpu.make_async_copy(weights_far.at[i], weights.at[i], sems.at[i])
        for i in range(2 * LAYERS)
    ]
    cot_arrival = pltpu.make_async_copy(
        cot_far, cot.at[pl.ds(LAYERS, rows)], sems.at[2 * LAYERS]
    )
    slots = back.shape[1]
    meta_arrival = pltpu.make_async_copy(
        meta_far.at[:, pl.ds(slots, 8), :], meta, sems.at[2 * LAYERS + 1]
    )
    for copy in arrivals[:LAYERS]:
        copy.start()
    cot_arrival.start()
    meta_arrival.start()
    for copy in arrivals[: LAYERS - 1 : -1]:
        copy.start()

    def put(ref, row, value):
        first = value[:, :channels]
        second = value[:, channels:]
        ref[row, :, 0:channels] = pltpu.roll(second, 1, 0).astype(BF)
        ref[row, :, channels : 3 * channels] = value.astype(BF)
        ref[row, :, 3 * channels :] = pltpu.roll(first, wide - 1, 0).astype(BF)

    def joined(west, center, east):
        return jnp.concatenate([west.astype(F32), center.astype(F32), east.astype(F32)], axis=0)

    def load(row, west, center, east):
        put(ping, row, joined(west, center, east))

    def load_outer(k, carry):
        load(k, corner_above[k, 0:PAIRS], above[k], corner_above[k, PAIRS:])
        load(EXT + rows + k, corner_below[k, 0:PAIRS], below[k], corner_below[k, PAIRS:])
        return carry

    def load_inner(k, carry):
        load(EXT + k, left[k], middle[k], right[k])
        return carry

    lax.fori_loop(0, EXT, load_outer, 0)
    lax.fori_loop(0, rows, load_inner, 0)
    for k in range(LAYERS):
        for corner, field, base in (
            (corner_above, cot_above, 0), (corner_below, cot_below, LAYERS + rows)
        ):
            west, east = corner[EXT + k, 0:PAIRS], corner[EXT + k, PAIRS:]
            cot[base + k] = joined(west, field[k], east).astype(BF)

    def matmul(ref, index, start, size):
        taps = [ref[pl.ds(start + tap, size)].reshape(size * wide, 2 * double) for tap in range(3)]
        total = jnp.dot(
            jnp.concatenate(taps, axis=1), weights[index], preferred_element_type=F32
        )
        sums[0:size] = total.reshape(size, wide, double)

    kept = [tall - 2 - 2 * layer for layer in range(LAYERS)]
    offsets = [sum(kept[:layer]) for layer in range(LAYERS)]

    def forward(layer, target, start, size):
        for side in range(size):
            here = start + side
            row = layer + 1 + here
            inside = jnp.where(
                ((row < EXT) & (edges[0] == 1)) | ((row >= EXT + rows) & (edges[1] == 1)), 0.0, 1.0
            )
            part = sums[side]
            twice = 1.0 + jnp.tanh(part)
            twice = jnp.concatenate(
                [
                    twice[:PAIRS] * jnp.where(edges[2] == 1, 0.0, inside),
                    twice[PAIRS : PAIRS + mid] * inside,
                    twice[PAIRS + mid :] * jnp.where(edges[3] == 1, 0.0, inside),
                ],
                axis=0,
            )
            active = part * twice
            slope = twice + active * (2.0 - twice)
            if layer < LAYERS - 1:
                put(target, here, active)
                slopes[offsets[layer] + here] = slope.astype(slopes.dtype)
            else:
                bev[here] = active[PAIRS : PAIRS + mid].astype(BF)
                put(target, here, cot[here].astype(F32) * slope)

    def backward(step, target, start, size):
        layer = LAYERS - 1 - step
        for side in range(size):
            here = start + side
            if layer > 0:
                slope = slopes[offsets[layer - 1] + here + 2 * (step + 1)].astype(F32)
                put(target, here, sums[side] * slope)
            else:
                value = sums[side, PAIRS : PAIRS + mid]
                for tile in range(mid // 8):
                    piece = value[tile * 8 : (tile + 1) * 8]
                    piece = jnp.concatenate([piece[:, :channels], piece[:, channels:]], axis=0)
                    at = pl.ds(pl.multiple_of(here * TS, TS), TS)
                    grad[tile, at, :] = piece.astype(BF)

    stages = []
    for layer in range(LAYERS):
        stages.append((layer, kept[layer], functools.partial(forward, layer)))
    for step in range(LAYERS):
        layer = LAYERS - 1 - step
        stages.append((LAYERS + layer, rows + 2 * layer, functools.partial(backward, step)))

    source, target = ping, pong
    finish = None
    for index, count, epilogue in stages:
        size, starts = chunks_of(count)
        arrivals[index].wait()
        if index == LAYERS - 1:
            cot_arrival.wait()
        if finish is not None:
            finish()
        matmul(source, index, 0, size)

        def steady(k, carry, index=index, count=count, size=size, source=source, target=target, epilogue=epilogue):
            epilogue(target, (k - 1) * size, size)
            matmul(source, index, jnp.minimum(k * size, count - size), size)
            return carry

        lax.fori_loop(1, len(starts), steady, 0)
        finish = functools.partial(epilogue, target, starts[-1], size)
        source, target = target, source
        if index == 2 * LAYERS - 1:
            bev_copy = pltpu.make_async_copy(
                bev.at[pl.ds(LAYERS, rows)], bev_far, sems.at[2 * LAYERS + 2]
            )
            bev_copy.start()
            meta_arrival.wait()
            columns[...] = meta[...].astype(F32)[:, 0, :].T.astype(jnp.int32)
    finish()

    owners = back.shape[0]
    bins = slots // 2
    _, cells, _ = grad.shape
    number = lax.broadcasted_iota(jnp.int32, (slots, cells), 1)

    def answer(chunk, carry):
        first = chunk * CHUNK
        mine = pltpu.roll(columns[...], lax.rem(owners - first, owners), 1)
        for s in range(CHUNK):
            hot = jnp.where(mine[:, s : s + 1] == number, 1.0, 0.0).astype(BF)
            both = jnp.concatenate(
                [grad[tiles[0, first + s]], grad[tiles[1, first + s]]], axis=1
            )
            picked = jnp.dot(hot, both, preferred_element_type=F32)
            back[first + s, 0:bins, :] = picked[:bins, :channels].astype(BF)
            back[first + s, bins:, :] = picked[bins:, channels:].astype(BF)
        here = pl.ds(pl.multiple_of(first, CHUNK), CHUNK)
        pltpu.make_async_copy(back.at[here], back_far.at[here], sems.at[2 * LAYERS + 3]).start()
        return carry

    lax.fori_loop(0, owners // CHUNK, answer, 0)
    bev_copy.wait()
    pltpu.make_async_copy(back, back_far, sems.at[2 * LAYERS + 3]).wait()


def convs(edges, tiles, message, cot, weights, *fields):
    middle = fields[0]
    rows, mid, double = middle.shape
    wide = mid + 2 * PAIRS
    tall = rows + 2 * EXT
    owners, height, channels = message.shape
    kept = sum(tall - 2 - 2 * layer for layer in range(LAYERS - 1))
    vmem = pl.BlockSpec(memory_space=pltpu.VMEM)
    smem = pl.BlockSpec(memory_space=pltpu.SMEM)
    hbm = pl.BlockSpec(memory_space=pltpu.HBM)
    buffer = pltpu.VMEM((tall, wide, 2 * double), BF)
    return pl.pallas_call(
        conv_kernel,
        out_shape=(
            pltpu.HBM(middle.shape, BF),
            pltpu.HBM((owners, height - 8, channels), BF),
        ),
        in_specs=[smem] + [vmem] * len(fields) + [smem] + [hbm] * 3,
        out_specs=(hbm, hbm),
        scratch_shapes=[
            buffer,
            buffer,
            pltpu.VMEM((kept, wide, double), F32),
            pltpu.VMEM((7, wide, double), F32),
            pltpu.VMEM(weights.shape, BF),
            pltpu.VMEM((rows + 2 * LAYERS, wide, double), BF),
            pltpu.VMEM((rows + 2 * LAYERS, mid, double), BF),
            pltpu.VMEM((mid // 8, rows * TS, channels), BF),
            pltpu.VMEM((owners, height - 8, channels), BF),
            pltpu.VMEM((owners, 8, channels), BF),
            pltpu.VMEM((height - 8, owners), jnp.int32),
            pltpu.SemaphoreType.DMA((2 * LAYERS + 4,)),
        ],
        compiler_params=pltpu.CompilerParams(vmem_limit_bytes=50 << 20),
        name="convs",
    )(edges, *fields, tiles, in_hbm(message), in_hbm(cot), in_hbm(weights))


def final_kernel(slots, returned, depth, context, grad_depth, grad_context, fetched, sems):
    step = pl.program_id(0)
    blocks, bins, _ = depth.shape
    halves = blocks // 2

    def fetch(first, group):
        for b in range(blocks):
            slot = slots[first + b]
            pltpu.make_async_copy(
                returned.at[
                    lax.shift_right_logical(slot, 1),
                    pl.ds(pl.multiple_of((slot & 1) * bins, bins), bins),
                    :,
                ],
                fetched.at[group * halves + b // 2, pl.ds((b % 2) * bins, bins), :],
                sems.at[group],
            ).start()

    @pl.when(step == 0)
    def _():
        fetch(0, 0)

    @pl.when(step + 1 < pl.num_programs(0))
    def _():
        fetch((step + 1) * blocks, step + 1)

    pltpu.make_async_copy(
        returned.at[pl.ds(0, halves)],
        fetched.at[pl.ds(pl.multiple_of(step * halves, halves), halves)],
        sems.at[step],
    ).wait()

    for b in range(blocks):
        rows = fetched[step * halves + b // 2, (b % 2) * bins : (b % 2 + 1) * bins, :]
        grad_depth[b] = lax.dot_general(
            rows, context[b], (((1,), (1,)), ((), ())), preferred_element_type=F32
        ).astype(BF)
        grad_context[b] = lax.dot_general(
            depth[b], rows, (((0,), (0,)), ((), ())), preferred_element_type=F32
        ).astype(BF)


def final(slots, returned, depth, context):
    blocks, bins, pixels = depth.shape
    channels = context.shape[2]
    steps = 4
    chunk = blocks // steps
    depth_block = pl.BlockSpec((chunk, bins, pixels), lambda i: (i, 0, 0))
    context_block = pl.BlockSpec((chunk, pixels, channels), lambda i: (i, 0, 0))
    return pl.pallas_call(
        final_kernel,
        out_shape=(
            jax.ShapeDtypeStruct(depth.shape, BF),
            jax.ShapeDtypeStruct(context.shape, BF),
        ),
        grid=(steps,),
        in_specs=[
            pl.BlockSpec(memory_space=pltpu.SMEM),
            pl.BlockSpec(memory_space=pltpu.HBM),
            depth_block,
            context_block,
        ],
        out_specs=(depth_block, context_block),
        scratch_shapes=[
            pltpu.VMEM((blocks // 2,) + returned.shape[1:], BF),
            pltpu.SemaphoreType.DMA((steps,)),
        ],
        compiler_params=pltpu.CompilerParams(vmem_limit_bytes=24 << 20),
        name="final",
    )(slots, in_hbm(returned), depth, context)


def paired_weights(kernel):
    layers, taps, _, inner, outer = kernel.shape
    first = jnp.pad(kernel, ((0, 0), (0, 0), (0, 1), (0, 0), (0, 0)))
    second = jnp.pad(kernel, ((0, 0), (0, 0), (1, 0), (0, 0), (0, 0)))
    return jnp.concatenate([first, second], axis=4).reshape(layers, 4 * taps * inner, 2 * outer)


def per_device(
    depth_weights, context, block_owner, block_local, block_cell, conv_weight, cotangent
):
    cams_here, blocks_cam, bins, pixels = depth_weights.shape
    channels = context.shape[3]
    rows, cols, _ = cotangent.shape
    mid = cols // 2
    axes = ("cam", "tile")
    owners = lax.axis_size(axes)
    blocks = cams_here * blocks_cam
    depth = depth_weights.reshape(blocks, bins, pixels)
    flat_context = context.reshape(blocks, pixels, channels)
    owner = block_owner.transpose(0, 2, 1)

    sent, slots = pack(
        in_hbm(owner), in_hbm(block_local), in_hbm(block_cell), in_hbm(depth),
        in_hbm(flat_context), owners,
    )
    message = lax.all_to_all(sent, axes, split_axis=0, concat_axis=0, tiled=True)

    cot = cotangent.reshape(rows, mid, 2 * channels)
    down, up = ring("cam")
    east, west = ring("tile")
    cot_above = lax.ppermute(cot[rows - LAYERS :], "cam", down)
    cot_below = lax.ppermute(cot[:LAYERS], "cam", up)
    cot_left = lax.ppermute(cot[:, mid - PAIRS :], "tile", east)
    cot_right = lax.ppermute(cot[:, :PAIRS], "tile", west)
    cot_middle = jnp.concatenate([cot_left, cot, cot_right], axis=1)
    turned_weight = conv_weight[:, ::-1, ::-1].swapaxes(3, 4)
    weights = jnp.concatenate([paired_weights(conv_weight), paired_weights(turned_weight)], axis=0)
    weights = weights * jnp.asarray(0.5, BF)
    cam = lax.axis_index("cam")
    tile = lax.axis_index("tile")
    edges = jnp.stack(
        [cam == 0, cam == lax.axis_size("cam") - 1, tile == 0, tile == lax.axis_size("tile") - 1]
    ).astype(jnp.int32)

    message, cot_middle = lax.optimization_barrier((message, cot_middle))
    middle, tiles = splat(message, rows, cols)

    above = lax.ppermute(middle[rows - EXT :], "cam", down)
    below = lax.ppermute(middle[:EXT], "cam", up)
    left = lax.ppermute(middle[:, mid - PAIRS :], "tile", east)
    right = lax.ppermute(middle[:, :PAIRS], "tile", west)
    sides = jnp.concatenate([left, right], axis=1)
    cot_sides = jnp.concatenate([cot_middle[:, :PAIRS], cot_middle[:, PAIRS + mid :]], axis=1)
    lower = jnp.concatenate([sides[rows - EXT :], cot_sides[rows - LAYERS :]], axis=0)
    upper = jnp.concatenate([sides[:EXT], cot_sides[:LAYERS]], axis=0)
    corner_above = lax.ppermute(lower, "cam", down)
    corner_below = lax.ppermute(upper, "cam", up)

    bev, rows_back = convs(
        edges, tiles, message, cot_middle, weights, middle, above, below, left, right, corner_above,
        corner_below, cot_above, cot_below,
    )
    returned = lax.all_to_all(rows_back, axes, split_axis=0, concat_axis=0, tiled=True)
    grad_depth, grad_context = final(slots, returned, depth, flat_context)
    return (
        bev.reshape(cotangent.shape),
        grad_depth.reshape(depth_weights.shape),
        grad_context.reshape(context.shape),
    )


def solution(mesh):
    placed = (
        P(("cam", "tile"), None, None, None),
        P(("cam", "tile"), None, None, None),
        P(("cam", "tile"), None, None),
        P(("cam", "tile"), None),
        P(("cam", "tile"), None, None),
        P(),
        P("cam", "tile", None),
    )
    return jax.shard_map(
        per_device,
        mesh=mesh,
        in_specs=placed,
        out_specs=(
            P("cam", "tile", None),
            P(("cam", "tile"), None, None, None),
            P(("cam", "tile"), None, None, None),
        ),
        check_vma=False,
    )
```

```python
import functools

import jax
import jax.numpy as jnp
from jax import lax
from jax.experimental import pallas as pl
from jax.experimental.pallas import tpu as pltpu
from jax.sharding import PartitionSpec as P

TS = 16
LAYERS = 4
EXT = 2 * LAYERS
PAIRS = 8
PARTS = 4
CHUNK = 16
EMPTY = 256.0
ABSENT = 255
BF = jnp.bfloat16
F32 = jnp.float32


def ring(axis):
    count = lax.axis_size(axis)
    ends = count - 1
    down = [(i, i + 1) for i in range(ends)]
    up = [(i + 1, i) for i in range(ends)]
    return down, up


def take_slot(owner, count):
    rank = count[owner]
    count[owner] = rank + 1
    return rank


def clear_counts(count, size):
    for i in range(size):
        count[i] = 0


def in_hbm(x):
    return pltpu.with_memory_space_constraint(x, pltpu.HBM)


def owner_of(owner, at):
    each = owner.shape[2]
    return owner[lax.div(at, each), 0, lax.rem(at, each)]


def pair_cells(cells):
    return (cells // TS) * TS + (cells % 2) * (TS // 2) + (cells % TS) // 2


def pack_kernel(
    owner, local, cells, depth_far, context_far, out, slots,
    count, depth, context, wide, lifted, meta, small, sems,
):
    blocks, bins, _ = depth.shape
    owners = out.shape[0]
    chunk = blocks // PARTS
    arrivals = []
    for part in range(PARTS):
        here = pl.ds(part * chunk, chunk)
        for k, (far, near) in enumerate(((depth_far, depth), (context_far, context))):
            copy = pltpu.make_async_copy(far.at[here], near.at[here], sems.at[2 * part + k])
            copy.start()
            arrivals.append(copy)
    clear_counts(count, owners)
    kind = lax.broadcasted_iota(jnp.int32, meta.shape, 1)
    meta[...] = jnp.where(kind == 0, EMPTY, ABSENT)
    numbers = pair_cells(cells[...]).astype(F32).reshape(blocks, bins)
    wide[...] = jnp.concatenate([numbers, numbers], axis=1)
    lane = lax.broadcasted_iota(jnp.int32, (1, 2 * bins), 1)
    each = local.shape[1]

    def describe(b, carry):
        to = owner_of(owner, b)
        tile = local[lax.div(b, each), lax.rem(b, each)].astype(F32)
        rank = take_slot(to, count)
        slots[b] = 2 * to + rank
        mine = (lane // bins) == rank
        row = wide[pl.ds(b, 1), :]
        meta[to, pl.ds(0, 1), :] = jnp.where(mine, row, meta[to, pl.ds(0, 1), :])
        meta[to, pl.ds(1, 1), :] = jnp.where(mine, tile, meta[to, pl.ds(1, 1), :])
        return carry

    lax.fori_loop(0, blocks, describe, 0, unroll=8)
    small[...] = meta[...].astype(BF)
    meta_copy = pltpu.make_async_copy(
        small, out.at[:, pl.ds(2 * bins, 8), :], sems.at[2 * PARTS]
    )
    meta_copy.start()

    for part in range(PARTS):
        for copy in arrivals[2 * part : 2 * part + 2]:
            copy.wait()
        for b in range(part * chunk, (part + 1) * chunk):
            product = jnp.dot(depth[b], context[b], preferred_element_type=F32)
            half = pl.ds((b % 2) * bins, bins)
            lifted[b // 2, half, :] = product.astype(BF)
        for b in range(part * chunk, (part + 1) * chunk):
            slot = slots[b]
            pltpu.make_async_copy(
                lifted.at[b // 2, pl.ds((b % 2) * bins, bins), :],
                out.at[
                    lax.shift_right_logical(slot, 1),
                    pl.ds(pl.multiple_of((slot & 1) * bins, bins), bins),
                    :,
                ],
                sems.at[2 * PARTS + 1],
            ).start()
    meta_copy.wait()
    pltpu.make_async_copy(
        lifted, out.at[pl.ds(0, blocks // 2), pl.ds(0, 2 * bins), :], sems.at[2 * PARTS + 1]
    ).wait()


def pack(owner, local, cells, depth, context, owners):
    blocks, bins, _ = depth.shape
    channels = context.shape[2]
    smem = pl.BlockSpec(memory_space=pltpu.SMEM)
    hbm = pl.BlockSpec(memory_space=pltpu.HBM)
    return pl.pallas_call(
        pack_kernel,
        out_shape=(
            pltpu.HBM((owners, 2 * bins + 8, channels), BF),
            jax.ShapeDtypeStruct((blocks,), jnp.int32),
        ),
        in_specs=[smem, smem, pl.BlockSpec(memory_space=pltpu.VMEM), hbm, hbm],
        out_specs=(hbm, smem),
        scratch_shapes=[
            pltpu.SMEM((owners,), jnp.int32),
            pltpu.VMEM(depth.shape, BF),
            pltpu.VMEM(context.shape, BF),
            pltpu.VMEM((blocks, 2 * bins), F32),
            pltpu.VMEM((blocks // 2, 2 * bins, channels), BF),
            pltpu.VMEM((owners, 8, 2 * bins), F32),
            pltpu.VMEM((owners, 8, 2 * bins), BF),
            pltpu.SemaphoreType.DMA((2 * PARTS + 2,)),
        ],
        compiler_params=pltpu.CompilerParams(vmem_limit_bytes=24 << 20),
        name="pack",
    )(owner, local, cells, depth, context)


def cell_onehot(cell_row, cells):
    number = lax.broadcasted_iota(jnp.int32, (cells, cell_row.shape[1]), 0)
    return jnp.where(number == cell_row, 1.0, 0.0).astype(BF)


def splat_kernel(
    meta_all, message, out, tiles_out, acc, rows, cells, codes, numbers, group, sems
):
    owners, _, channels = meta_all.shape
    bins = channels // 2
    tile_count = acc.shape[1] // 8
    groups = group.shape[0] // 4 - owners // 2
    arrival = pltpu.make_async_copy(
        message.at[:, pl.ds(0, 2 * bins), :], rows.at[pl.ds(0, owners)], sems.at[0]
    )
    arrival.start()
    meta = meta_all[...].astype(F32)
    cells[0:owners, :] = meta[:, 0, :].astype(jnp.int32)
    cells[owners:, :] = jnp.full((8, channels), TS * TS, jnp.int32)
    rows[owners] = jnp.zeros((2 * bins, channels), BF)
    lane = lax.broadcasted_iota(jnp.int32, (owners, channels), 1)
    line = lax.broadcasted_iota(jnp.int32, (owners, channels), 0)
    named = meta[:, 1, :]
    swapped = pltpu.roll(named, bins, 1)
    across, place, amount = [], [], []
    for rank in range(2):
        down = jnp.where((lane < bins) == (rank == 0), named, swapped).astype(jnp.int32)
        tile = down.T
        earlier = (down == tile) & (line < lane)
        across.append(tile)
        place.append(jnp.sum(earlier.astype(jnp.int32), axis=0, keepdims=True))
        amount.append(jnp.sum((line == tile).astype(jnp.int32), axis=1, keepdims=True))
    needed = lax.shift_right_logical(jnp.maximum(amount[0], amount[1]) + 1, 1)
    needed = jnp.where(line < tile_count, needed, 0)
    for rank in range(2):
        tile = across[rank][0:1]
        base = jnp.sum(jnp.where(line < across[rank], needed, 0), axis=0, keepdims=True)
        at = jnp.where(tile < tile_count, base, groups) + lax.shift_right_logical(place[rank], 1)
        codes[rank : rank + 1, :] = 4 * at + 2 * rank + (place[rank] & 1)
        codes[2 + rank : 3 + rank, :] = 256 * tile + lane[0:1]
        tiles_out[rank : rank + 1, :] = jnp.minimum(tile, tile_count - 1)
    codes[4:5, :] = jnp.sum(needed, axis=0, keepdims=True)
    copy = pltpu.make_async_copy(codes, numbers, sems.at[1])
    copy.start()
    acc[...] = jnp.zeros(acc.shape, F32)
    for i in range(4 * groups):
        group[i] = owners
    copy.wait()
    total = numbers[4, 0]

    for s in range(owners):
        for rank in range(2):
            group[numbers[rank, s]] = numbers[2 + rank, s]
    arrival.wait()
    low = lax.broadcasted_iota(jnp.int32, (1, channels), 1) < bins

    def batch(b, carry):
        for q in range(8):
            named_slots = [group[4 * (8 * b + q) + slot] for slot in range(4)]
            ids = [slot & 255 for slot in named_slots]
            tile = lax.shift_right_logical(jnp.maximum(named_slots[0], named_slots[2]), 8)
            hot = [
                cell_onehot(
                    jnp.where(low, cells[pl.ds(ids[k], 1), :], cells[pl.ds(ids[2 + k], 1), :]),
                    TS * TS,
                )
                for k in range(2)
            ]
            parts = []
            for k in range(2):
                parts += [rows[ids[k], 0:bins, :], rows[ids[2 + k], bins : 2 * bins, :]]
            sums = jnp.dot(
                jnp.concatenate(hot, axis=1),
                jnp.concatenate(parts, axis=0),
                preferred_element_type=F32,
            ).reshape(TS, 2, 8, channels)
            here = pl.ds(pl.multiple_of(tile * 8, 8), 8)
            for side in range(2):
                acc[:, here, side * channels : (side + 1) * channels] += sums[:, side]
        return carry

    lax.fori_loop(0, lax.div(total + 7, 8), batch, 0)
    out[...] = acc[...].astype(BF)


def splat(message, rows, cols):
    owners, height, channels = message.shape
    shape = (rows, cols // 2, 2 * channels)
    groups = owners + cols // TS
    spare = groups + owners // 2
    return pl.pallas_call(
        splat_kernel,
        out_shape=(
            jax.ShapeDtypeStruct(shape, BF),
            jax.ShapeDtypeStruct((2, owners), jnp.int32),
        ),
        grid=(1,),
        in_specs=[
            pl.BlockSpec((owners, 8, channels), lambda i: (0, height // 8 - 1, 0)),
            pl.BlockSpec(memory_space=pltpu.HBM),
        ],
        out_specs=(
            pl.BlockSpec(shape, lambda i: (0, 0, 0)),
            pl.BlockSpec((2, owners), lambda i: (0, 0)),
        ),
        scratch_shapes=[
            pltpu.VMEM(shape, F32),
            pltpu.VMEM((owners + 1, height - 8, channels), BF),
            pltpu.VMEM((owners + 8, channels), jnp.int32),
            pltpu.VMEM((8, owners), jnp.int32),
            pltpu.SMEM((8, owners), jnp.int32),
            pltpu.SMEM((4 * spare,), jnp.int32),
            pltpu.SemaphoreType.DMA((2,)),
        ],
        compiler_params=pltpu.CompilerParams(vmem_limit_bytes=24 << 20),
        name="splat",
    )(in_hbm(message), in_hbm(message))


def chunks_of(count):
    parts = -(-count // 7)
    size = -(-count // parts)
    return size, parts, count - (parts - 1) * size


def conv_kernel(
    edges, middle, above, below, left, right, corner_above, corner_below,
    cot_above, cot_below, tiles, meta_far, cot_far, weights_far,
    bev_far, back_far, ping, pong, slopes, sums, weights, cot, bev, grad, back, meta, columns, sems,
):
    rows, mid, double = middle.shape
    channels = double // 2
    wide = mid + 2 * PAIRS
    tall = rows + 2 * EXT
    arrivals = [
        pltpu.make_async_copy(weights_far.at[i], weights.at[i], sems.at[i])
        for i in range(2 * LAYERS)
    ]
    cot_arrival = pltpu.make_async_copy(
        cot_far, cot.at[pl.ds(LAYERS, rows)], sems.at[2 * LAYERS]
    )
    slots = back.shape[1]
    meta_arrival = pltpu.make_async_copy(
        meta_far.at[:, pl.ds(slots, 8), :], meta, sems.at[2 * LAYERS + 1]
    )
    for copy in arrivals[:LAYERS]:
        copy.start()
    cot_arrival.start()
    meta_arrival.start()
    for copy in arrivals[: LAYERS - 1 : -1]:
        copy.start()

    def put(ref, row, value):
        first = value[:, :channels]
        second = value[:, channels:]
        ref[row, :, 0:channels] = pltpu.roll(second, 1, 0).astype(BF)
        ref[row, :, channels : 3 * channels] = value.astype(BF)
        ref[row, :, 3 * channels :] = pltpu.roll(first, wide - 1, 0).astype(BF)

    def joined(west, center, east):
        return jnp.concatenate([west.astype(F32), center.astype(F32), east.astype(F32)], axis=0)

    def load(row, west, center, east):
        put(ping, row, joined(west, center, east))

    def load_outer(k, carry):
        load(k, corner_above[k, 0:PAIRS], above[k], corner_above[k, PAIRS:])
        load(EXT + rows + k, corner_below[k, 0:PAIRS], below[k], corner_below[k, PAIRS:])
        return carry

    def load_inner(k, carry):
        load(EXT + k, left[k], middle[k], right[k])
        return carry

    lax.fori_loop(0, EXT, load_outer, 0)
    lax.fori_loop(0, rows, load_inner, 0)
    for k in range(LAYERS):
        for corner, field, base in (
            (corner_above, cot_above, 0), (corner_below, cot_below, LAYERS + rows)
        ):
            west, east = corner[EXT + k, 0:PAIRS], corner[EXT + k, PAIRS:]
            cot[base + k] = joined(west, field[k], east).astype(BF)

    def matmul(ref, index, start, size):
        taps = [ref[pl.ds(start + tap, size)].reshape(size * wide, 2 * double) for tap in range(3)]
        total = jnp.dot(
            jnp.concatenate(taps, axis=1), weights[index], preferred_element_type=F32
        )
        sums[0:size] = total.reshape(size, wide, double)

    kept = [tall - 2 - 2 * layer for layer in range(LAYERS)]
    offsets = [sum(kept[:layer]) for layer in range(LAYERS)]

    def forward(layer, target, start, size):
        for side in range(size):
            here = start + side
            row = layer + 1 + here
            inside = jnp.where(
                ((row < EXT) & (edges[0] == 1)) | ((row >= EXT + rows) & (edges[1] == 1)), 0.0, 1.0
            )
            part = sums[side]
            twice = 1.0 + jnp.tanh(part)
            twice = jnp.concatenate(
                [
                    twice[:PAIRS] * jnp.where(edges[2] == 1, 0.0, inside),
                    twice[PAIRS : PAIRS + mid] * inside,
                    twice[PAIRS + mid :] * jnp.where(edges[3] == 1, 0.0, inside),
                ],
                axis=0,
            )
            active = part * twice
            slope = twice + active * (2.0 - twice)
            if layer < LAYERS - 1:
                put(target, here, active)
                slopes[offsets[layer] + here] = slope.astype(slopes.dtype)
            else:
                bev[here] = active[PAIRS : PAIRS + mid].astype(BF)
                put(target, here, cot[here].astype(F32) * slope)

    def backward(step, target, start, size):
        layer = LAYERS - 1 - step
        for side in range(size):
            here = start + side
            if layer > 0:
                slope = slopes[offsets[layer - 1] + here + 2 * (step + 1)].astype(F32)
                put(target, here, sums[side] * slope)
            else:
                value = sums[side, PAIRS : PAIRS + mid]
                for tile in range(mid // 8):
                    piece = value[tile * 8 : (tile + 1) * 8]
                    piece = jnp.concatenate([piece[:, :channels], piece[:, channels:]], axis=0)
                    at = pl.ds(pl.multiple_of(here * TS, TS), TS)
                    grad[tile, at, :] = piece.astype(BF)

    stages = []
    for layer in range(LAYERS):
        stages.append((layer, kept[layer], functools.partial(forward, layer)))
    for step in range(LAYERS):
        layer = LAYERS - 1 - step
        stages.append((LAYERS + layer, rows + 2 * layer, functools.partial(backward, step)))

    source, target = ping, pong
    finish = None
    for index, count, epilogue in stages:
        size, parts, last = chunks_of(count)
        arrivals[index].wait()
        if index == LAYERS - 1:
            cot_arrival.wait()
        if finish is not None:
            finish()
        matmul(source, index, 0, size)

        def steady(k, carry, index=index, count=count, size=size, source=source, target=target, epilogue=epilogue):
            epilogue(target, (k - 1) * size, size)
            matmul(source, index, k * size, size)
            return carry

        lax.fori_loop(1, parts if last == size else parts - 1, steady, 0)
        if last < size:
            epilogue(target, (parts - 2) * size, size)
            matmul(source, index, (parts - 1) * size, last)
        finish = functools.partial(epilogue, target, (parts - 1) * size, last)
        source, target = target, source
        if index == 2 * LAYERS - 1:
            bev_copy = pltpu.make_async_copy(
                bev.at[pl.ds(LAYERS, rows)], bev_far, sems.at[2 * LAYERS + 2]
            )
            bev_copy.start()
            meta_arrival.wait()
            columns[...] = meta[...].astype(F32)[:, 0, :].T.astype(jnp.int32)
    finish()

    owners = back.shape[0]
    bins = slots // 2
    _, cells, _ = grad.shape
    number = lax.broadcasted_iota(jnp.int32, (slots, cells), 1)

    def answer(chunk, carry):
        first = chunk * CHUNK
        mine = pltpu.roll(columns[...], lax.rem(owners - first, owners), 1)
        for s in range(CHUNK):
            hot = jnp.where(mine[:, s : s + 1] == number, 1.0, 0.0).astype(BF)
            both = jnp.concatenate(
                [grad[tiles[0, first + s]], grad[tiles[1, first + s]]], axis=1
            )
            picked = jnp.dot(hot, both, preferred_element_type=F32)
            back[first + s, 0:bins, :] = picked[:bins, :channels].astype(BF)
            back[first + s, bins:, :] = picked[bins:, channels:].astype(BF)
        here = pl.ds(pl.multiple_of(first, CHUNK), CHUNK)
        pltpu.make_async_copy(back.at[here], back_far.at[here], sems.at[2 * LAYERS + 3]).start()
        return carry

    lax.fori_loop(0, owners // CHUNK, answer, 0)
    bev_copy.wait()
    pltpu.make_async_copy(back, back_far, sems.at[2 * LAYERS + 3]).wait()


def convs(edges, tiles, message, cot, weights, *fields):
    middle = fields[0]
    rows, mid, double = middle.shape
    wide = mid + 2 * PAIRS
    tall = rows + 2 * EXT
    owners, height, channels = message.shape
    kept = sum(tall - 2 - 2 * layer for layer in range(LAYERS - 1))
    vmem = pl.BlockSpec(memory_space=pltpu.VMEM)
    smem = pl.BlockSpec(memory_space=pltpu.SMEM)
    hbm = pl.BlockSpec(memory_space=pltpu.HBM)
    buffer = pltpu.VMEM((tall, wide, 2 * double), BF)
    return pl.pallas_call(
        conv_kernel,
        out_shape=(
            pltpu.HBM(middle.shape, BF),
            pltpu.HBM((owners, height - 8, channels), BF),
        ),
        in_specs=[smem] + [vmem] * len(fields) + [smem] + [hbm] * 3,
        out_specs=(hbm, hbm),
        scratch_shapes=[
            buffer,
            buffer,
            pltpu.VMEM((kept, wide, double), F32),
            pltpu.VMEM((7, wide, double), F32),
            pltpu.VMEM(weights.shape, BF),
            pltpu.VMEM((rows + 2 * LAYERS, wide, double), BF),
            pltpu.VMEM((rows + 2 * LAYERS, mid, double), BF),
            pltpu.VMEM((mid // 8, rows * TS, channels), BF),
            pltpu.VMEM((owners, height - 8, channels), BF),
            pltpu.VMEM((owners, 8, channels), BF),
            pltpu.VMEM((height - 8, owners), jnp.int32),
            pltpu.SemaphoreType.DMA((2 * LAYERS + 4,)),
        ],
        compiler_params=pltpu.CompilerParams(vmem_limit_bytes=50 << 20),
        name="convs",
    )(edges, *fields, tiles, in_hbm(message), in_hbm(cot), in_hbm(weights))


def final_kernel(slots, returned, depth, context, grad_depth, grad_context, fetched, sems):
    step = pl.program_id(0)
    blocks, bins, _ = depth.shape
    halves = blocks // 2

    def fetch(first, group):
        for b in range(blocks):
            slot = slots[first + b]
            pltpu.make_async_copy(
                returned.at[
                    lax.shift_right_logical(slot, 1),
                    pl.ds(pl.multiple_of((slot & 1) * bins, bins), bins),
                    :,
                ],
                fetched.at[group * halves + b // 2, pl.ds((b % 2) * bins, bins), :],
                sems.at[group],
            ).start()

    @pl.when(step == 0)
    def _():
        fetch(0, 0)

    @pl.when(step + 1 < pl.num_programs(0))
    def _():
        fetch((step + 1) * blocks, step + 1)

    pltpu.make_async_copy(
        returned.at[pl.ds(0, halves)],
        fetched.at[pl.ds(pl.multiple_of(step * halves, halves), halves)],
        sems.at[step],
    ).wait()

    for b in range(blocks):
        rows = fetched[step * halves + b // 2, (b % 2) * bins : (b % 2 + 1) * bins, :]
        grad_depth[b] = lax.dot_general(
            rows, context[b], (((1,), (1,)), ((), ())), preferred_element_type=F32
        ).astype(BF)
        grad_context[b] = lax.dot_general(
            depth[b], rows, (((0,), (0,)), ((), ())), preferred_element_type=F32
        ).astype(BF)


def final(slots, returned, depth, context):
    blocks, bins, pixels = depth.shape
    channels = context.shape[2]
    steps = 4
    chunk = blocks // steps
    depth_block = pl.BlockSpec((chunk, bins, pixels), lambda i: (i, 0, 0))
    context_block = pl.BlockSpec((chunk, pixels, channels), lambda i: (i, 0, 0))
    return pl.pallas_call(
        final_kernel,
        out_shape=(
            jax.ShapeDtypeStruct(depth.shape, BF),
            jax.ShapeDtypeStruct(context.shape, BF),
        ),
        grid=(steps,),
        in_specs=[
            pl.BlockSpec(memory_space=pltpu.SMEM),
            pl.BlockSpec(memory_space=pltpu.HBM),
            depth_block,
            context_block,
        ],
        out_specs=(depth_block, context_block),
        scratch_shapes=[
            pltpu.VMEM((blocks // 2,) + returned.shape[1:], BF),
            pltpu.SemaphoreType.DMA((steps,)),
        ],
        compiler_params=pltpu.CompilerParams(vmem_limit_bytes=24 << 20),
        name="final",
    )(slots, in_hbm(returned), depth, context)


def paired_weights(kernel):
    layers, taps, _, inner, outer = kernel.shape
    first = jnp.pad(kernel, ((0, 0), (0, 0), (0, 1), (0, 0), (0, 0)))
    second = jnp.pad(kernel, ((0, 0), (0, 0), (1, 0), (0, 0), (0, 0)))
    return jnp.concatenate([first, second], axis=4).reshape(layers, 4 * taps * inner, 2 * outer)


def per_device(
    depth_weights, context, block_owner, block_local, block_cell, conv_weight, cotangent
):
    cams_here, blocks_cam, bins, pixels = depth_weights.shape
    channels = context.shape[3]
    rows, cols, _ = cotangent.shape
    mid = cols // 2
    axes = ("cam", "tile")
    owners = lax.axis_size(axes)
    blocks = cams_here * blocks_cam
    depth = depth_weights.reshape(blocks, bins, pixels)
    flat_context = context.reshape(blocks, pixels, channels)
    owner = block_owner.transpose(0, 2, 1)

    sent, slots = pack(
        in_hbm(owner), in_hbm(block_local), in_hbm(block_cell), in_hbm(depth),
        in_hbm(flat_context), owners,
    )
    message = lax.all_to_all(sent, axes, split_axis=0, concat_axis=0, tiled=True)

    cot = cotangent.reshape(rows, mid, 2 * channels)
    down, up = ring("cam")
    east, west = ring("tile")
    cot_above = lax.ppermute(cot[rows - LAYERS :], "cam", down)
    cot_below = lax.ppermute(cot[:LAYERS], "cam", up)
    cot_left = lax.ppermute(cot[:, mid - PAIRS :], "tile", east)
    cot_right = lax.ppermute(cot[:, :PAIRS], "tile", west)
    cot_middle = jnp.concatenate([cot_left, cot, cot_right], axis=1)
    turned_weight = conv_weight[:, ::-1, ::-1].swapaxes(3, 4)
    weights = jnp.concatenate([paired_weights(conv_weight), paired_weights(turned_weight)], axis=0)
    weights = weights * jnp.asarray(0.5, BF)
    cam = lax.axis_index("cam")
    tile = lax.axis_index("tile")
    edges = jnp.stack(
        [cam == 0, cam == lax.axis_size("cam") - 1, tile == 0, tile == lax.axis_size("tile") - 1]
    ).astype(jnp.int32)

    message, cot_middle = lax.optimization_barrier((message, cot_middle))
    middle, tiles = splat(message, rows, cols)

    above = lax.ppermute(middle[rows - EXT :], "cam", down)
    below = lax.ppermute(middle[:EXT], "cam", up)
    left = lax.ppermute(middle[:, mid - PAIRS :], "tile", east)
    right = lax.ppermute(middle[:, :PAIRS], "tile", west)
    sides = jnp.concatenate([left, right], axis=1)
    cot_sides = jnp.concatenate([cot_middle[:, :PAIRS], cot_middle[:, PAIRS + mid :]], axis=1)
    lower = jnp.concatenate([sides[rows - EXT :], cot_sides[rows - LAYERS :]], axis=0)
    upper = jnp.concatenate([sides[:EXT], cot_sides[:LAYERS]], axis=0)
    corner_above = lax.ppermute(lower, "cam", down)
    corner_below = lax.ppermute(upper, "cam", up)

    bev, rows_back = convs(
        edges, tiles, message, cot_middle, weights, middle, above, below, left, right, corner_above,
        corner_below, cot_above, cot_below,
    )
    returned = lax.all_to_all(rows_back, axes, split_axis=0, concat_axis=0, tiled=True)
    grad_depth, grad_context = final(slots, returned, depth, flat_context)
    return (
        bev.reshape(cotangent.shape),
        grad_depth.reshape(depth_weights.shape),
        grad_context.reshape(context.shape),
    )


def solution(mesh):
    placed = (
        P(("cam", "tile"), None, None, None),
        P(("cam", "tile"), None, None, None),
        P(("cam", "tile"), None, None),
        P(("cam", "tile"), None),
        P(("cam", "tile"), None, None),
        P(),
        P("cam", "tile", None),
    )
    return jax.shard_map(
        per_device,
        mesh=mesh,
        in_specs=placed,
        out_specs=(
            P("cam", "tile", None),
            P(("cam", "tile"), None, None, None),
            P(("cam", "tile"), None, None, None),
        ),
        check_vma=False,
    )
```
